32 devices in a mesh: dp: 16 (over z, y, x), seq: 2 (over core).
Axes of the slice: x: 2, y: 2, z: 4, core: 2. Of those that a mesh axis runs over, the one named last changes fastest.
Arguments:
- tokens: bfloat16 [16, 2048, 1024], P('dp', 'seq'), may hold values from -6 to 6
- segments: int32 [16, 2048], P('dp'), may hold values from 0 to 3, never falling along the last dimension, each value on 1 to 768 neighbouring positions
- ln1_gain: bfloat16 [1024], P(('dp', 'seq')), may hold values from 0.5 to 1.5
- ln1_bias: bfloat16 [1024], P(('dp', 'seq')), may hold values from -1.75 to 1.75
- w_query: bfloat16 [1024, 1024], P(('dp', 'seq')), may hold values from -0.1875 to 0.1875
- w_key: bfloat16 [1024, 1024], P(('dp', 'seq')), may hold values from -0.1875 to 0.1875
- w_value: bfloat16 [1024, 1024], P(('dp', 'seq')), may hold values from -0.1875 to 0.1875
- w_out: bfloat16 [1024, 1024], P(('dp', 'seq')), may hold values from -3 to 3
- ln2_gain: bfloat16 [1024], P(('dp', 'seq')), may hold values from 0.5 to 1.5
- ln2_bias: bfloat16 [1024], P(('dp', 'seq')), may hold values from -1.75 to 1.75
- w_up: bfloat16 [1024, 4096], P(('dp', 'seq')), may hold values from -0.1875 to 0.1875
- w_down: bfloat16 [4096, 1024], P(('dp', 'seq')), may hold values from -0.09375 to 0.09375
- cotangent: bfloat16 [16, 2048, 1024], P('dp', 'seq'), may hold values from -6 to 6
Outputs:
- mixed: bfloat16 [16, 2048, 1024], P('dp', 'seq')
- token_grad: bfloat16 [16, 2048, 1024], P('dp', 'seq')
- grad_ln1_gain: float32 [1024], P(('dp', 'seq'))
- grad_ln1_bias: float32 [1024], P(('dp', 'seq'))
- grad_w_query: float32 [1024, 1024], P(('dp', 'seq'))
- grad_w_key: float32 [1024, 1024], P(('dp', 'seq'))
- grad_w_value: float32 [1024, 1024], P(('dp', 'seq'))
- grad_w_out: float32 [1024, 1024], P(('dp', 'seq'))
- grad_ln2_gain: float32 [1024], P(('dp', 'seq'))
- grad_ln2_bias: float32 [1024], P(('dp', 'seq'))
- grad_w_up: float32 [1024, 4096], P(('dp', 'seq'))
- grad_w_down: float32 [4096, 1024], P(('dp', 'seq'))
The draws below stay inside these ranges and needn't reach their ends.
Inputs may be any that keep to these rules, and one draw needn't show every extreme that they name: `segments`: along each sequence the scene ids never fall; each of the 4 scenes has 1 to 768 tokens and one has exactly 768.
All inputs are finite; a program needn't handle non-finite values.
Results may differ from the reference program's by a relative error of at most 0.012.
Values may be sent and summed in bfloat16 or wider, within the bound.
No kernel may reach another device: no remote copies, remote signals or barrier semaphores. Data moves between devices by JAX's collectives and lax.ppermute only.
A program may use at most 256 MiB of HBM per device.

```python
import math
import jax
import jax.numpy as jnp
import numpy as np
from jax import lax

D = 1024
HEADS = 16
HEAD_DIM = 64
FF = 4096
SCENES = 4
QBLK = 512
SEQ_LEN = 2048
SEQS = 16
SCENE_MAX = 768


def with_spikes(result, rng, source, target, shards_of, factor):
    def block_of(position):
        return (jnp.arange(result.shape[position]) // (result.shape[position] // shards_of)).reshape((-1,) + (1,) * (result.ndim - 1 - position))

    first = jax.random.permutation(rng, shards_of)[block_of(target)]
    other_side = (block_of(target) + shards_of // 2) % shards_of
    return jnp.where((block_of(source) == first) | (block_of(source) == other_side), factor * result, result)


def levels(rng, extent, split, least, high):
    def one(position, blocks):
        steps = jax.random.uniform(jax.random.fold_in(jax.random.fold_in(rng, 6), position), (blocks,), jnp.float32, least / len(split), high / len(split))
        return jnp.repeat(jnp.exp(steps), extent[position] // blocks).reshape((-1,) + (1,) * (len(extent) - position - 1))

    loudness = one(*split[0])
    for cut in split[1:]:
        loudness = loudness * one(*cut)
    return loudness


def length_profile(number_of, total, reach, skew):
    weights = [(1 << 20) // math.isqrt(standing ** skew) + 1 for standing in range(2, number_of + 1)]
    rest, holding = total - reach - (number_of - 1), [1] * (number_of - 1)
    while rest > 0:
        candidates = [i for i in range(number_of - 1) if holding[i] < reach]
        mass, remaining = sum([weights[i] for i in candidates]), rest
        for i in candidates:
            addition = min(reach - holding[i], max(1, remaining * weights[i] // mass), rest)
            holding[i] = holding[i] + addition
            rest = rest - addition
    return np.array([reach] + holding)


def ragged(stream_key, number_of, total, most, lean):
    if number_of == 2:
        one = jax.random.randint(stream_key, (), max(1, total - most), min(most, total - 1) + 1)
        return jnp.stack([one, total - one])
    sizes = jnp.asarray(length_profile(number_of, total, most, lean), jnp.int32)
    twos = (number_of - 1) // 2
    source_of, taker = sizes[1:1 + 2 * twos:2], sizes[2:2 + 2 * twos:2]
    margin = jnp.minimum(source_of - 1, most - taker)
    passed = jax.random.randint(jax.random.fold_in(stream_key, 1), (twos,), 0, 1 << 20) % (margin + 1)
    sizes = sizes.at[1:1 + 2 * twos:2].set(source_of - passed).at[2:2 + 2 * twos:2].set(taker + passed)
    return sizes[jax.random.permutation(jax.random.fold_in(stream_key, 2), number_of)]


def scatter_about(own_key, dims, scale, limit, shards=(), held_as=jnp.bfloat16):
    gain = levels(own_key, dims, shards, -0.22, 0.18) if shards else 1.0
    result = jax.random.normal(own_key, dims, jnp.float32) * scale * gain
    return jnp.minimum(jnp.maximum(result, -limit), limit).astype(held_as)


def bell_draw_with(key, extent, scale, reach, cuts, heavy, held_as=jnp.bfloat16):
    drawn = scale * jax.random.normal(key, extent, jnp.float32)
    if cuts:
        drawn = drawn * levels(key, extent, cuts, -0.22, 0.18)
    return jnp.clip(with_spikes(drawn, jax.random.fold_in(key, 3), *heavy), -reach, reach).astype(held_as)


def setup_inputs(seed: int = 0) -> dict:
    key_of = jax.random.split(jax.random.key(seed), 14)
    return {
        "tokens": bell_draw_with(key_of[0], (SEQS, SEQ_LEN, D), 1.0, 6.0, ((0, 16), (1, 2)), (0, 2, 16, 2.0)),
        "segments": jax.vmap(lambda own: jnp.searchsorted(jnp.cumsum(ragged(own, SCENES, SEQ_LEN, SCENE_MAX, 0)), jnp.arange(SEQ_LEN), side="right"))(jax.random.split(key_of[1], SEQS)).reshape((SEQS, SEQ_LEN)).astype(jnp.int32),
        "ln1_gain": jnp.clip(1.0 + 0.1 * jax.random.normal(key_of[2], (D,), jnp.float32), 0.5, 1.5).astype(jnp.bfloat16),
        "ln1_bias": scatter_about(key_of[3], (D,), 0.3, 1.75, ((0, 32),)),
        "w_query": scatter_about(key_of[4], (D, D), D ** -0.5, 0.1875, ((0, 32),)),
        "w_key": scatter_about(key_of[5], (D, D), D ** -0.5, 0.1875, ((0, 32),)),
        "w_value": scatter_about(key_of[6], (D, D), D ** -0.5, 0.1875, ((0, 32),)),
        "w_out": scatter_about(key_of[7], (D, D), (max(D // 256, 4)) ** -0.5, 3.0, ((0, 32),)),
        "ln2_gain": jnp.clip(1.0 + 0.1 * jax.random.normal(key_of[8], (D,), jnp.float32), 0.5, 1.5).astype(jnp.bfloat16),
        "ln2_bias": scatter_about(key_of[9], (D,), 0.3, 1.75, ((0, 32),)),
        "w_up": scatter_about(key_of[10], (D, FF), D ** -0.5, 0.1875, ((0, 32),)),
        "w_down": scatter_about(key_of[11], (FF, D), FF ** -0.5, 0.09375, ((0, 32),)),
        "cotangent": scatter_about(key_of[12], (SEQS, SEQ_LEN, D), 1.0, 6.0, ((0, 16), (1, 2))),
    }


@jax.custom_vjp
def low(v):
    return lax.optimization_barrier(v.astype(jnp.bfloat16)).astype(jnp.float32)

@jax.custom_vjp
def low_back(v):
    return v

def low_keep(v):
    return (low(v), None)

def low_pass(kept, grad):
    return (grad,)

def back_keep(v):
    return (v, None)

def back_low(kept, grad):
    return (low(grad),)
low.defvjp(low_keep, low_pass)
low_back.defvjp(back_keep, back_low)
HIGHEST_MODE = lax.Precision.HIGHEST

def layer_norm(values, gain_vec, bias_vec):
    centre = values - lax.optimization_barrier(jnp.mean(values, axis=-1, keepdims=True))
    spread = lax.optimization_barrier(jnp.mean(centre * centre, axis=-1, keepdims=True))
    return centre * lax.rsqrt(spread + 1e-05) * gain_vec + bias_vec

def forward(inputs, seg_ids, params):
    gain_one, bias_one, query_w, key_w, value_w, out_w, gain_two, bias_two, up_w, down_w = params
    length = inputs.shape[0]
    normed_one = low(layer_norm(inputs, gain_one, bias_one))
    queries = low(low_back(jnp.dot(normed_one, query_w, precision=HIGHEST_MODE)))
    keys_all = low(low_back(jnp.dot(normed_one, key_w, precision=HIGHEST_MODE)))
    values_all = low(low_back(jnp.dot(normed_one, value_w, precision=HIGHEST_MODE)))
    query_heads = queries.reshape(length // QBLK, QBLK, HEADS, HEAD_DIM)
    key_heads = keys_all.reshape(length, HEADS, HEAD_DIM)
    value_heads = values_all.reshape(length, HEADS, HEAD_DIM)
    seg_blocks = seg_ids.reshape(length // QBLK, QBLK)
    score_scale = HEAD_DIM ** (-0.5)

    def attend(packed):
        query_block, seg_block = packed
        scores = jnp.einsum('qhd,khd->hqk', query_block, key_heads, precision=HIGHEST_MODE) * score_scale
        same_scene = seg_block[:, None] == seg_ids[None, :]
        scores = low_back(jnp.where(same_scene[None], scores, -1000000000.0))
        weights = low(jax.nn.softmax(scores, axis=-1))
        return jnp.einsum('hqk,khd->qhd', weights, value_heads, precision=HIGHEST_MODE)
    attended = lax.map(jax.checkpoint(attend), (query_heads, seg_blocks)).reshape(length, D)
    attended = low(low_back(attended))
    branch = low_back(jnp.dot(attended, out_w, precision=HIGHEST_MODE))
    middle = inputs + branch
    normed_two = low(layer_norm(middle, gain_two, bias_two))
    upward = low_back(jnp.dot(normed_two, up_w, precision=HIGHEST_MODE))
    activated = low(jax.nn.gelu(upward, approximate=False))
    return middle + jnp.dot(activated, down_w, precision=HIGHEST_MODE)

def reference(tokens, segments, ln1_gain, ln1_bias, w_query, w_key, w_value, w_out, ln2_gain, ln2_bias, w_up, w_down, cotangent):
    params = tuple((weight.astype(jnp.float32) for weight in (ln1_gain, ln1_bias, w_query, w_key, w_value, w_out, ln2_gain, ln2_bias, w_up, w_down)))

    def per_sequence(totals, packed):
        rows, seg_ids, grad_out = packed

        def run(values, weights):
            return forward(values, seg_ids, weights)
        outputs, pull = jax.vjp(run, rows.astype(jnp.float32), params)
        grad_rows, grad_params = pull(grad_out.astype(jnp.float32))
        totals = tuple((first + second for first, second in zip(totals, grad_params)))
        return (totals, (outputs.astype(jnp.bfloat16), grad_rows.astype(jnp.bfloat16)))
    start = tuple((jnp.zeros(weight.shape, jnp.float32) for weight in params))
    totals, (mixed, token_grad) = lax.scan(per_sequence, start, (tokens, segments, cotangent))
    return (mixed, token_grad, totals[0], totals[1], totals[2], totals[3], totals[4], totals[5], totals[6], totals[7], totals[8], totals[9])
```

```python
from functools import partial

import jax
import jax.numpy as jnp
from jax import lax
from jax.experimental import pallas as pl
from jax.experimental.pallas import tpu as pltpu
from jax.sharding import PartitionSpec as P

BF16 = jnp.bfloat16
F32 = jnp.float32
HEAD_DIM = 64
GROUP = 4
GROUP_WIDTH = GROUP * HEAD_DIM
NEG = -1000000000.0
BOTH = ("dp", "seq")
LN_ROWS = 16
ATT_Q = 256
ATT_K = 512
ROWS = 256
FF_COLS = 512


def dot_nn(left, right):
    return lax.dot_general(left, right, (((1,), (0,)), ((), ())), preferred_element_type=F32)


def dot_nt(left, right):
    return lax.dot_general(left, right, (((1,), (1,)), ((), ())), preferred_element_type=F32)


def dot_tn(left, right):
    return lax.dot_general(left, right, (((0,), (0,)), ((), ())), preferred_element_type=F32)


def params(mib):
    return pltpu.CompilerParams(vmem_limit_bytes=mib << 20)


def cost(flops, nbytes):
    return pl.CostEstimate(flops=flops, bytes_accessed=nbytes, transcendentals=0)


def normed(values):
    centre = values - jnp.mean(values, axis=-1, keepdims=True)
    scale = lax.rsqrt(jnp.mean(centre * centre, axis=-1, keepdims=True) + 1e-05)
    return centre * scale, scale


def norm_back(grad, gain_vec, hat, scale):
    inner = grad * gain_vec
    return scale * (
        inner
        - jnp.mean(inner, axis=-1, keepdims=True)
        - hat * jnp.mean(inner * hat, axis=-1, keepdims=True)
    )


def flat(ref):
    value = ref[...]
    return value.reshape(-1, value.shape[-1])


def resident(shape):
    zeros = (0,) * len(shape)
    return pl.BlockSpec(shape, lambda *_: zeros, pipeline_mode=pl.Buffered(1))


def tile_spec(gathered, rows, t):
    devices, _, width = gathered.shape
    return pl.BlockSpec((devices, rows, width), lambda *_: (0, t, 0), pipeline_mode=pl.Buffered(1))


def kv_kernel(x_ref, gain_ref, bias_ref, wk_ref, wv_ref, h_ref, kv_ref):
    hat, _ = normed(x_ref[...].astype(F32))
    low = (hat * gain_ref[...] + bias_ref[...]).astype(BF16)
    h_ref[...] = low
    kv_ref[0] = dot_nn(low, flat(wk_ref)).astype(BF16)
    kv_ref[1] = dot_nn(low, flat(wv_ref)).astype(BF16)


def kv_call(x, gain, bias, gathered, rows):
    n, d = x.shape
    return pl.pallas_call(
        kv_kernel,
        grid=(n // ROWS,),
        in_specs=[
            pl.BlockSpec((ROWS, d), lambda i: (i, 0)),
            resident((1, d)),
            resident((1, d)),
            tile_spec(gathered, rows, 1),
            tile_spec(gathered, rows, 2),
        ],
        out_specs=[
            pl.BlockSpec((ROWS, d), lambda i: (i, 0)),
            pl.BlockSpec((2, ROWS, d), lambda i: (0, i, 0)),
        ],
        out_shape=[jax.ShapeDtypeStruct((n, d), BF16), jax.ShapeDtypeStruct((2, n, d), BF16)],
        compiler_params=params(40),
        cost_estimate=cost(4 * n * d * d, 4 * d * d + 8 * n * d),
        name="kv_proj",
    )(x, gain, bias, gathered, gathered)


def q_kernel(h_ref, wq_ref, q_ref):
    q_ref[...] = (dot_nn(h_ref[...], flat(wq_ref)).astype(BF16).astype(F32) * 0.125).astype(BF16)


def q_call(h, gathered, rows):
    n, d = h.shape
    return pl.pallas_call(
        q_kernel,
        grid=(n // ROWS,),
        in_specs=[pl.BlockSpec((ROWS, d), lambda i: (i, 0)), tile_spec(gathered, rows, 0)],
        out_specs=pl.BlockSpec((ROWS, d), lambda i: (i, 0)),
        out_shape=jax.ShapeDtypeStruct((n, d), BF16),
        compiler_params=params(32),
        cost_estimate=cost(2 * n * d * d, 2 * d * d + 4 * n * d),
        name="q_proj",
    )(h, gathered)


def stack_heads(block):
    lane = lax.broadcasted_iota(jnp.int32, block.shape, 1) // HEAD_DIM
    zero = jnp.zeros_like(block)
    return jnp.concatenate([jnp.where(lane == h, block, zero) for h in range(GROUP)], axis=0)


def head_cols(value, h, width):
    return value[:, h * width : (h + 1) * width]


def head_rows(value, h):
    return value[h * HEAD_DIM : (h + 1) * HEAD_DIM, :]


def attend_kernel(bq, bk, tab, q_ref, ko_ref, vo_ref, kp_ref, vp_ref, sq_ref, so_ref, sp_ref, o_ref, lse_ref):
    i = pl.program_id(1)
    stacked = stack_heads(q_ref[...])
    seg_q = jnp.concatenate([sq_ref[0]] * GROUP, axis=1)

    def over(k_ref, v_ref, s_ref, first, count, state):
        def step(j, carry):
            top, total, acc = carry
            at = pl.multiple_of((first + j) * bk, bk)
            scores = dot_nt(k_ref[0, pl.ds(at, bk), :], stacked)
            scores = jnp.where(s_ref[pl.ds(at, bk), :] == seg_q, scores, NEG)
            new_top = jnp.maximum(top, jnp.max(scores, axis=0, keepdims=True))
            decay = jnp.exp(top - new_top)
            probs = jnp.exp(scores - new_top)
            total = total * decay + jnp.sum(probs, axis=0, keepdims=True)
            low = probs.astype(BF16)
            values = v_ref[0, pl.ds(at, bk), :].T
            acc = tuple(
                acc[h] * head_cols(decay, h, bq) + dot_nn(head_rows(values, h), head_cols(low, h, bq))
                for h in range(GROUP)
            )
            return new_top, total, acc

        return lax.fori_loop(0, count, step, state)

    state = (
        jnp.full((1, GROUP * bq), -jnp.inf, F32),
        jnp.zeros((1, GROUP * bq), F32),
        tuple(jnp.zeros((HEAD_DIM, bq), F32) for _ in range(GROUP)),
    )
    state = over(ko_ref, vo_ref, so_ref, tab[4 * i], tab[4 * i + 1], state)
    top, total, acc = over(kp_ref, vp_ref, sp_ref, tab[4 * i + 2], tab[4 * i + 3], state)
    out = jnp.concatenate([acc[h] / head_cols(total, h, bq) for h in range(GROUP)], axis=0)
    o_ref[...] = out.T.astype(BF16)
    lse_ref[0, 0] = top + jnp.log(total)


def attend_call(tab, q, own, other, seg_q, seg_own, seg_other, bq, bk):
    n, d = q.shape
    groups, blocks = d // GROUP_WIDTH, n // bq
    query = pl.BlockSpec((bq, GROUP_WIDTH), lambda g, i, *_: (i, g))

    def half(which):
        return pl.BlockSpec((1, n, GROUP_WIDTH), lambda g, i, *_: (which, 0, g))

    column = pl.BlockSpec((n, 1), lambda g, i, *_: (0, 0))
    spec = pltpu.PrefetchScalarGridSpec(
        num_scalar_prefetch=1,
        grid=(groups, blocks),
        in_specs=[
            query,
            half(0),
            half(1),
            half(0),
            half(1),
            pl.BlockSpec((1, 1, bq), lambda g, i, *_: (i, 0, 0)),
            column,
            column,
        ],
        out_specs=[query, pl.BlockSpec((1, 1, 1, GROUP * bq), lambda g, i, *_: (g, i, 0, 0))],
    )
    return pl.pallas_call(
        partial(attend_kernel, bq, bk),
        grid_spec=spec,
        out_shape=[
            jax.ShapeDtypeStruct((n, d), BF16),
            jax.ShapeDtypeStruct((groups, blocks, 1, GROUP * bq), F32),
        ],
        compiler_params=params(56),
        cost_estimate=cost(30_000_000_000, 12 * n * d),
        name="attend",
    )(tab, q, own, own, other, other, seg_q, seg_own, seg_other)


def attend_back_kernel(
    bq, bk, tab, q_ref, go_ref, o_ref, ko_ref, vo_ref, kp_ref, vp_ref, sq_ref, so_ref, sp_ref, lse_ref,
    dq_ref, down_ref, dpart_ref, dko, dvo, dkp, dvp,
):
    i = pl.program_id(1)

    @pl.when(i == 0)
    def _():
        for ref in (dko, dvo, dkp, dvp):
            ref[...] = jnp.zeros_like(ref)

    stacked = stack_heads(q_ref[...])
    grad = go_ref[...]
    stacked_grad = stack_heads(grad)
    product = (grad.astype(F32) * o_ref[...].astype(F32)).T
    inner = jnp.concatenate(
        [jnp.sum(head_rows(product, h), axis=0, keepdims=True) for h in range(GROUP)], axis=1
    )
    seg_q = jnp.concatenate([sq_ref[0]] * GROUP, axis=1)
    lse = lse_ref[0, 0]

    def over(k_ref, v_ref, s_ref, dk, dv, first, count, state):
        def step(j, acc):
            at = pl.multiple_of((first + j) * bk, bk)
            keys = k_ref[0, pl.ds(at, bk), :]
            scores = dot_nt(keys, stacked)
            scores = jnp.where(s_ref[pl.ds(at, bk), :] == seg_q, scores, NEG)
            probs = jnp.exp(scores - lse)
            grad_probs = dot_nt(v_ref[0, pl.ds(at, bk), :], stacked_grad)
            grad_scores = (probs * (grad_probs - inner)).astype(BF16)
            dv[pl.ds(at, bk), :] += dot_nn(probs.astype(BF16), stacked_grad)
            dk[pl.ds(at, bk), :] += dot_nn(grad_scores, stacked)
            keys_t = keys.T
            return tuple(
                acc[h] + dot_nn(head_rows(keys_t, h), head_cols(grad_scores, h, bq)) for h in range(GROUP)
            )

        return lax.fori_loop(0, count, step, state)

    state = tuple(jnp.zeros((HEAD_DIM, bq), F32) for _ in range(GROUP))
    state = over(ko_ref, vo_ref, so_ref, dko, dvo, tab[4 * i], tab[4 * i + 1], state)
    state = over(kp_ref, vp_ref, sp_ref, dkp, dvp, tab[4 * i + 2], tab[4 * i + 3], state)
    dq_ref[...] = (jnp.concatenate(state, axis=0).T * 0.125).astype(BF16)

    @pl.when(i == pl.num_programs(1) - 1)
    def _():
        down_ref[0] = dko[...].astype(BF16)
        down_ref[1] = dvo[...].astype(BF16)
        dpart_ref[0] = dkp[...].astype(BF16)
        dpart_ref[1] = dvp[...].astype(BF16)


def attend_back_call(tab, q, grad, out, own, other, seg_q, seg_own, seg_other, lse, bq, bk):
    n, d = q.shape
    groups, blocks = d // GROUP_WIDTH, n // bq
    query = pl.BlockSpec((bq, GROUP_WIDTH), lambda g, i, *_: (i, g))

    def half(which):
        return pl.BlockSpec((1, n, GROUP_WIDTH), lambda g, i, *_: (which, 0, g))

    column = pl.BlockSpec((n, 1), lambda g, i, *_: (0, 0))
    pair = pl.BlockSpec((2, n, GROUP_WIDTH), lambda g, i, *_: (0, 0, g))
    spec = pltpu.PrefetchScalarGridSpec(
        num_scalar_prefetch=1,
        grid=(groups, blocks),
        in_specs=[
            query,
            query,
            query,
            half(0),
            half(1),
            half(0),
            half(1),
            pl.BlockSpec((1, 1, bq), lambda g, i, *_: (i, 0, 0)),
            column,
            column,
            pl.BlockSpec((1, 1, 1, GROUP * bq), lambda g, i, *_: (g, i, 0, 0)),
        ],
        out_specs=[query, pair, pair],
        scratch_shapes=[pltpu.VMEM((n, GROUP_WIDTH), F32)] * 4,
    )
    return pl.pallas_call(
        partial(attend_back_kernel, bq, bk),
        grid_spec=spec,
        out_shape=[
            jax.ShapeDtypeStruct((n, d), BF16),
            jax.ShapeDtypeStruct((2, n, d), BF16),
            jax.ShapeDtypeStruct((2, n, d), BF16),
        ],
        compiler_params=params(56),
        cost_estimate=cost(45_000_000_000, 24 * n * d),
        name="attend_back",
    )(tab, q, grad, out, own, own, other, other, seg_q, seg_own, seg_other, lse)


def mid_kernel(x_ref, o_ref, wo_ref, gain_ref, bias_ref, r_ref, h_ref):
    mid = x_ref[...].astype(F32) + dot_nn(o_ref[...], flat(wo_ref))
    r_ref[...] = mid
    hat, _ = normed(mid)
    h_ref[...] = (hat * gain_ref[...] + bias_ref[...]).astype(BF16)


def mid_call(x, o, gathered, rows, t, gain, bias):
    n, d = x.shape
    row = pl.BlockSpec((ROWS, d), lambda i: (i, 0))
    return pl.pallas_call(
        mid_kernel,
        grid=(n // ROWS,),
        in_specs=[row, row, tile_spec(gathered, rows, t), resident((1, d)), resident((1, d))],
        out_specs=[row, row],
        out_shape=[jax.ShapeDtypeStruct((n, d), F32), jax.ShapeDtypeStruct((n, d), BF16)],
        compiler_params=params(32),
        cost_estimate=cost(2 * n * d * d, 2 * d * d + 10 * n * d),
        name="out_proj",
    )(x, o, gathered, gain, bias)


def mid_back_kernel(gh_ref, r_ref, g_ref, o_ref, wo_ref, gain_ref, gr_ref, go_ref, dwo_ref, dln_ref, acc):
    i = pl.program_id(0)
    hat, scale = normed(r_ref[...])
    grad = gh_ref[...]
    total = g_ref[...].astype(F32) + norm_back(grad, gain_ref[...], hat, scale)
    gr_ref[...] = total
    low = total.astype(BF16)
    go_ref[...] = dot_nt(low, flat(wo_ref)).astype(BF16)
    part = dot_tn(o_ref[...], low)
    dgain = jnp.sum(grad * hat, axis=0, keepdims=True)
    dbias = jnp.sum(grad, axis=0, keepdims=True)

    @pl.when(i == 0)
    def _():
        acc[...] = part
        dln_ref[0:1, :] = dgain
        dln_ref[1:2, :] = dbias

    @pl.when(i > 0)
    def _():
        acc[...] += part
        dln_ref[0:1, :] += dgain
        dln_ref[1:2, :] += dbias

    @pl.when(i == pl.num_programs(0) - 1)
    def _():
        dwo_ref[...] = acc[...].astype(BF16)


def mid_back_call(grad, mid, cot, o, gathered, rows, t, gain):
    n, d = mid.shape
    row = pl.BlockSpec((ROWS, d), lambda i: (i, 0))
    return pl.pallas_call(
        mid_back_kernel,
        grid=(n // ROWS,),
        in_specs=[row, row, row, row, tile_spec(gathered, rows, t), resident((1, d))],
        out_specs=[
            row,
            row,
            pl.BlockSpec((d, d), lambda i: (0, 0)),
            pl.BlockSpec((2, d), lambda i: (0, 0)),
        ],
        out_shape=[
            jax.ShapeDtypeStruct((n, d), F32),
            jax.ShapeDtypeStruct((n, d), BF16),
            jax.ShapeDtypeStruct((d, d), BF16),
            jax.ShapeDtypeStruct((2, d), F32),
        ],
        scratch_shapes=[pltpu.VMEM((d, d), F32)],
        compiler_params=params(48),
        cost_estimate=cost(4 * n * d * d, 4 * d * d + 18 * n * d),
        name="out_proj_back",
    )(grad, mid, cot, o, gathered, gain)


def ffn_kernel(last, h_ref, g_ref, wu_ref, wd_ref, mi_ref, gi_ref, mo_ref, go_ref, dwu_ref, dwd_ref, *rest):
    j = pl.program_id(0)
    h, grad = h_ref[...], g_ref[...]
    wu, wd = flat(wu_ref), flat(wd_ref)
    up = dot_nn(h, wu)
    cdf = 0.5 * (1.0 + lax.erf(up * 0.7071067811865476))
    act = (up * cdf).astype(BF16)
    slope = cdf + up * (jnp.exp(-0.5 * up * up) * 0.3989422804014327)
    gu = (dot_nt(grad, wd) * slope).astype(BF16)
    dwd_ref[...] = dot_tn(act, grad).astype(BF16).reshape(dwd_ref.shape)
    dwu_ref[...] = dot_tn(h, gu).astype(BF16).reshape(dwu_ref.shape)
    mo = rest[0] if last else mo_ref

    @pl.when(j == 0)
    def _():
        mo[...] = mi_ref[...] + dot_nn(act, wd)
        if gi_ref is None:
            go_ref[...] = dot_nt(gu, wu)
        else:
            go_ref[...] = gi_ref[...] + dot_nt(gu, wu)

    @pl.when(j > 0)
    def _():
        mo[...] += dot_nn(act, wd)
        go_ref[...] += dot_nt(gu, wu)

    if last:

        @pl.when(j == pl.num_programs(0) - 1)
        def _():
            mo_ref[...] = mo[...].astype(BF16)


def ffn_call(h, cot, wu, wu_specs, wd, wd_specs, mid, gmid, width, last):
    n, d = h.shape
    steps = width // FF_COLS
    full = resident((n, d))
    const = pl.BlockSpec((n, d), lambda j: (0, 0))
    in_specs = [full, full, wu_specs[0], wd_specs[0], full]
    args = [h, cot, wu, wd, mid]
    aliases = {} if last else {4: 0}
    body = partial(ffn_kernel, last)
    if gmid is None:
        def body(h_ref, g_ref, wu_ref, wd_ref, mi_ref, *refs):
            ffn_kernel(last, h_ref, g_ref, wu_ref, wd_ref, mi_ref, None, *refs)
    else:
        in_specs.append(full)
        args.append(gmid)
        aliases[5] = 1
    return pl.pallas_call(
        body,
        grid=(steps,),
        in_specs=in_specs,
        out_specs=[const, const, wu_specs[1], wd_specs[1]],
        out_shape=[
            jax.ShapeDtypeStruct((n, d), BF16 if last else F32),
            jax.ShapeDtypeStruct((n, d), F32),
            wu_specs[2],
            wd_specs[2],
        ],
        scratch_shapes=[pltpu.VMEM((n, d), F32)] if last else [],
        input_output_aliases=aliases,
        compiler_params=params(60),
        cost_estimate=cost(12 * n * d * width, 8 * d * width + 20 * n * d),
        name="ffn",
    )(*args)


def head_back_kernel(dq_ref, dk_ref, rk_ref, dv_ref, rv_ref, x_ref, gr_ref, wq_ref, wk_ref, wv_ref, gain_ref, tg_ref, dkv_ref, dln_ref):
    i = pl.program_id(0)
    dk = (dk_ref[0].astype(F32) + rk_ref[0].astype(F32)).astype(BF16)
    dv = (dv_ref[0].astype(F32) + rv_ref[0].astype(F32)).astype(BF16)
    dkv_ref[0] = dk
    dkv_ref[1] = dv
    grad = dot_nt(dq_ref[...], flat(wq_ref)) + dot_nt(dk, flat(wk_ref)) + dot_nt(dv, flat(wv_ref))
    hat, scale = normed(x_ref[...].astype(F32))
    tg_ref[...] = (gr_ref[...] + norm_back(grad, gain_ref[...], hat, scale)).astype(BF16)
    dgain = jnp.sum(grad * hat, axis=0, keepdims=True)
    dbias = jnp.sum(grad, axis=0, keepdims=True)

    @pl.when(i == 0)
    def _():
        dln_ref[0:1, :] = dgain
        dln_ref[1:2, :] = dbias

    @pl.when(i > 0)
    def _():
        dln_ref[0:1, :] += dgain
        dln_ref[1:2, :] += dbias


def head_back_call(dq, dkv, rkv, x, gr, gathered, rows, gain):
    n, d = x.shape
    row = pl.BlockSpec((ROWS, d), lambda i: (i, 0))

    def half(which):
        return pl.BlockSpec((1, ROWS, d), lambda i: (which, i, 0))

    return pl.pallas_call(
        head_back_kernel,
        grid=(n // ROWS,),
        in_specs=[
            row,
            half(0),
            half(0),
            half(1),
            half(1),
            row,
            row,
            tile_spec(gathered, rows, 0),
            tile_spec(gathered, rows, 1),
            tile_spec(gathered, rows, 2),
            resident((1, d)),
        ],
        out_specs=[
            row,
            pl.BlockSpec((2, ROWS, d), lambda i: (0, i, 0)),
            pl.BlockSpec((2, d), lambda i: (0, 0)),
        ],
        out_shape=[
            jax.ShapeDtypeStruct((n, d), BF16),
            jax.ShapeDtypeStruct((2, n, d), BF16),
            jax.ShapeDtypeStruct((2, d), F32),
        ],
        compiler_params=params(48),
        cost_estimate=cost(6 * n * d * d, 6 * d * d + 18 * n * d),
        name="qkv_back",
    )(dq, dkv, rkv, dkv, rkv, x, gr, gathered, gathered, gathered, gain)


def qkv_grad_kernel(h_ref, dq_ref, dk_ref, dv_ref, out_ref):
    h = h_ref[...]
    out_ref[0] = dot_tn(h, dq_ref[...]).astype(BF16)
    out_ref[1] = dot_tn(h, dk_ref[0]).astype(BF16)
    out_ref[2] = dot_tn(h, dv_ref[0]).astype(BF16)


def qkv_grad_call(h, dq, dkv):
    n, d = h.shape
    width = 256
    return pl.pallas_call(
        qkv_grad_kernel,
        grid=(d // width,),
        in_specs=[
            resident((n, d)),
            pl.BlockSpec((n, width), lambda j: (0, j)),
            pl.BlockSpec((1, n, width), lambda j: (0, 0, j)),
            pl.BlockSpec((1, n, width), lambda j: (1, 0, j)),
        ],
        out_specs=pl.BlockSpec((3, d, width), lambda j: (0, 0, j)),
        out_shape=jax.ShapeDtypeStruct((3, d, d), BF16),
        compiler_params=params(40),
        cost_estimate=cost(6 * n * d * d, 6 * d * d + 8 * n * d),
        name="qkv_grad",
    )(h, dq, dkv, dkv)


def block_table(seg_full, seg_local, my_index, n, bq, bk):
    first, last = seg_local[::bq], seg_local[bq - 1 :: bq]
    low = jnp.sum((seg_full[None, :] < first[:, None]).astype(jnp.int32), axis=1)
    high = jnp.sum((seg_full[None, :] <= last[:, None]).astype(jnp.int32), axis=1)
    columns = []
    for index in (my_index, 1 - my_index):
        start = jnp.clip(low - index * n, 0, n)
        stop = jnp.clip(high - index * n, 0, n)
        block = start // bk
        columns += [block, jnp.where(stop > start, (stop + bk - 1) // bk - block, 0)]
    return jnp.stack(columns, axis=1).reshape(-1).astype(jnp.int32)


def body(
    tokens,
    segments,
    ln1_gain,
    ln1_bias,
    w_query,
    w_key,
    w_value,
    w_out,
    ln2_gain,
    ln2_bias,
    w_up,
    w_down,
    cotangent,
):
    x = tokens[0]
    n, d = x.shape
    cot = cotangent[0]
    rows = w_query.shape[0]
    devices = d // rows
    hidden = w_up.shape[1]
    per_device = hidden // devices
    parts = 2
    sub = per_device // parts
    width = hidden // parts
    my_index = lax.axis_index("seq")
    seg_full = segments[0]
    seg_local = lax.dynamic_slice_in_dim(seg_full, my_index * n, n)
    seg_other = lax.dynamic_slice_in_dim(seg_full, (1 - my_index) * n, n)
    tab = block_table(seg_full, seg_local, my_index, n, ATT_Q, ATT_K)
    seg_q = seg_local.reshape(n // ATT_Q, 1, ATT_Q)
    seg_own_col, seg_other_col = seg_local[:, None], seg_other[:, None]

    vectors = jnp.concatenate([ln1_gain, ln1_bias, ln2_gain, ln2_bias]).reshape(1, 4 * rows)
    ln_block = jnp.pad(vectors, ((0, LN_ROWS - 1), (0, d - 4 * rows)))
    first_local = jnp.concatenate([w_query, w_key, w_value, ln_block], axis=0)
    up_parts = w_up.reshape(rows, devices, parts, sub).transpose(2, 0, 1, 3).reshape(parts, rows, width // d, d)
    up_parts = up_parts.transpose(0, 2, 1, 3).reshape(parts, (width // d) * rows, d)
    part_local = [
        jnp.concatenate([up_parts[p], w_down[p * sub : (p + 1) * sub]], axis=0) for p in range(parts)
    ]
    part_local[0] = jnp.concatenate([part_local[0], w_out], axis=0)

    def gather(local):
        out = lax.all_gather(local, BOTH, axis=0, tiled=True)
        return out.reshape(devices, local.shape[0], d)

    first = gather(first_local)
    second = [gather(p) for p in part_local]

    aligned = rows % 16 == 0
    if aligned:
        qkv_w, qkv_rows = first, rows
        out_w, out_t, out_rows = second[0], second[0].shape[1] // rows - 1, rows
    else:
        qkv_w = first[:, : 3 * rows].reshape(devices, 3, rows, d).transpose(1, 0, 2, 3).reshape(1, 3 * d, d)
        qkv_rows = d
        out_w, out_t, out_rows = second[0][:, -rows:].reshape(1, d, d), 0, d
    ln = first[:, 3 * rows, : 4 * rows].reshape(devices, 4, rows).transpose(1, 0, 2).reshape(4, 1, d).astype(F32)

    h1, own = kv_call(x, ln[0], ln[1], qkv_w, qkv_rows)
    swap = [(0, 1), (1, 0)]
    other = lax.ppermute(own, "seq", swap)
    q = q_call(h1, qkv_w, qkv_rows)
    attended, lse = attend_call(tab, q, own, other, seg_q, seg_own_col, seg_other_col, ATT_Q, ATT_K)
    mid, h2 = mid_call(x, attended, out_w, out_rows, out_t, ln[2], ln[3])

    up_rows = (width // d) * rows
    group = FF_COLS // sub
    carry, gmid, shares = mid, None, []
    for p in range(parts):
        if aligned:
            per_tile = d // FF_COLS
            wu = wd = second[p]
            wu_specs = (
                pl.BlockSpec((devices, rows, FF_COLS), lambda j: (0, j // per_tile, j % per_tile)),
                pl.BlockSpec((devices, rows, FF_COLS), lambda j: (0, j // per_tile, j % per_tile)),
                jax.ShapeDtypeStruct((devices, up_rows, d), BF16),
            )
            tile = up_rows // sub
            wd_specs = (
                pl.BlockSpec((group, sub, d), lambda j: (j, tile, 0)),
                pl.BlockSpec((group, sub, d), lambda j: (j, 0, 0)),
                jax.ShapeDtypeStruct((devices, sub, d), BF16),
            )
        else:
            wu = second[p][:, :up_rows].reshape(devices, width // d, rows, d).transpose(0, 2, 1, 3).reshape(d, width)
            wd = second[p][:, up_rows : up_rows + sub].reshape(width, d)
            wu_block = pl.BlockSpec((d, FF_COLS), lambda j: (0, j))
            wd_block = pl.BlockSpec((FF_COLS, d), lambda j: (j, 0))
            wu_specs = (wu_block, wu_block, jax.ShapeDtypeStruct((d, width), BF16))
            wd_specs = (wd_block, wd_block, jax.ShapeDtypeStruct((width, d), BF16))
        carry, gmid, dwu, dwd = ffn_call(
            h2, cot, wu, wu_specs, wd, wd_specs, carry, gmid, width, p == parts - 1
        )
        if not aligned:
            dwu = dwu.reshape(devices, rows, width // d, d).transpose(0, 2, 1, 3)
        packed = jnp.concatenate(
            [dwu.reshape(devices, up_rows, d), dwd.reshape(devices, sub, d)], axis=1
        ).reshape(devices * (up_rows + sub), d)
        shares.append(lax.psum_scatter(packed, BOTH, scatter_dimension=0, tiled=True))
    mixed = carry

    grad_mid, grad_att, dwo, dln2 = mid_back_call(gmid, mid, cot, attended, out_w, out_rows, out_t, ln[2])
    dq, dkv, sent = attend_back_call(
        tab, q, grad_att, attended, own, other, seg_q, seg_own_col, seg_other_col, lse, ATT_Q, ATT_K
    )
    received = lax.ppermute(sent, "seq", swap)
    token_grad, dkv, dln1 = head_back_call(dq, dkv, received, x, grad_mid, qkv_w, qkv_rows, ln[0])
    dqkv = qkv_grad_call(h1, dq, dkv)

    dln = jnp.concatenate([dln1, dln2], axis=0).astype(BF16)
    dln = dln.reshape(4, devices, rows).transpose(1, 0, 2).reshape(devices, 1, 4 * rows)
    dln = jnp.pad(dln, ((0, 0), (0, LN_ROWS - 1), (0, d - 4 * rows)))
    dqkv = dqkv.reshape(3, devices, rows, d).transpose(1, 0, 2, 3).reshape(devices, 3 * rows, d)
    packed = jnp.concatenate([dqkv, dwo.reshape(devices, rows, d), dln], axis=1)
    packed = packed.reshape(devices * packed.shape[1], d)
    tail = lax.psum_scatter(packed, BOTH, scatter_dimension=0, tiled=True).astype(F32)
    dln = tail[4 * rows, : 4 * rows].reshape(4, rows)

    up_share = jnp.stack([s[:up_rows] for s in shares]).astype(F32)
    up_share = up_share.reshape(parts, width // d, rows, d).transpose(0, 2, 1, 3).reshape(parts, rows, devices, sub)
    up_share = up_share.transpose(1, 2, 0, 3).reshape(rows, hidden)
    down_share = jnp.concatenate([s[up_rows:] for s in shares], axis=0).astype(F32)
    return (
        mixed[None],
        token_grad[None],
        dln[0],
        dln[1],
        tail[:rows],
        tail[rows : 2 * rows],
        tail[2 * rows : 3 * rows],
        tail[3 * rows : 4 * rows],
        dln[2],
        dln[3],
        up_share,
        down_share,
    )


def solution(mesh):
    row, act, vec = P(BOTH, None), P("dp", "seq", None), P(BOTH)
    in_specs = (act, P("dp", None), vec, vec, row, row, row, row, vec, vec, row, row, act)
    out_specs = (act, act, vec, vec, row, row, row, row, vec, vec, row, row)
    return jax.shard_map(body, mesh=mesh, in_specs=in_specs, out_specs=out_specs, check_vma=False)
```

```python
from functools import partial

import jax
import jax.numpy as jnp
from jax import lax
from jax.experimental import pallas as pl
from jax.experimental.pallas import tpu as pltpu
from jax.sharding import PartitionSpec as P

BF16 = jnp.bfloat16
F32 = jnp.float32
HEAD_DIM = 64
GROUP = 4
GROUP_WIDTH = GROUP * HEAD_DIM
NEG = -1000000000.0
BOTH = ("dp", "seq")
LN_ROWS = 16
ATT_Q = 256
ATT_K = 512
ROWS = 256
FF_COLS = 512


def dot_nn(left, right):
    return lax.dot_general(left, right, (((1,), (0,)), ((), ())), preferred_element_type=F32)


def dot_nt(left, right):
    return lax.dot_general(left, right, (((1,), (1,)), ((), ())), preferred_element_type=F32)


def dot_tn(left, right):
    return lax.dot_general(left, right, (((0,), (0,)), ((), ())), preferred_element_type=F32)


def params(mib):
    return pltpu.CompilerParams(vmem_limit_bytes=mib << 20)


def cost(flops, nbytes):
    return pl.CostEstimate(flops=flops, bytes_accessed=nbytes, transcendentals=0)


def normed(values):
    centre = values - jnp.mean(values, axis=-1, keepdims=True)
    scale = lax.rsqrt(jnp.mean(centre * centre, axis=-1, keepdims=True) + 1e-05)
    return centre * scale, scale


def norm_back(grad, gain_vec, hat, scale):
    inner = grad * gain_vec
    return scale * (
        inner
        - jnp.mean(inner, axis=-1, keepdims=True)
        - hat * jnp.mean(inner * hat, axis=-1, keepdims=True)
    )


def flat(ref):
    value = ref[...]
    return value.reshape(-1, value.shape[-1])


def resident(shape):
    zeros = (0,) * len(shape)
    return pl.BlockSpec(shape, lambda *_: zeros, pipeline_mode=pl.Buffered(1))


def tile_spec(gathered, rows, t):
    devices, _, width = gathered.shape
    return pl.BlockSpec((devices, rows, width), lambda *_: (0, t, 0), pipeline_mode=pl.Buffered(1))


def kv_kernel(x_ref, gain_ref, bias_ref, wk_ref, wv_ref, h_ref, kv_ref):
    hat, _ = normed(x_ref[...].astype(F32))
    low = (hat * gain_ref[...] + bias_ref[...]).astype(BF16)
    h_ref[...] = low
    kv_ref[0] = dot_nn(low, flat(wk_ref)).astype(BF16)
    kv_ref[1] = dot_nn(low, flat(wv_ref)).astype(BF16)


def kv_call(x, gain, bias, gathered, rows):
    n, d = x.shape
    return pl.pallas_call(
        kv_kernel,
        grid=(n // ROWS,),
        in_specs=[
            pl.BlockSpec((ROWS, d), lambda i: (i, 0)),
            resident((1, d)),
            resident((1, d)),
            tile_spec(gathered, rows, 1),
            tile_spec(gathered, rows, 2),
        ],
        out_specs=[
            pl.BlockSpec((ROWS, d), lambda i: (i, 0)),
            pl.BlockSpec((2, ROWS, d), lambda i: (0, i, 0)),
        ],
        out_shape=[jax.ShapeDtypeStruct((n, d), BF16), jax.ShapeDtypeStruct((2, n, d), BF16)],
        compiler_params=params(40),
        cost_estimate=cost(4 * n * d * d, 4 * d * d + 8 * n * d),
        name="kv_proj",
    )(x, gain, bias, gathered, gathered)


def q_kernel(h_ref, wq_ref, q_ref):
    q_ref[...] = (dot_nn(h_ref[...], flat(wq_ref)).astype(BF16).astype(F32) * 0.125).astype(BF16)


def q_call(h, gathered, rows):
    n, d = h.shape
    return pl.pallas_call(
        q_kernel,
        grid=(n // ROWS,),
        in_specs=[pl.BlockSpec((ROWS, d), lambda i: (i, 0)), tile_spec(gathered, rows, 0)],
        out_specs=pl.BlockSpec((ROWS, d), lambda i: (i, 0)),
        out_shape=jax.ShapeDtypeStruct((n, d), BF16),
        compiler_params=params(32),
        cost_estimate=cost(2 * n * d * d, 2 * d * d + 4 * n * d),
        name="q_proj",
    )(h, gathered)


def stack_heads(block):
    lane = lax.broadcasted_iota(jnp.int32, block.shape, 1) // HEAD_DIM
    zero = jnp.zeros_like(block)
    return jnp.concatenate([jnp.where(lane == h, block, zero) for h in range(GROUP)], axis=0)


def head_cols(value, h, width):
    return value[:, h * width : (h + 1) * width]


def head_rows(value, h):
    return value[h * HEAD_DIM : (h + 1) * HEAD_DIM, :]


def attend_kernel(bq, bk, tab, q_ref, ko_ref, vo_ref, kp_ref, vp_ref, sq_ref, so_ref, sp_ref, o_ref, lse_ref):
    i = pl.program_id(1)
    stacked = stack_heads(q_ref[...])
    seg_q = jnp.concatenate([sq_ref[0]] * GROUP, axis=1)

    def over(k_ref, v_ref, s_ref, first, count, state):
        def step(j, carry):
            top, total, acc = carry
            at = pl.multiple_of((first + j) * bk, bk)
            scores = dot_nt(k_ref[0, pl.ds(at, bk), :], stacked)
            scores = jnp.where(s_ref[pl.ds(at, bk), :] == seg_q, scores, NEG)
            new_top = jnp.maximum(top, jnp.max(scores, axis=0, keepdims=True))
            decay = jnp.exp(top - new_top)
            probs = jnp.exp(scores - new_top)
            total = total * decay + jnp.sum(probs, axis=0, keepdims=True)
            low = probs.astype(BF16)
            values = v_ref[0, pl.ds(at, bk), :].T
            acc = tuple(
                acc[h] * head_cols(decay, h, bq) + dot_nn(head_rows(values, h), head_cols(low, h, bq))
                for h in range(GROUP)
            )
            return new_top, total, acc

        return lax.fori_loop(0, count, step, state)

    state = (
        jnp.full((1, GROUP * bq), -jnp.inf, F32),
        jnp.zeros((1, GROUP * bq), F32),
        tuple(jnp.zeros((HEAD_DIM, bq), F32) for _ in range(GROUP)),
    )
    state = over(ko_ref, vo_ref, so_ref, tab[4 * i], tab[4 * i + 1], state)
    top, total, acc = over(kp_ref, vp_ref, sp_ref, tab[4 * i + 2], tab[4 * i + 3], state)
    out = jnp.concatenate([acc[h] / head_cols(total, h, bq) for h in range(GROUP)], axis=0)
    o_ref[...] = out.T.astype(BF16)
    lse_ref[0, 0] = top + jnp.log(total)


def attend_call(tab, q, own, other, seg_q, seg_own, seg_other, bq, bk):
    n, d = q.shape
    groups, blocks = d // GROUP_WIDTH, n // bq
    query = pl.BlockSpec((bq, GROUP_WIDTH), lambda g, i, *_: (i, g))

    def half(which):
        return pl.BlockSpec((1, n, GROUP_WIDTH), lambda g, i, *_: (which, 0, g))

    column = pl.BlockSpec((n, 1), lambda g, i, *_: (0, 0))
    spec = pltpu.PrefetchScalarGridSpec(
        num_scalar_prefetch=1,
        grid=(groups, blocks),
        in_specs=[
            query,
            half(0),
            half(1),
            half(0),
            half(1),
            pl.BlockSpec((1, 1, bq), lambda g, i, *_: (i, 0, 0)),
            column,
            column,
        ],
        out_specs=[query, pl.BlockSpec((1, 1, 1, GROUP * bq), lambda g, i, *_: (g, i, 0, 0))],
    )
    return pl.pallas_call(
        partial(attend_kernel, bq, bk),
        grid_spec=spec,
        out_shape=[
            jax.ShapeDtypeStruct((n, d), BF16),
            jax.ShapeDtypeStruct((groups, blocks, 1, GROUP * bq), F32),
        ],
        compiler_params=params(56),
        cost_estimate=cost(30_000_000_000, 12 * n * d),
        name="attend",
    )(tab, q, own, own, other, other, seg_q, seg_own, seg_other)


def attend_back_kernel(
    bq, bk, tab, q_ref, go_ref, o_ref, ko_ref, vo_ref, kp_ref, vp_ref, sq_ref, so_ref, sp_ref, lse_ref,
    dq_ref, down_ref, dpart_ref, dko, dvo, dkp, dvp,
):
    i = pl.program_id(1)

    @pl.when(i == 0)
    def _():
        for ref in (dko, dvo, dkp, dvp):
            ref[...] = jnp.zeros_like(ref)

    stacked = stack_heads(q_ref[...])
    grad = go_ref[...]
    stacked_grad = stack_heads(grad)
    product = (grad.astype(F32) * o_ref[...].astype(F32)).T
    inner = jnp.concatenate(
        [jnp.sum(head_rows(product, h), axis=0, keepdims=True) for h in range(GROUP)], axis=1
    )
    seg_q = jnp.concatenate([sq_ref[0]] * GROUP, axis=1)
    lse = lse_ref[0, 0]

    def over(k_ref, v_ref, s_ref, dk, dv, first, count, state):
        def step(j, acc):
            at = pl.multiple_of((first + j) * bk, bk)
            keys = k_ref[0, pl.ds(at, bk), :]
            scores = dot_nt(keys, stacked)
            scores = jnp.where(s_ref[pl.ds(at, bk), :] == seg_q, scores, NEG)
            probs = jnp.exp(scores - lse)
            grad_probs = dot_nt(v_ref[0, pl.ds(at, bk), :], stacked_grad)
            grad_scores = (probs * (grad_probs - inner)).astype(BF16)
            dv[pl.ds(at, bk), :] += dot_nn(probs.astype(BF16), stacked_grad)
            dk[pl.ds(at, bk), :] += dot_nn(grad_scores, stacked)
            keys_t = keys.T
            return tuple(
                acc[h] + dot_nn(head_rows(keys_t, h), head_cols(grad_scores, h, bq)) for h in range(GROUP)
            )

        return lax.fori_loop(0, count, step, state)

    state = tuple(jnp.zeros((HEAD_DIM, bq), F32) for _ in range(GROUP))
    state = over(ko_ref, vo_ref, so_ref, dko, dvo, tab[4 * i], tab[4 * i + 1], state)
    state = over(kp_ref, vp_ref, sp_ref, dkp, dvp, tab[4 * i + 2], tab[4 * i + 3], state)
    dq_ref[...] = (jnp.concatenate(state, axis=0).T * 0.125).astype(BF16)

    @pl.when(i == pl.num_programs(1) - 1)
    def _():
        down_ref[0] = dko[...].astype(BF16)
        down_ref[1] = dvo[...].astype(BF16)
        dpart_ref[0] = dkp[...].astype(BF16)
        dpart_ref[1] = dvp[...].astype(BF16)


def attend_back_call(tab, q, grad, out, own, other, seg_q, seg_own, seg_other, lse, bq, bk, g):
    n, d = q.shape
    blocks = n // bq
    query = pl.BlockSpec((bq, GROUP_WIDTH), lambda _, i, *__: (i, g))

    def half(which):
        return pl.BlockSpec((1, n, GROUP_WIDTH), lambda *_: (which, 0, g))

    column = pl.BlockSpec((n, 1), lambda *_: (0, 0))
    pair = pl.BlockSpec((2, n, GROUP_WIDTH), lambda *_: (0, 0, 0))
    spec = pltpu.PrefetchScalarGridSpec(
        num_scalar_prefetch=1,
        grid=(1, blocks),
        in_specs=[
            query,
            query,
            query,
            half(0),
            half(1),
            half(0),
            half(1),
            pl.BlockSpec((1, 1, bq), lambda _, i, *__: (i, 0, 0)),
            column,
            column,
            pl.BlockSpec((1, 1, 1, GROUP * bq), lambda _, i, *__: (g, i, 0, 0)),
        ],
        out_specs=[pl.BlockSpec((bq, GROUP_WIDTH), lambda _, i, *__: (i, 0)), pair, pair],
        scratch_shapes=[pltpu.VMEM((n, GROUP_WIDTH), F32)] * 4,
    )
    return pl.pallas_call(
        partial(attend_back_kernel, bq, bk),
        grid_spec=spec,
        out_shape=[
            jax.ShapeDtypeStruct((n, GROUP_WIDTH), BF16),
            jax.ShapeDtypeStruct((2, n, GROUP_WIDTH), BF16),
            jax.ShapeDtypeStruct((2, n, GROUP_WIDTH), BF16),
        ],
        compiler_params=params(56),
        cost_estimate=cost(12_000_000_000, 6 * n * d),
        name="attend_back",
    )(tab, q, grad, out, own, own, other, other, seg_q, seg_own, seg_other, lse)


def mid_kernel(x_ref, o_ref, wo_ref, gain_ref, bias_ref, r_ref, h_ref):
    mid = x_ref[...].astype(F32) + dot_nn(o_ref[...], flat(wo_ref))
    r_ref[...] = mid
    hat, _ = normed(mid)
    h_ref[...] = (hat * gain_ref[...] + bias_ref[...]).astype(BF16)


def mid_call(x, o, gathered, rows, t, gain, bias):
    n, d = x.shape
    row = pl.BlockSpec((ROWS, d), lambda i: (i, 0))
    return pl.pallas_call(
        mid_kernel,
        grid=(n // ROWS,),
        in_specs=[row, row, tile_spec(gathered, rows, t), resident((1, d)), resident((1, d))],
        out_specs=[row, row],
        out_shape=[jax.ShapeDtypeStruct((n, d), F32), jax.ShapeDtypeStruct((n, d), BF16)],
        compiler_params=params(32),
        cost_estimate=cost(2 * n * d * d, 2 * d * d + 10 * n * d),
        name="out_proj",
    )(x, o, gathered, gain, bias)


def mid_back_kernel(me, gh_ref, r_ref, g_ref, o_ref, wo_ref, gain_ref, gr_ref, go_ref, keep_ref, send_ref, dln_ref, acc):
    i = pl.program_id(0)
    hat, scale = normed(r_ref[...])
    grad = gh_ref[...]
    total = g_ref[...].astype(F32) + norm_back(grad, gain_ref[...], hat, scale)
    gr_ref[...] = total
    low = total.astype(BF16)
    go_ref[...] = dot_nt(low, flat(wo_ref)).astype(BF16)
    part = dot_tn(o_ref[...], low)
    dgain = jnp.sum(grad * hat, axis=0, keepdims=True)
    dbias = jnp.sum(grad, axis=0, keepdims=True)

    @pl.when(i == 0)
    def _():
        acc[...] = part
        dln_ref[0:1, :] = dgain
        dln_ref[1:2, :] = dbias

    @pl.when(i > 0)
    def _():
        acc[...] += part
        dln_ref[0:1, :] += dgain
        dln_ref[1:2, :] += dbias

    @pl.when(i == pl.num_programs(0) - 1)
    def _():
        lanes = keep_ref.shape[3]
        for ref, value in zip(
            (keep_ref, send_ref), split_pairs(acc[...].astype(BF16), keep_ref.shape[1], me[0]), strict=True
        ):
            for t in range(ref.shape[0]):
                ref[t] = value[:, :, t * lanes : (t + 1) * lanes]


def mid_back_call(me, grad, mid, cot, o, gathered, rows, t, gain, groups):
    n, d = mid.shape
    row = pl.BlockSpec((ROWS, d), lambda i, *_: (i, 0))
    share = (d // GROUP_WIDTH, groups, d // (2 * groups), GROUP_WIDTH)
    spec = pltpu.PrefetchScalarGridSpec(
        num_scalar_prefetch=1,
        grid=(n // ROWS,),
        in_specs=[row, row, row, row, tile_spec(gathered, rows, t), resident((1, d))],
        out_specs=[
            row,
            row,
            pl.BlockSpec(share, lambda *_: (0, 0, 0, 0)),
            pl.BlockSpec(share, lambda *_: (0, 0, 0, 0)),
            pl.BlockSpec((2, d), lambda *_: (0, 0)),
        ],
        scratch_shapes=[pltpu.VMEM((d, d), F32)],
    )
    return pl.pallas_call(
        mid_back_kernel,
        grid_spec=spec,
        out_shape=[
            jax.ShapeDtypeStruct((n, d), F32),
            jax.ShapeDtypeStruct((n, d), BF16),
            jax.ShapeDtypeStruct(share, BF16),
            jax.ShapeDtypeStruct(share, BF16),
            jax.ShapeDtypeStruct((2, d), F32),
        ],
        compiler_params=params(48),
        cost_estimate=cost(4 * n * d * d, 4 * d * d + 18 * n * d),
        name="out_proj_back",
    )(me, grad, mid, cot, o, gathered, gain)


def split_pairs(value, groups, my_index):
    rows = value.shape[0] // (2 * groups)
    pairs = value.reshape(groups, 2, rows, value.shape[1])
    even, odd = pairs[:, 0], pairs[:, 1]
    first = my_index == 0
    return jnp.where(first, even, odd), jnp.where(first, odd, even)


def ffn_kernel(last, first, aligned, me, *refs):
    h_ref, g_ref, wu_ref, wd_ref, mi_ref = refs[:5]
    refs = refs[5:]
    gi_ref = None
    if not first:
        gi_ref, refs = refs[0], refs[1:]
    mo_ref, go_ref = refs[:2]
    refs = refs[2:]
    grads, rest = (refs[:4], refs[4:]) if aligned else (refs[:2], refs[2:])
    j = pl.program_id(0)
    h, grad = h_ref[...], g_ref[...]
    wu, wd = flat(wu_ref), flat(wd_ref)
    up = dot_nn(h, wu)
    cdf = 0.5 * (1.0 + lax.erf(up * 0.7071067811865476))
    act = (up * cdf).astype(BF16)
    slope = cdf + up * (jnp.exp(-0.5 * up * up) * 0.3989422804014327)
    gu = (dot_nt(grad, wd) * slope).astype(BF16)
    dwd = dot_tn(act, grad).astype(BF16)
    dwu = dot_tn(h, gu).astype(BF16)
    if aligned:
        my_index = me[0]
        grads[0][...], grads[1][...] = split_pairs(dwu, grads[0].shape[0], my_index)
        for ref, value in zip(grads[2:], split_pairs(dwd, grads[2].shape[1], my_index), strict=True):
            for t in range(ref.shape[0]):
                ref[t] = value[:, t * ref.shape[2] : (t + 1) * ref.shape[2]]
    else:
        grads[0][...] = dwu
        grads[1][...] = dwd
    mo = rest[0] if last else mo_ref

    @pl.when(j == 0)
    def _():
        mo[...] = mi_ref[...] + dot_nn(act, wd)
        if first:
            go_ref[...] = dot_nt(gu, wu)
        else:
            go_ref[...] = gi_ref[...] + dot_nt(gu, wu)

    @pl.when(j > 0)
    def _():
        mo[...] += dot_nn(act, wd)
        go_ref[...] += dot_nt(gu, wu)

    if last:

        @pl.when(j == pl.num_programs(0) - 1)
        def _():
            mo_ref[...] = mo[...].astype(BF16)


def ffn_call(me, h, cot, wu, wd, mid, gmid, grad_specs, width, last, aligned):
    n, d = h.shape
    full = resident((n, d))
    const = pl.BlockSpec((n, d), lambda j, *_: (0, 0))
    in_specs = [full, full, wu[1], wd[1], full]
    args = [h, cot, wu[0], wd[0], mid]
    aliases = {} if last else {5: 0}
    if gmid is not None:
        in_specs.append(full)
        args.append(gmid)
        aliases[6] = 1
    spec = pltpu.PrefetchScalarGridSpec(
        num_scalar_prefetch=1,
        grid=(width // FF_COLS,),
        in_specs=in_specs,
        out_specs=[const, const] + [g[0] for g in grad_specs],
        scratch_shapes=[pltpu.VMEM((n, d), F32)] if last else [],
    )
    return pl.pallas_call(
        partial(ffn_kernel, last, gmid is None, aligned),
        grid_spec=spec,
        out_shape=[
            jax.ShapeDtypeStruct((n, d), BF16 if last else F32),
            jax.ShapeDtypeStruct((n, d), F32),
        ]
        + [g[1] for g in grad_specs],
        input_output_aliases=aliases,
        compiler_params=params(60),
        cost_estimate=cost(12 * n * d * width, 8 * d * width + 20 * n * d),
        name="ffn",
    )(me, *args)


def qkv_grad_kernel(groups, me, h_ref, dq_ref, dkv_ref, rkv_ref, keep_ref, send_ref, sum_ref):
    h = h_ref[...]
    my_index = me[0]
    keep_ref[0], send_ref[0] = split_pairs(dot_tn(h, dq_ref[...]).astype(BF16), groups, my_index)
    for t in range(2):
        grad = (dkv_ref[t].astype(F32) + rkv_ref[t].astype(F32)).astype(BF16)
        sum_ref[t] = grad
        keep_ref[t + 1], send_ref[t + 1] = split_pairs(dot_tn(h, grad).astype(BF16), groups, my_index)


def qkv_grad_call(me, h, dq, dkv, rkv, groups):
    n, d = h.shape
    width = dq.shape[1]
    rows = d // (2 * groups)
    whole = pl.BlockSpec(memory_space=pltpu.VMEM)
    out = jax.ShapeDtypeStruct((3, groups, rows, width), BF16)
    return pl.pallas_call(
        partial(qkv_grad_kernel, groups),
        in_specs=[pl.BlockSpec(memory_space=pltpu.SMEM)] + [whole] * 4,
        out_specs=[whole] * 3,
        out_shape=[out, out, jax.ShapeDtypeStruct((2, n, width), BF16)],
        compiler_params=params(40),
        cost_estimate=cost(6 * n * d * width, 6 * d * width + 2 * n * d + 8 * n * width),
        name="qkv_grad",
    )(me, h, dq, dkv, rkv)


def head_back_kernel(count, *refs):
    dqs, dkvs = refs[:count], refs[count : 2 * count]
    x_ref, gr_ref, wq_ref, wk_ref, wv_ref, gain_ref, tg_ref, dln_ref = refs[2 * count :]
    i = pl.program_id(0)
    dq = jnp.concatenate([r[...] for r in dqs], axis=1)
    dk = jnp.concatenate([r[0] for r in dkvs], axis=1)
    dv = jnp.concatenate([r[1] for r in dkvs], axis=1)
    grad = dot_nt(dq, flat(wq_ref)) + dot_nt(dk, flat(wk_ref)) + dot_nt(dv, flat(wv_ref))
    hat, scale = normed(x_ref[...].astype(F32))
    tg_ref[...] = (gr_ref[...] + norm_back(grad, gain_ref[...], hat, scale)).astype(BF16)
    dgain = jnp.sum(grad * hat, axis=0, keepdims=True)
    dbias = jnp.sum(grad, axis=0, keepdims=True)

    @pl.when(i == 0)
    def _():
        dln_ref[0:1, :] = dgain
        dln_ref[1:2, :] = dbias

    @pl.when(i > 0)
    def _():
        dln_ref[0:1, :] += dgain
        dln_ref[1:2, :] += dbias


def head_back_call(dqs, dkvs, x, gr, gathered, rows, gain):
    n, d = x.shape
    row = pl.BlockSpec((ROWS, d), lambda i: (i, 0))
    width = dqs[0].shape[1]
    return pl.pallas_call(
        partial(head_back_kernel, len(dqs)),
        grid=(n // ROWS,),
        in_specs=[pl.BlockSpec((ROWS, width), lambda i: (i, 0))] * len(dqs)
        + [pl.BlockSpec((2, ROWS, width), lambda i: (0, i, 0))] * len(dkvs)
        + [
            row,
            row,
            tile_spec(gathered, rows, 0),
            tile_spec(gathered, rows, 1),
            tile_spec(gathered, rows, 2),
            resident((1, d)),
        ],
        out_specs=[row, pl.BlockSpec((2, d), lambda i: (0, 0))],
        out_shape=[jax.ShapeDtypeStruct((n, d), BF16), jax.ShapeDtypeStruct((2, d), F32)],
        compiler_params=params(48),
        cost_estimate=cost(6 * n * d * d, 6 * d * d + 14 * n * d),
        name="qkv_back",
    )(*dqs, *dkvs, x, gr, gathered, gathered, gathered, gain)


class Term:
    def __init__(self, array, axes, first=0, count=None):
        self.array, self.axes, self.first = array, axes, first
        self.count = array.shape[0] if count is None else count

    def pick(self, mine, settled, flipped):
        starts, sizes = [self.first], [self.count]
        for b in self.axes:
            fixed = b in settled or b == flipped
            starts.append((1 - mine[b] if b == flipped else mine[b]) if fixed else 0)
            sizes.append(1 if fixed else 2)
        shape = self.array.shape[-2:]
        piece = lax.dynamic_slice(self.array, starts + [0, 0], sizes + list(shape))
        return piece.reshape((self.count,) + (2,) * sizes[1:].count(2) + shape).astype(F32)


class Cube:
    def __init__(self, dp, index):
        self.bits = dp.bit_length() - 1
        self.dp = dp
        self.mine = [(index >> b) & 1 for b in range(self.bits)]

    def swap(self, array, bit):
        return lax.ppermute(array, "dp", [(i, i ^ (1 << bit)) for i in range(self.dp)])

    def terms(self, arrays, first=0, count=None):
        made = []
        for array in arrays:
            lead, _, rows, width = array.shape
            shape = (lead,) + (2,) * self.bits + (rows, width)
            made.append(Term(array.reshape(shape), list(range(self.bits))[::-1], first, count))
        return made

    def total(self, terms, settled, flipped=None):
        out = terms[0].pick(self.mine, settled, flipped)
        for term in terms[1:]:
            out = out + term.pick(self.mine, settled, flipped)
        return out


class Scatter:
    def __init__(self, cube, one, two):
        self.cube, self.sides, self.step = cube, (one, two), 0
        self.settled = [[], []]
        self.last = []

    def advance(self):
        bit = self.step
        if self.step < 2:
            plan = [((0,), bit), ((1,), 1 - bit)]
        else:
            plan = [((0, 1), bit)]
        self.last = []
        for sides, bit in plan:
            streams = [(s, stream) for s in sides for stream in self.sides[s]]
            sent = [self.cube.total(stream, self.settled[s], bit).astype(BF16) for s, stream in streams]
            got = self.cube.swap(sent[0] if len(sent) == 1 else jnp.concatenate(sent, axis=0), bit)
            self.last.append(got)
            at = 0
            for s, stream in streams:
                count = stream[0].count
                axes = [b for b in stream[0].axes if b not in self.settled[s] and b != bit]
                stream.append(Term(got, axes, at, count))
                at += count
            for s in sides:
                self.settled[s].append(bit)
        self.step += 1
        return self

    def finish(self):
        while self.step < self.cube.bits:
            self.advance()
        return [[self.cube.total(stream, self.settled[s]) for stream in self.sides[s]] for s in range(2)]


def gate(value, *others):
    return lax.optimization_barrier((value, others))[0]


def block_table(seg_full, seg_local, my_index, n, bq, bk):
    first, last = seg_local[::bq], seg_local[bq - 1 :: bq]
    low = jnp.sum((seg_full[None, :] < first[:, None]).astype(jnp.int32), axis=1)
    high = jnp.sum((seg_full[None, :] <= last[:, None]).astype(jnp.int32), axis=1)
    columns = []
    for index in (my_index, 1 - my_index):
        start = jnp.clip(low - index * n, 0, n)
        stop = jnp.clip(high - index * n, 0, n)
        block = start // bk
        columns += [block, jnp.where(stop > start, (stop + bk - 1) // bk - block, 0)]
    return jnp.stack(columns, axis=1).reshape(-1).astype(jnp.int32)


def body(
    tokens,
    segments,
    ln1_gain,
    ln1_bias,
    w_query,
    w_key,
    w_value,
    w_out,
    ln2_gain,
    ln2_bias,
    w_up,
    w_down,
    cotangent,
):
    x = tokens[0]
    n, d = x.shape
    cot = cotangent[0]
    rows = w_query.shape[0]
    devices = d // rows
    hidden = w_up.shape[1]
    per_device = hidden // devices
    parts = 2
    sub = per_device // parts
    width = hidden // parts
    my_index = lax.axis_index("seq")
    seg_full = segments[0]
    seg_local = lax.dynamic_slice_in_dim(seg_full, my_index * n, n)
    seg_other = lax.dynamic_slice_in_dim(seg_full, (1 - my_index) * n, n)
    tab = block_table(seg_full, seg_local, my_index, n, ATT_Q, ATT_K)
    seg_q = seg_local.reshape(n // ATT_Q, 1, ATT_Q)
    seg_own_col, seg_other_col = seg_local[:, None], seg_other[:, None]

    vectors = jnp.concatenate([ln1_gain, ln1_bias, ln2_gain, ln2_bias]).reshape(1, 4 * rows)
    ln_block = jnp.pad(vectors, ((0, LN_ROWS - 1), (0, d - 4 * rows)))
    first_local = jnp.concatenate([w_query, w_key, w_value, ln_block], axis=0)
    up_parts = w_up.reshape(rows, devices, parts, sub).transpose(2, 0, 1, 3).reshape(parts, rows, width // d, d)
    up_parts = up_parts.transpose(0, 2, 1, 3).reshape(parts, (width // d) * rows, d)
    part_local = [
        jnp.concatenate([up_parts[p], w_down[p * sub : (p + 1) * sub]], axis=0) for p in range(parts)
    ]
    part_local[0] = jnp.concatenate([part_local[0], w_out], axis=0)

    def gather(local):
        out = lax.all_gather(local, BOTH, axis=0, tiled=True)
        return out.reshape(devices, local.shape[0], d)

    first = gather(first_local)
    second = [gather(p) for p in part_local]

    aligned = rows % 16 == 0
    if aligned:
        qkv_w, qkv_rows = first, rows
        out_w, out_t, out_rows = second[0], second[0].shape[1] // rows - 1, rows
    else:
        qkv_w = first[:, : 3 * rows].reshape(devices, 3, rows, d).transpose(1, 0, 2, 3).reshape(1, 3 * d, d)
        qkv_rows = d
        out_w, out_t, out_rows = second[0][:, -rows:].reshape(1, d, d), 0, d
    ln = first[:, 3 * rows, : 4 * rows].reshape(devices, 4, rows).transpose(1, 0, 2).reshape(4, 1, d).astype(F32)

    h1, own = kv_call(x, ln[0], ln[1], qkv_w, qkv_rows)
    swap = [(0, 1), (1, 0)]
    other = lax.ppermute(own, "seq", swap)
    q = q_call(h1, qkv_w, qkv_rows)
    attended, lse = attend_call(tab, q, own, other, seg_q, seg_own_col, seg_other_col, ATT_Q, ATT_K)
    mid, h2 = mid_call(x, attended, out_w, out_rows, out_t, ln[2], ln[3])

    dp = devices // 2
    cube = Cube(dp, lax.axis_index("dp"))
    me = my_index.reshape(1).astype(jnp.int32)

    def exchange(value):
        return lax.ppermute(value, "seq", swap)

    def halves(value, axis):
        keep = lax.dynamic_index_in_dim(value, my_index, axis, keepdims=False)
        send = lax.dynamic_index_in_dim(value, 1 - my_index, axis, keepdims=False)
        return keep, send

    up_rows = (width // d) * rows
    tiles = width // d
    group = FF_COLS // sub
    carry, gmid, ffn, crossed = mid, None, [], []
    for p in range(parts):
        if aligned:
            per_tile = d // FF_COLS
            tile = up_rows // sub
            wu = (second[p], pl.BlockSpec((devices, rows, FF_COLS), lambda j, *_: (0, j // per_tile, j % per_tile)))
            wd = (second[p], pl.BlockSpec((group, sub, d), lambda j, *_: (j, tile, 0)))
            up_out = (
                pl.BlockSpec((None, dp, rows, FF_COLS), lambda j, *_: (j // per_tile, 0, 0, j % per_tile)),
                jax.ShapeDtypeStruct((tiles, dp, rows, d), BF16),
            )
            down_out = (
                pl.BlockSpec((tiles, group // 2, rows, d), lambda j, *_: (0, j, 0, 0)),
                jax.ShapeDtypeStruct((tiles, dp, rows, d), BF16),
            )
            grad_specs = [up_out, up_out, down_out, down_out]
        else:
            up_w = second[p][:, :up_rows].reshape(devices, tiles, rows, d).transpose(0, 2, 1, 3).reshape(d, width)
            down_w = second[p][:, up_rows : up_rows + sub].reshape(width, d)
            up_block = pl.BlockSpec((d, FF_COLS), lambda j, *_: (0, j))
            down_block = pl.BlockSpec((FF_COLS, d), lambda j, *_: (j, 0))
            wu, wd = (up_w, up_block), (down_w, down_block)
            grad_specs = [
                (up_block, jax.ShapeDtypeStruct((d, width), BF16)),
                (down_block, jax.ShapeDtypeStruct((width, d), BF16)),
            ]
        carry, gmid, *grads = ffn_call(
            me, h2, cot, wu, wd, carry, gmid, grad_specs, width, p == parts - 1, aligned
        )
        if not aligned:
            dwu = grads[0].reshape(dp, 2, rows, tiles, d).transpose(3, 0, 1, 2, 4)
            dwd = grads[1].reshape(dp, 2, tiles, rows, d).transpose(2, 0, 1, 3, 4)
            grads = [*halves(dwu, 2), *halves(dwd, 2)]
        keep_up, send_up, keep_down, send_down = grads
        crossed.append((exchange(send_up), exchange(send_down)))
        ffn.append(
            Scatter(cube, [cube.terms([keep_up, crossed[p][0]])], [cube.terms([keep_down, crossed[p][1]])])
        )
    mixed = carry

    early, late = ffn
    gmid = gate(gmid, crossed[0])
    early.advance()
    grad_mid, grad_att, keep_out, send_out, dln2 = mid_back_call(
        me, gmid, mid, cot, attended, out_w, out_rows, out_t, ln[2], dp
    )
    got_out = exchange(send_out)
    late.advance()
    dqs, dkvs, qkv_terms, raw = [], [], [], []

    def finish_group(g):
        dq, dkv, got = raw[g]
        keep, send, dkv = qkv_grad_call(me, h1, dq, dkv, got, dp)
        dqs.append(dq)
        dkvs.append(dkv)
        qkv_terms.append([keep, exchange(send)])
        return dkv

    def attend_group(g, *waited):
        dq, dkv, sent = attend_back_call(
            gate(tab, *waited), q, grad_att, attended, own, other, seg_q, seg_own_col, seg_other_col, lse,
            ATT_Q, ATT_K, g,
        )
        raw.append((dq, dkv, exchange(sent)))

    attend_group(0, crossed[1])
    waited = early.last
    early.advance()
    attend_group(1, waited)
    done = finish_group(0)
    waited = early.last + late.last + [done]
    early.advance()
    late.advance()
    attend_group(2, waited)
    done = finish_group(1)
    tail_one = Scatter(
        cube,
        [cube.terms(qkv_terms[0]), cube.terms([keep_out, got_out], 0, 2)],
        [cube.terms(qkv_terms[1]), cube.terms([keep_out, got_out], 2, 2)],
    )
    waited = early.last + late.last + [done]
    early.advance()
    late.advance()
    tail_one.advance()
    attend_group(3, waited)
    finish_group(2)
    finish_group(3)
    tail_two = Scatter(cube, [cube.terms(qkv_terms[2])], [cube.terms(qkv_terms[3])])
    waited = early.last + late.last + tail_one.last
    late.advance()
    tail_one.advance()
    tail_two.advance()
    token_grad, dln1 = head_back_call(dqs, dkvs, x, gate(grad_mid, *waited), qkv_w, qkv_rows, ln[0])

    dln = jnp.concatenate([dln1, dln2], axis=0).reshape(4, dp, 2, rows).transpose(2, 1, 0, 3)
    keep, send = halves(dln.reshape(2, dp, 4 * rows), 0)
    dln = keep + exchange(send)
    for b in range(cube.bits)[::-1]:
        pair = dln.reshape(2, -1, 4 * rows)
        sent = lax.dynamic_index_in_dim(pair, 1 - cube.mine[b], 0, keepdims=False)
        dln = lax.dynamic_index_in_dim(pair, cube.mine[b], 0, keepdims=False) + cube.swap(sent, b)
    dln = dln.reshape(4, rows)

    ffn_sums = [f.finish() for f in ffn]
    (one_a, one_b), (two_a, two_b) = tail_one.finish(), tail_two.finish()
    up_share = jnp.stack([s[0][0] for s in ffn_sums]).reshape(parts, tiles, rows, devices // tiles, sub)
    up_share = up_share.transpose(2, 1, 3, 0, 4).reshape(rows, hidden)
    down_share = jnp.concatenate([s[1][0].reshape(sub, d) for s in ffn_sums], axis=0)
    qkv_share = jnp.concatenate([one_a[0], one_b[0], two_a[0], two_b[0]], axis=-1)
    out_share = jnp.concatenate([one_a[1], one_b[1]], axis=0).transpose(1, 0, 2).reshape(rows, d)
    return (
        mixed[None],
        token_grad[None],
        dln[0],
        dln[1],
        qkv_share[0],
        qkv_share[1],
        qkv_share[2],
        out_share,
        dln[2],
        dln[3],
        up_share,
        down_share,
    )


def solution(mesh):
    row, act, vec = P(BOTH, None), P("dp", "seq", None), P(BOTH)
    in_specs = (act, P("dp", None), vec, vec, row, row, row, row, vec, vec, row, row, act)
    out_specs = (act, act, vec, vec, row, row, row, row, vec, vec, row, row)
    return jax.shard_map(body, mesh=mesh, in_specs=in_specs, out_specs=out_specs, check_vma=False)
```

```python
import math
from functools import partial

import jax
import jax.numpy as jnp
from jax import lax
from jax.experimental import pallas as pl
from jax.experimental.pallas import tpu as pltpu
from jax.sharding import PartitionSpec as P

BF16 = jnp.bfloat16
F32 = jnp.float32
HEAD_DIM = 64
GROUP = 4
GROUP_WIDTH = GROUP * HEAD_DIM
NEG = -1000000000.0
BOTH = ("dp", "seq")
LN_ROWS = 16
ATT_Q = 256
ATT_K = 512
ROWS = 256
FF_COLS = 512
COST_SCALE = 100


def dot_nn(left, right):
    return lax.dot_general(left, right, (((1,), (0,)), ((), ())), preferred_element_type=F32)


def dot_nt(left, right):
    return lax.dot_general(left, right, (((1,), (1,)), ((), ())), preferred_element_type=F32)


def dot_tn(left, right):
    return lax.dot_general(left, right, (((0,), (0,)), ((), ())), preferred_element_type=F32)


def params(mib):
    return pltpu.CompilerParams(vmem_limit_bytes=mib << 20)


def cost(flops, nbytes):
    return pl.CostEstimate(flops=flops // COST_SCALE, bytes_accessed=nbytes // COST_SCALE, transcendentals=0)


def normed(values):
    centre = values - jnp.mean(values, axis=-1, keepdims=True)
    scale = lax.rsqrt(jnp.mean(centre * centre, axis=-1, keepdims=True) + 1e-05)
    return centre * scale, scale


def norm_back(grad, gain_vec, hat, scale):
    inner = grad * gain_vec
    return scale * (
        inner
        - jnp.mean(inner, axis=-1, keepdims=True)
        - hat * jnp.mean(inner * hat, axis=-1, keepdims=True)
    )


def flat(ref):
    value = ref[...]
    return value.reshape(-1, value.shape[-1])


def resident(shape):
    zeros = (0,) * len(shape)
    return pl.BlockSpec(shape, lambda *_: zeros, pipeline_mode=pl.Buffered(1))


def tile_spec(gathered, rows, t):
    devices, _, width = gathered.shape
    return pl.BlockSpec((devices, rows, width), lambda *_: (0, t, 0), pipeline_mode=pl.Buffered(1))


def kv_kernel(x_ref, gain_ref, bias_ref, wk_ref, wv_ref, h_ref, kv_ref):
    hat, _ = normed(x_ref[...].astype(F32))
    low = (hat * gain_ref[...] + bias_ref[...]).astype(BF16)
    h_ref[...] = low
    kv_ref[0] = dot_nn(low, flat(wk_ref)).astype(BF16)
    kv_ref[1] = dot_nn(low, flat(wv_ref)).astype(BF16)


def kv_call(x, gain, bias, gathered, rows):
    n, d = x.shape
    return pl.pallas_call(
        kv_kernel,
        grid=(n // ROWS,),
        in_specs=[
            pl.BlockSpec((ROWS, d), lambda i: (i, 0)),
            resident((1, d)),
            resident((1, d)),
            tile_spec(gathered, rows, 1),
            tile_spec(gathered, rows, 2),
        ],
        out_specs=[
            pl.BlockSpec((ROWS, d), lambda i: (i, 0)),
            pl.BlockSpec((2, ROWS, d), lambda i: (0, i, 0)),
        ],
        out_shape=[jax.ShapeDtypeStruct((n, d), BF16), jax.ShapeDtypeStruct((2, n, d), BF16)],
        compiler_params=params(40),
        cost_estimate=cost(4 * n * d * d, 4 * d * d + 8 * n * d),
        name="kv_proj",
    )(x, gain, bias, gathered, gathered)


def q_kernel(h_ref, wq_ref, q_ref):
    q_ref[...] = (dot_nn(h_ref[...], flat(wq_ref)).astype(BF16).astype(F32) * 0.125).astype(BF16)


def q_call(h, gathered, rows):
    n, d = h.shape
    return pl.pallas_call(
        q_kernel,
        grid=(n // ROWS,),
        in_specs=[pl.BlockSpec((ROWS, d), lambda i: (i, 0)), tile_spec(gathered, rows, 0)],
        out_specs=pl.BlockSpec((ROWS, d), lambda i: (i, 0)),
        out_shape=jax.ShapeDtypeStruct((n, d), BF16),
        compiler_params=params(32),
        cost_estimate=cost(2 * n * d * d, 2 * d * d + 4 * n * d),
        name="q_proj",
    )(h, gathered)


def stack_heads(block):
    lane = lax.broadcasted_iota(jnp.int32, block.shape, 1) // HEAD_DIM
    zero = jnp.zeros_like(block)
    return jnp.concatenate([jnp.where(lane == h, block, zero) for h in range(GROUP)], axis=0)


def head_cols(value, h, width):
    return value[:, h * width : (h + 1) * width]


def head_rows(value, h):
    return value[h * HEAD_DIM : (h + 1) * HEAD_DIM, :]


def attend_kernel(bq, bk, tab, q_ref, ko_ref, vo_ref, kp_ref, vp_ref, sq_ref, so_ref, sp_ref, o_ref, lse_ref):
    i = pl.program_id(1)
    stacked = stack_heads(q_ref[...])
    seg_q = jnp.concatenate([sq_ref[0]] * GROUP, axis=1)

    def over(k_ref, v_ref, s_ref, first, count, state):
        def step(j, carry):
            top, total, acc = carry
            at = pl.multiple_of((first + j) * bk, bk)
            scores = dot_nt(k_ref[0, pl.ds(at, bk), :], stacked)
            scores = jnp.where(s_ref[pl.ds(at, bk), :] == seg_q, scores, NEG)
            new_top = jnp.maximum(top, jnp.max(scores, axis=0, keepdims=True))
            decay = jnp.exp(top - new_top)
            probs = jnp.exp(scores - new_top)
            total = total * decay + jnp.sum(probs, axis=0, keepdims=True)
            low = probs.astype(BF16)
            values = v_ref[0, pl.ds(at, bk), :].T
            acc = tuple(
                acc[h] * head_cols(decay, h, bq) + dot_nn(head_rows(values, h), head_cols(low, h, bq))
                for h in range(GROUP)
            )
            return new_top, total, acc

        return lax.fori_loop(0, count, step, state)

    state = (
        jnp.full((1, GROUP * bq), -jnp.inf, F32),
        jnp.zeros((1, GROUP * bq), F32),
        tuple(jnp.zeros((HEAD_DIM, bq), F32) for _ in range(GROUP)),
    )
    state = over(ko_ref, vo_ref, so_ref, tab[4 * i], tab[4 * i + 1], state)
    top, total, acc = over(kp_ref, vp_ref, sp_ref, tab[4 * i + 2], tab[4 * i + 3], state)
    out = jnp.concatenate([acc[h] / head_cols(total, h, bq) for h in range(GROUP)], axis=0)
    o_ref[...] = out.T.astype(BF16)
    lse_ref[0, 0] = top + jnp.log(total)


def attend_call(tab, q, own, other, seg_q, seg_own, seg_other, bq, bk):
    n, d = q.shape
    groups, blocks = d // GROUP_WIDTH, n // bq
    query = pl.BlockSpec((bq, GROUP_WIDTH), lambda g, i, *_: (i, g))

    def half(which):
        return pl.BlockSpec((1, n, GROUP_WIDTH), lambda g, i, *_: (which, 0, g))

    column = pl.BlockSpec((n, 1), lambda g, i, *_: (0, 0))
    spec = pltpu.PrefetchScalarGridSpec(
        num_scalar_prefetch=1,
        grid=(groups, blocks),
        in_specs=[
            query,
            half(0),
            half(1),
            half(0),
            half(1),
            pl.BlockSpec((1, 1, bq), lambda g, i, *_: (i, 0, 0)),
            column,
            column,
        ],
        out_specs=[query, pl.BlockSpec((1, 1, 1, GROUP * bq), lambda g, i, *_: (g, i, 0, 0))],
    )
    return pl.pallas_call(
        partial(attend_kernel, bq, bk),
        grid_spec=spec,
        out_shape=[
            jax.ShapeDtypeStruct((n, d), BF16),
            jax.ShapeDtypeStruct((groups, blocks, 1, GROUP * bq), F32),
        ],
        compiler_params=params(56),
        cost_estimate=cost(30_000_000_000, 12 * n * d),
        name="attend",
    )(tab, q, own, own, other, other, seg_q, seg_own, seg_other)


def attend_back_kernel(
    bq, bk, tab, q_ref, go_ref, o_ref, ko_ref, vo_ref, kp_ref, vp_ref, sq_ref, so_ref, sp_ref, lse_ref,
    dq_ref, down_ref, dpart_ref, dko, dvo, dkp, dvp,
):
    i = pl.program_id(1)

    @pl.when(i == 0)
    def _():
        for ref in (dko, dvo, dkp, dvp):
            ref[...] = jnp.zeros_like(ref)

    stacked = stack_heads(q_ref[...])
    grad = go_ref[...]
    stacked_grad = stack_heads(grad)
    product = (grad.astype(F32) * o_ref[...].astype(F32)).T
    inner = jnp.concatenate(
        [jnp.sum(head_rows(product, h), axis=0, keepdims=True) for h in range(GROUP)], axis=1
    )
    seg_q = jnp.concatenate([sq_ref[0]] * GROUP, axis=1)
    lse = lse_ref[0, 0]

    def over(k_ref, v_ref, s_ref, dk, dv, first, count, state):
        def step(j, acc):
            at = pl.multiple_of((first + j) * bk, bk)
            keys = k_ref[0, pl.ds(at, bk), :]
            scores = dot_nt(keys, stacked)
            scores = jnp.where(s_ref[pl.ds(at, bk), :] == seg_q, scores, NEG)
            probs = jnp.exp(scores - lse)
            grad_probs = dot_nt(v_ref[0, pl.ds(at, bk), :], stacked_grad)
            grad_scores = (probs * (grad_probs - inner)).astype(BF16)
            dv[pl.ds(at, bk), :] += dot_nn(probs.astype(BF16), stacked_grad)
            dk[pl.ds(at, bk), :] += dot_nn(grad_scores, stacked)
            keys_t = keys.T
            return tuple(
                acc[h] + dot_nn(head_rows(keys_t, h), head_cols(grad_scores, h, bq)) for h in range(GROUP)
            )

        return lax.fori_loop(0, count, step, state)

    state = tuple(jnp.zeros((HEAD_DIM, bq), F32) for _ in range(GROUP))
    state = over(ko_ref, vo_ref, so_ref, dko, dvo, tab[4 * i], tab[4 * i + 1], state)
    state = over(kp_ref, vp_ref, sp_ref, dkp, dvp, tab[4 * i + 2], tab[4 * i + 3], state)
    dq_ref[...] = (jnp.concatenate(state, axis=0).T * 0.125).astype(BF16)

    @pl.when(i == pl.num_programs(1) - 1)
    def _():
        down_ref[0] = dko[...].astype(BF16)
        down_ref[1] = dvo[...].astype(BF16)
        dpart_ref[0] = dkp[...].astype(BF16)
        dpart_ref[1] = dvp[...].astype(BF16)


def attend_back_call(tab, q, grad, out, own, other, seg_q, seg_own, seg_other, lse, bq, bk, g):
    n, d = q.shape
    blocks = n // bq
    query = pl.BlockSpec((bq, GROUP_WIDTH), lambda _, i, *__: (i, g))

    def half(which):
        return pl.BlockSpec((1, n, GROUP_WIDTH), lambda *_: (which, 0, g))

    column = pl.BlockSpec((n, 1), lambda *_: (0, 0))
    pair = pl.BlockSpec((2, n, GROUP_WIDTH), lambda *_: (0, 0, 0))
    spec = pltpu.PrefetchScalarGridSpec(
        num_scalar_prefetch=1,
        grid=(1, blocks),
        in_specs=[
            query,
            query,
            query,
            half(0),
            half(1),
            half(0),
            half(1),
            pl.BlockSpec((1, 1, bq), lambda _, i, *__: (i, 0, 0)),
            column,
            column,
            pl.BlockSpec((1, 1, 1, GROUP * bq), lambda _, i, *__: (g, i, 0, 0)),
        ],
        out_specs=[pl.BlockSpec((bq, GROUP_WIDTH), lambda _, i, *__: (i, 0)), pair, pair],
        scratch_shapes=[pltpu.VMEM((n, GROUP_WIDTH), F32)] * 4,
    )
    return pl.pallas_call(
        partial(attend_back_kernel, bq, bk),
        grid_spec=spec,
        out_shape=[
            jax.ShapeDtypeStruct((n, GROUP_WIDTH), BF16),
            jax.ShapeDtypeStruct((2, n, GROUP_WIDTH), BF16),
            jax.ShapeDtypeStruct((2, n, GROUP_WIDTH), BF16),
        ],
        compiler_params=params(56),
        cost_estimate=cost(12_000_000_000, 6 * n * d),
        name="attend_back",
    )(tab, q, grad, out, own, own, other, other, seg_q, seg_own, seg_other, lse)


def mid_kernel(x_ref, o_ref, wo_ref, gain_ref, bias_ref, r_ref, h_ref):
    mid = x_ref[...].astype(F32) + dot_nn(o_ref[...], flat(wo_ref))
    r_ref[...] = mid
    hat, _ = normed(mid)
    h_ref[...] = (hat * gain_ref[...] + bias_ref[...]).astype(BF16)


def mid_call(x, o, gathered, rows, t, gain, bias):
    n, d = x.shape
    row = pl.BlockSpec((ROWS, d), lambda i: (i, 0))
    return pl.pallas_call(
        mid_kernel,
        grid=(n // ROWS,),
        in_specs=[row, row, tile_spec(gathered, rows, t), resident((1, d)), resident((1, d))],
        out_specs=[row, row],
        out_shape=[jax.ShapeDtypeStruct((n, d), F32), jax.ShapeDtypeStruct((n, d), BF16)],
        compiler_params=params(32),
        cost_estimate=cost(2 * n * d * d, 2 * d * d + 10 * n * d),
        name="out_proj",
    )(x, o, gathered, gain, bias)


def mid_back_kernel(me, gh_ref, r_ref, g_ref, o_ref, wo_ref, gain_ref, gr_ref, go_ref, keep_ref, send_ref, dln_ref, acc):
    i = pl.program_id(0)
    hat, scale = normed(r_ref[...])
    grad = gh_ref[...]
    total = g_ref[...].astype(F32) + norm_back(grad, gain_ref[...], hat, scale)
    gr_ref[...] = total
    low = total.astype(BF16)
    go_ref[...] = dot_nt(low, flat(wo_ref)).astype(BF16)
    part = dot_tn(o_ref[...], low)
    dgain = jnp.sum(grad * hat, axis=0, keepdims=True)
    dbias = jnp.sum(grad, axis=0, keepdims=True)

    @pl.when(i == 0)
    def _():
        acc[...] = part
        dln_ref[0:1, :] = dgain
        dln_ref[1:2, :] = dbias

    @pl.when(i > 0)
    def _():
        acc[...] += part
        dln_ref[0:1, :] += dgain
        dln_ref[1:2, :] += dbias

    @pl.when(i == pl.num_programs(0) - 1)
    def _():
        lanes = keep_ref.shape[3]
        for ref, value in zip(
            (keep_ref, send_ref), split_pairs(acc[...].astype(BF16), keep_ref.shape[1], me[0]), strict=True
        ):
            for t in range(ref.shape[0]):
                ref[t] = value[:, :, t * lanes : (t + 1) * lanes]


def mid_back_call(me, grad, mid, cot, o, gathered, rows, t, gain, groups):
    n, d = mid.shape
    row = pl.BlockSpec((ROWS, d), lambda i, *_: (i, 0))
    share = (d // GROUP_WIDTH, groups, d // (2 * groups), GROUP_WIDTH)
    spec = pltpu.PrefetchScalarGridSpec(
        num_scalar_prefetch=1,
        grid=(n // ROWS,),
        in_specs=[row, row, row, row, tile_spec(gathered, rows, t), resident((1, d))],
        out_specs=[
            row,
            row,
            pl.BlockSpec(share, lambda *_: (0, 0, 0, 0)),
            pl.BlockSpec(share, lambda *_: (0, 0, 0, 0)),
            pl.BlockSpec((2, d), lambda *_: (0, 0)),
        ],
        scratch_shapes=[pltpu.VMEM((d, d), F32)],
    )
    return pl.pallas_call(
        mid_back_kernel,
        grid_spec=spec,
        out_shape=[
            jax.ShapeDtypeStruct((n, d), F32),
            jax.ShapeDtypeStruct((n, d), BF16),
            jax.ShapeDtypeStruct(share, BF16),
            jax.ShapeDtypeStruct(share, BF16),
            jax.ShapeDtypeStruct((2, d), F32),
        ],
        compiler_params=params(48),
        cost_estimate=cost(4 * n * d * d, 4 * d * d + 18 * n * d),
        name="out_proj_back",
    )(me, grad, mid, cot, o, gathered, gain)


def split_pairs(value, groups, my_index):
    rows = value.shape[0] // (2 * groups)
    pairs = value.reshape(groups, 2, rows, value.shape[1])
    even, odd = pairs[:, 0], pairs[:, 1]
    first = my_index == 0
    return jnp.where(first, even, odd), jnp.where(first, odd, even)


def ffn_kernel(aligned, me, h_ref, g_ref, wu_ref, wd_ref, mid_ref, mixed_ref, gh_ref, *refs):
    grads, acc = refs[:-1], refs[-1]
    j = pl.program_id(0)
    h, grad = h_ref[...], g_ref[...]
    wu, wd = flat(wu_ref), flat(wd_ref)
    up = dot_nn(h, wu)
    cdf = 0.5 * (1.0 + lax.erf(up * 0.7071067811865476))
    act = (up * cdf).astype(BF16)
    slope = cdf + up * (jnp.exp(-0.5 * up * up) * 0.3989422804014327)
    gu = (dot_nt(grad, wd) * slope).astype(BF16)
    dwd = dot_tn(act, grad).astype(BF16)
    dwu = dot_tn(h, gu).astype(BF16)
    if aligned:
        my_index = me[0]
        grads[0][...], grads[1][...] = split_pairs(dwu, grads[0].shape[0], my_index)
        for ref, value in zip(grads[2:], split_pairs(dwd, grads[2].shape[1], my_index), strict=True):
            for t in range(ref.shape[0]):
                ref[t] = value[:, t * ref.shape[2] : (t + 1) * ref.shape[2]]
    else:
        grads[0][...] = dwu
        grads[1][...] = dwd

    @pl.when(j == 0)
    def _():
        acc[...] = mid_ref[...] + dot_nn(act, wd)
        gh_ref[...] = dot_nt(gu, wu)

    @pl.when(j > 0)
    def _():
        acc[...] += dot_nn(act, wd)
        gh_ref[...] += dot_nt(gu, wu)

    @pl.when(j == pl.num_programs(0) - 1)
    def _():
        mixed_ref[...] = acc[...].astype(BF16)


def ffn_call(me, h, cot, wu, wd, mid, grad_specs, hidden, aligned):
    n, d = h.shape
    full = resident((n, d))
    const = pl.BlockSpec((n, d), lambda j, *_: (0, 0))
    spec = pltpu.PrefetchScalarGridSpec(
        num_scalar_prefetch=1,
        grid=(hidden // FF_COLS,),
        in_specs=[full, full, wu[1], wd[1], full],
        out_specs=[const, const] + [g[0] for g in grad_specs],
        scratch_shapes=[pltpu.VMEM((n, d), F32)],
    )
    return pl.pallas_call(
        partial(ffn_kernel, aligned),
        grid_spec=spec,
        out_shape=[jax.ShapeDtypeStruct((n, d), BF16), jax.ShapeDtypeStruct((n, d), F32)]
        + [g[1] for g in grad_specs],
        compiler_params=params(60),
        cost_estimate=cost(12 * n * d * hidden, 8 * d * hidden + 14 * n * d),
        name="ffn",
    )(me, h, cot, wu[0], wd[0], mid)


def qkv_grad_kernel(groups, me, h_ref, dq_ref, dkv_ref, rkv_ref, keep_ref, send_ref, sum_ref):
    h = h_ref[...]
    my_index = me[0]
    keep_ref[0], send_ref[0] = split_pairs(dot_tn(h, dq_ref[...]).astype(BF16), groups, my_index)
    for t in range(2):
        grad = (dkv_ref[t].astype(F32) + rkv_ref[t].astype(F32)).astype(BF16)
        sum_ref[t] = grad
        keep_ref[t + 1], send_ref[t + 1] = split_pairs(dot_tn(h, grad).astype(BF16), groups, my_index)


def qkv_grad_call(me, h, dq, dkv, rkv, groups):
    n, d = h.shape
    width = dq.shape[1]
    rows = d // (2 * groups)
    whole = pl.BlockSpec(memory_space=pltpu.VMEM)
    out = jax.ShapeDtypeStruct((3, groups, rows, width), BF16)
    return pl.pallas_call(
        partial(qkv_grad_kernel, groups),
        in_specs=[pl.BlockSpec(memory_space=pltpu.SMEM)] + [whole] * 4,
        out_specs=[whole] * 3,
        out_shape=[out, out, jax.ShapeDtypeStruct((2, n, width), BF16)],
        compiler_params=params(40),
        cost_estimate=cost(6 * n * d * width, 6 * d * width + 2 * n * d + 8 * n * width),
        name="qkv_grad",
    )(me, h, dq, dkv, rkv)


def head_back_kernel(count, *refs):
    dqs, dkvs = refs[:count], refs[count : 2 * count]
    x_ref, gr_ref, wq_ref, wk_ref, wv_ref, gain_ref, tg_ref, dln_ref = refs[2 * count :]
    i = pl.program_id(0)
    dq = jnp.concatenate([r[...] for r in dqs], axis=1)
    dk = jnp.concatenate([r[0] for r in dkvs], axis=1)
    dv = jnp.concatenate([r[1] for r in dkvs], axis=1)
    grad = dot_nt(dq, flat(wq_ref)) + dot_nt(dk, flat(wk_ref)) + dot_nt(dv, flat(wv_ref))
    hat, scale = normed(x_ref[...].astype(F32))
    tg_ref[...] = (gr_ref[...] + norm_back(grad, gain_ref[...], hat, scale)).astype(BF16)
    dgain = jnp.sum(grad * hat, axis=0, keepdims=True)
    dbias = jnp.sum(grad, axis=0, keepdims=True)

    @pl.when(i == 0)
    def _():
        dln_ref[0:1, :] = dgain
        dln_ref[1:2, :] = dbias

    @pl.when(i > 0)
    def _():
        dln_ref[0:1, :] += dgain
        dln_ref[1:2, :] += dbias


def head_back_call(dqs, dkvs, x, gr, gathered, rows, gain):
    n, d = x.shape
    row = pl.BlockSpec((ROWS, d), lambda i: (i, 0))
    width = dqs[0].shape[1]
    return pl.pallas_call(
        partial(head_back_kernel, len(dqs)),
        grid=(n // ROWS,),
        in_specs=[pl.BlockSpec((ROWS, width), lambda i: (i, 0))] * len(dqs)
        + [pl.BlockSpec((2, ROWS, width), lambda i: (0, i, 0))] * len(dkvs)
        + [
            row,
            row,
            tile_spec(gathered, rows, 0),
            tile_spec(gathered, rows, 1),
            tile_spec(gathered, rows, 2),
            resident((1, d)),
        ],
        out_specs=[row, pl.BlockSpec((2, d), lambda i: (0, 0))],
        out_shape=[jax.ShapeDtypeStruct((n, d), BF16), jax.ShapeDtypeStruct((2, d), F32)],
        compiler_params=params(48),
        cost_estimate=cost(6 * n * d * d, 6 * d * d + 14 * n * d),
        name="qkv_back",
    )(*dqs, *dkvs, x, gr, gathered, gathered, gathered, gain)


class Term:
    def __init__(self, array, axes, first=0, count=None):
        self.array, self.axes, self.first = array, axes, first
        self.count = array.shape[0] if count is None else count
        self.whole = first % self.count != 0

    def spec(self, settled, flipped, open_bits):
        def index_map(step, mine):
            at = [0 if self.whole else self.first // self.count]
            for b in self.axes:
                if b == flipped:
                    at.append(1 - mine[b])
                elif b in settled:
                    at.append(mine[b])
                else:
                    at.append((step >> (len(open_bits) - 1 - open_bits.index(b))) & 1)
            return (*at, 0, 0)

        lead = self.array.shape[0] if self.whole else self.count
        return pl.BlockSpec((lead,) + (None,) * len(self.axes) + self.array.shape[-2:], index_map)

    def read(self, ref):
        start = self.first if self.whole else 0
        return ref[start : start + self.count].astype(F32)


class Cube:
    def __init__(self, dp, index):
        self.bits = dp.bit_length() - 1
        self.dp = dp
        self.mine = ((index >> jnp.arange(self.bits, dtype=jnp.int32)) & 1).astype(jnp.int32)

    def swap(self, array, bit):
        return lax.ppermute(array, "dp", [(i, i ^ (1 << bit)) for i in range(self.dp)])

    def terms(self, arrays, first=0, count=None):
        made = []
        for array in arrays:
            lead, _, rows, width = array.shape
            shape = (lead,) + (2,) * self.bits + (rows, width)
            made.append(Term(array.reshape(shape), list(range(self.bits))[::-1], first, count))
        return made

    def add(self, outputs, dtype):
        in_specs, args, plan, out_specs, out_shape = [], [], [], [], []
        steps = 1
        for output in outputs:
            lead = 0
            for stream, settled, flipped in output:
                open_bits = [b for b in range(self.bits)[::-1] if b not in settled and b != flipped]
                steps = 2 ** len(open_bits)
                for term in stream:
                    in_specs.append(term.spec(settled, flipped, open_bits))
                    args.append(term.array)
                plan.append((len(out_specs), lead, list(stream)))
                lead += stream[0].count
            count = len(open_bits)

            def out_map(step, mine, count=count):
                return (0, *[(step >> (count - 1 - k)) & 1 for k in range(count)], 0, 0)

            shape = output[0][0][0].array.shape[-2:]
            out_specs.append(pl.BlockSpec((lead,) + (None,) * count + shape, out_map))
            out_shape.append(jax.ShapeDtypeStruct((lead,) + (2,) * count + shape, dtype))

        def kernel(mine, *refs):
            ins, outs = refs[: len(args)], refs[len(args) :]
            at = 0
            for out, first, stream in plan:
                total = stream[0].read(ins[at])
                for k in range(1, len(stream)):
                    total = total + stream[k].read(ins[at + k])
                outs[out][first : first + stream[0].count] = total.astype(dtype)
                at += len(stream)

        spec = pltpu.PrefetchScalarGridSpec(
            num_scalar_prefetch=1, grid=(steps,), in_specs=in_specs, out_specs=out_specs
        )
        size = sum(math.prod(o.shape) for o in out_shape)
        return pl.pallas_call(
            kernel,
            grid_spec=spec,
            out_shape=out_shape,
            compiler_params=params(40),
            cost_estimate=cost(4 * size, 8 * size),
            name="add_terms",
        )(self.mine, *args)


class Scatter:
    def __init__(self, cube, one, two):
        self.cube, self.sides, self.step = cube, (one, two), 0
        self.settled = []
        self.sent, self.last = [], []

    def advance(self):
        step = self.step
        done = (self.settled, self.settled)
        if step == 0:
            flips, groups = (0, 1), ((0,), (1,))
            done = ([], [])
        elif step == 1:
            flips, groups = (1, 0), ((0,), (1,))
            done = ([0], [1])
        else:
            flips, groups = (step, step), ((0, 1),)
            done = (list(range(step)),) * 2
        self.sent = self.cube.add(
            [[(stream, done[s], flips[s]) for s in group for stream in self.sides[s]] for group in groups], BF16
        )
        self.last = []
        for group, sent in zip(groups, self.sent, strict=True):
            got = self.cube.swap(sent, flips[group[0]])
            self.last.append(got)
            at = 0
            for s in group:
                axes = [b for b in range(self.cube.bits)[::-1] if b not in done[s] and b != flips[s]]
                for stream in self.sides[s]:
                    stream.append(Term(got, axes, at, stream[0].count))
                    at += stream[0].count
        self.step += 1
        return self

    def finish(self):
        while self.step < self.cube.bits:
            self.advance()
        done = list(range(self.cube.bits))
        outs = self.cube.add([[(stream, done, None)] for side in self.sides for stream in side], F32)
        return outs


def gate(value, *others):
    return lax.optimization_barrier((value, others))[0]


def block_table(seg_full, seg_local, my_index, n, bq, bk):
    first, last = seg_local[::bq], seg_local[bq - 1 :: bq]
    low = jnp.sum((seg_full[None, :] < first[:, None]).astype(jnp.int32), axis=1)
    high = jnp.sum((seg_full[None, :] <= last[:, None]).astype(jnp.int32), axis=1)
    columns = []
    for index in (my_index, 1 - my_index):
        start = jnp.clip(low - index * n, 0, n)
        stop = jnp.clip(high - index * n, 0, n)
        block = start // bk
        columns += [block, jnp.where(stop > start, (stop + bk - 1) // bk - block, 0)]
    return jnp.stack(columns, axis=1).reshape(-1).astype(jnp.int32)


def body(
    tokens,
    segments,
    ln1_gain,
    ln1_bias,
    w_query,
    w_key,
    w_value,
    w_out,
    ln2_gain,
    ln2_bias,
    w_up,
    w_down,
    cotangent,
):
    x = tokens[0]
    n, d = x.shape
    cot = cotangent[0]
    rows = w_query.shape[0]
    devices = d // rows
    hidden = w_up.shape[1]
    per_device = hidden // devices
    my_index = lax.axis_index("seq")
    seg_full = segments[0]
    seg_local = lax.dynamic_slice_in_dim(seg_full, my_index * n, n)
    seg_other = lax.dynamic_slice_in_dim(seg_full, (1 - my_index) * n, n)
    tab = block_table(seg_full, seg_local, my_index, n, ATT_Q, ATT_K)
    seg_q = seg_local.reshape(n // ATT_Q, 1, ATT_Q)
    seg_own_col, seg_other_col = seg_local[:, None], seg_other[:, None]

    vectors = jnp.concatenate([ln1_gain, ln1_bias, ln2_gain, ln2_bias]).reshape(1, 4 * rows)
    ln_block = jnp.pad(vectors, ((0, LN_ROWS - 1), (0, d - 4 * rows)))
    first_local = jnp.concatenate([w_query, w_key, w_value, ln_block], axis=0)
    tiles = hidden // d
    up_local = w_up.reshape(rows, tiles, d).transpose(1, 0, 2).reshape(tiles * rows, d)
    second_local = jnp.concatenate([up_local, w_down, w_out], axis=0)

    def gather(local):
        out = lax.all_gather(local, BOTH, axis=0, tiled=True)
        return out.reshape(devices, local.shape[0], d)

    first = gather(first_local)
    second = gather(second_local)

    aligned = rows % 16 == 0
    if aligned:
        qkv_w, qkv_rows = first, rows
        out_w, out_t, out_rows = second, second.shape[1] // rows - 1, rows
    else:
        qkv_w = first[:, : 3 * rows].reshape(devices, 3, rows, d).transpose(1, 0, 2, 3).reshape(1, 3 * d, d)
        qkv_rows = d
        out_w, out_t, out_rows = second[:, -rows:].reshape(1, d, d), 0, d
    ln = first[:, 3 * rows, : 4 * rows].reshape(devices, 4, rows).transpose(1, 0, 2).reshape(4, 1, d).astype(F32)

    h1, own = kv_call(x, ln[0], ln[1], qkv_w, qkv_rows)
    swap = [(0, 1), (1, 0)]
    other = lax.ppermute(own, "seq", swap)
    q = q_call(h1, qkv_w, qkv_rows)
    attended, lse = attend_call(tab, q, own, other, seg_q, seg_own_col, seg_other_col, ATT_Q, ATT_K)
    mid, h2 = mid_call(x, attended, out_w, out_rows, out_t, ln[2], ln[3])

    dp = devices // 2
    cube = Cube(dp, lax.axis_index("dp"))
    me = my_index.reshape(1).astype(jnp.int32)

    def exchange(value):
        return lax.ppermute(value, "seq", swap)

    def halves(value, axis):
        keep = lax.dynamic_index_in_dim(value, my_index, axis, keepdims=False)
        send = lax.dynamic_index_in_dim(value, 1 - my_index, axis, keepdims=False)
        return keep, send

    up_rows = tiles * rows
    group = FF_COLS // per_device
    if aligned:
        per_tile = d // FF_COLS
        wu = (second, pl.BlockSpec((devices, rows, FF_COLS), lambda j, *_: (0, j // per_tile, j % per_tile)))
        wd = (second, pl.BlockSpec((group, per_device, d), lambda j, *_: (j, up_rows // per_device, 0)))
        up_out = (
            pl.BlockSpec((None, dp, rows, FF_COLS), lambda j, *_: (j // per_tile, 0, 0, j % per_tile)),
            jax.ShapeDtypeStruct((tiles, dp, rows, d), BF16),
        )
        down_out = (
            pl.BlockSpec((tiles, group // 2, rows, d), lambda j, *_: (0, j, 0, 0)),
            jax.ShapeDtypeStruct((tiles, dp, rows, d), BF16),
        )
        grad_specs = [up_out, up_out, down_out, down_out]
    else:
        up_w = second[:, :up_rows].reshape(devices, tiles, rows, d).transpose(0, 2, 1, 3).reshape(d, hidden)
        down_w = second[:, up_rows : up_rows + per_device].reshape(hidden, d)
        up_block = pl.BlockSpec((d, FF_COLS), lambda j, *_: (0, j))
        down_block = pl.BlockSpec((FF_COLS, d), lambda j, *_: (j, 0))
        wu, wd = (up_w, up_block), (down_w, down_block)
        grad_specs = [
            (up_block, jax.ShapeDtypeStruct((d, hidden), BF16)),
            (down_block, jax.ShapeDtypeStruct((hidden, d), BF16)),
        ]
    mixed, gmid, *grads = ffn_call(me, h2, cot, wu, wd, mid, grad_specs, hidden, aligned)
    if not aligned:
        dwu = grads[0].reshape(dp, 2, rows, tiles, d).transpose(3, 0, 1, 2, 4)
        dwd = grads[1].reshape(dp, 2, tiles, rows, d).transpose(2, 0, 1, 3, 4)
        grads = [*halves(dwu, 2), *halves(dwd, 2)]
    keep_up, send_up, keep_down, send_down = grads
    got_up, got_down = exchange(send_up), exchange(send_down)
    big = Scatter(cube, [cube.terms([keep_up, got_up])], [cube.terms([keep_down, got_down])])
    big.advance()
    grad_mid, grad_att, keep_out, send_out, dln2 = mid_back_call(
        me, gate(gmid, big.sent), mid, cot, attended, out_w, out_rows, out_t, ln[2], dp
    )
    got_out = exchange(send_out)
    dqs, dkvs, qkv_terms, raw = [], [], [], []

    def finish_group(g, *waited):
        dq, dkv, got = raw[g]
        keep, send, dkv = qkv_grad_call(me, h1, gate(dq, *waited), dkv, got, dp)
        dqs.append(dq)
        dkvs.append(dkv)
        qkv_terms.append([keep, exchange(send)])
        return dkv

    def attend_group(g, *waited):
        if raw:
            waited += (raw[-1][0],)
        dq, dkv, sent = attend_back_call(
            gate(tab, *waited), q, grad_att, attended, own, other, seg_q, seg_own_col, seg_other_col, lse,
            ATT_Q, ATT_K, g,
        )
        raw.append((dq, dkv, exchange(sent)))

    attend_group(0)
    attend_group(1)
    first_done = big.last
    big.advance()
    finish_group(0, first_done, big.sent)
    done = finish_group(1)
    tail_one = Scatter(
        cube,
        [cube.terms(qkv_terms[0]), cube.terms([keep_out, got_out], 0, 2)],
        [cube.terms(qkv_terms[1]), cube.terms([keep_out, got_out], 2, 2)],
    )
    tail_one.advance()
    attend_group(2, tail_one.sent, done)
    waited = [big.last, tail_one.last]
    big.advance()
    tail_one.advance()
    attend_group(3, *waited, big.sent, tail_one.sent)
    waited = [big.last, tail_one.last]
    big.advance()
    tail_one.advance()
    finish_group(2, big.sent)
    finish_group(3, dkvs[-1], tail_one.sent)
    tail_two = Scatter(cube, [cube.terms(qkv_terms[2])], [cube.terms(qkv_terms[3])])
    tail_two.advance()
    waited = [big.last, tail_one.last]
    tail_one.advance()
    waited += [tail_one.sent, tail_two.sent]
    token_grad, dln1 = head_back_call(dqs, dkvs, x, gate(grad_mid, *waited), qkv_w, qkv_rows, ln[0])

    dln = jnp.concatenate([dln1, dln2], axis=0).reshape(4, devices, rows).transpose(1, 0, 2)
    dln = lax.all_to_all(dln.reshape(devices, 4 * rows), BOTH, 0, 0, tiled=True)
    dln = jnp.sum(dln.reshape(devices, 4, rows), axis=0)

    up_share, down_share = big.finish()
    one_a, out_a, one_b, out_b = tail_one.finish()
    two_a, two_b = tail_two.finish()
    up_share = up_share.transpose(1, 0, 2).reshape(rows, hidden)
    down_share = down_share.reshape(per_device, d)
    qkv_share = jnp.concatenate([one_a, one_b, two_a, two_b], axis=-1)
    out_share = jnp.concatenate([out_a, out_b], axis=0).transpose(1, 0, 2).reshape(rows, d)
    return (
        mixed[None],
        token_grad[None],
        dln[0],
        dln[1],
        qkv_share[0],
        qkv_share[1],
        qkv_share[2],
        out_share,
        dln[2],
        dln[3],
        up_share,
        down_share,
    )


def solution(mesh):
    row, act, vec = P(BOTH, None), P("dp", "seq", None), P(BOTH)
    in_specs = (act, P("dp", None), vec, vec, row, row, row, row, vec, vec, row, row, act)
    out_specs = (act, act, vec, vec, row, row, row, row, vec, vec, row, row)
    return jax.shard_map(body, mesh=mesh, in_specs=in_specs, out_specs=out_specs, check_vma=False)
```

```python
import math
from functools import partial

import jax
import jax.numpy as jnp
from jax import lax
from jax.experimental import pallas as pl
from jax.experimental.pallas import tpu as pltpu
from jax.sharding import PartitionSpec as P

BF16 = jnp.bfloat16
F32 = jnp.float32
HEAD_DIM = 64
GROUP = 4
GROUP_WIDTH = GROUP * HEAD_DIM
NEG = -1000000000.0
BOTH = ("dp", "seq")
ATT_Q = 256
ATT_K = 512
ROWS = 256
FF_COLS = 512
COST_SCALE = 100000
STEP_BITS = 1


def dot_nn(left, right):
    return lax.dot_general(left, right, (((1,), (0,)), ((), ())), preferred_element_type=F32)


def dot_nt(left, right):
    return lax.dot_general(left, right, (((1,), (1,)), ((), ())), preferred_element_type=F32)


def dot_tn(left, right):
    return lax.dot_general(left, right, (((0,), (0,)), ((), ())), preferred_element_type=F32)


def params(mib):
    return pltpu.CompilerParams(vmem_limit_bytes=mib << 20)


def cost(flops, nbytes, scale=None):
    if scale:
        return pl.CostEstimate(flops=scale * flops, bytes_accessed=scale * nbytes, transcendentals=0)
    return pl.CostEstimate(flops=flops // COST_SCALE, bytes_accessed=nbytes // COST_SCALE, transcendentals=0)


def normed(values):
    centre = values - jnp.mean(values, axis=-1, keepdims=True)
    scale = lax.rsqrt(jnp.mean(centre * centre, axis=-1, keepdims=True) + 1e-05)
    return centre * scale, scale


def norm_back(grad, gain_vec, hat, scale):
    inner = grad * gain_vec
    return scale * (
        inner
        - jnp.mean(inner, axis=-1, keepdims=True)
        - hat * jnp.mean(inner * hat, axis=-1, keepdims=True)
    )


def flat(ref):
    value = ref[...]
    return value.reshape(-1, value.shape[-1])


def resident(shape):
    zeros = (0,) * len(shape)
    return pl.BlockSpec(shape, lambda *_: zeros, pipeline_mode=pl.Buffered(1))


class Spread:
    def __init__(self, block, pieces):
        self.block, self.pieces = block, pieces
        self.args = [b for rounds, *_ in pieces for b in rounds.buffers]

    def start(self, refs, place, target, sem, columns=None):
        for i, (rounds, first, count, at) in enumerate(self.pieces):
            for ref, (flips, core) in zip(refs[4 * i : 4 * i + 4], rounds.parts, strict=True):
                for e, flip in enumerate(flips):
                    device = (place[0] ^ flip) * 2 + (place[1] ^ core)
                    row = pl.multiple_of(device * self.block + at, count)
                    source = ref.at[e, pl.ds(first, count)]
                    if columns is not None:
                        source = ref.at[e, pl.ds(first, count), columns]
                    pltpu.make_async_copy(source, target.at[pl.ds(row, count), :], sem).start()

    def start_rows(self, refs, place, target, sem, first, group):
        ((rounds, begin, count, _),) = self.pieces
        for k in range(group):
            device = first + k
            flip = (device // 2) ^ place[0]
            at, last = rounds.index(flip)
            core = (device % 2) ^ place[1]
            for i, ref in enumerate(refs):

                @pl.when((last == i % 2) & (core == i // 2))
                def _(ref=ref, at=at, k=k):
                    pltpu.make_async_copy(
                        ref.at[at, pl.ds(begin, count)], target.at[pl.ds(k * count, count), :], sem
                    ).start()


class Plain:
    def __init__(self, array, block):
        self.args, self.block = [array], block

    def start(self, refs, place, target, sem, columns=None):
        source = refs[0] if columns is None else refs[0].at[:, columns]
        pltpu.make_async_copy(source, target, sem).start()

    def start_rows(self, refs, place, target, sem, first, group):
        pltpu.make_async_copy(refs[0].at[pl.ds(first * self.block, group * self.block), :], target, sem).start()


def arrived(target, sem):
    pltpu.make_async_copy(target, target, sem).wait()


def cut(refs, weights):
    parts = []
    for weight in weights:
        parts.append(refs[: len(weight.args)])
        refs = refs[len(weight.args) :]
    return parts, refs


def load_all(weights, parts, place, targets, sem):
    @pl.when(pl.program_id(0) == 0)
    def _():
        for i, weight in enumerate(weights):
            weight.start(parts[i], place, targets[i], sem.at[i])
        for i in range(len(weights)):
            arrived(targets[i], sem.at[i])


HBM = pl.BlockSpec(memory_space=pl.ANY)


def weight_args(weights):
    args = [a for w in weights for a in w.args]
    return [HBM] * len(args), args


def kv_kernel(weights, place, x_ref, gain_ref, bias_ref, *refs):
    parts, refs = cut(refs, weights)
    h_ref, kv_ref, wk, wv, sem = refs
    load_all(weights, parts, place, (wk, wv), sem)
    hat, _ = normed(x_ref[...].astype(F32))
    low = (hat * gain_ref[...] + bias_ref[...]).astype(BF16)
    h_ref[...] = low
    kv_ref[0] = dot_nn(low, wk[...]).astype(BF16)
    kv_ref[1] = dot_nn(low, wv[...]).astype(BF16)


def kv_call(place, x, gain, bias, weights):
    n, d = x.shape
    row = pl.BlockSpec((ROWS, d), lambda i, *_: (i, 0))
    specs, args = weight_args(weights)
    spec = pltpu.PrefetchScalarGridSpec(
        num_scalar_prefetch=1,
        grid=(n // ROWS,),
        in_specs=[row, resident((1, d)), resident((1, d))] + specs,
        out_specs=[row, pl.BlockSpec((2, ROWS, d), lambda i, *_: (0, i, 0))],
        scratch_shapes=[pltpu.VMEM((d, d), BF16)] * 2 + [pltpu.SemaphoreType.DMA((2,))],
    )
    return pl.pallas_call(
        partial(kv_kernel, weights),
        grid_spec=spec,
        out_shape=[jax.ShapeDtypeStruct((n, d), BF16), jax.ShapeDtypeStruct((2, n, d), BF16)],
        compiler_params=params(40),
        cost_estimate=cost(4 * n * d * d, 4 * d * d + 8 * n * d),
        name="kv_proj",
    )(place, x, gain, bias, *args)


def q_kernel(weights, place, h_ref, *refs):
    parts, refs = cut(refs, weights)
    q_ref, wq, sem = refs
    load_all(weights, parts, place, (wq,), sem)
    q_ref[...] = (dot_nn(h_ref[...], wq[...]).astype(BF16).astype(F32) * 0.125).astype(BF16)


def q_call(place, h, weights):
    n, d = h.shape
    row = pl.BlockSpec((ROWS, d), lambda i, *_: (i, 0))
    specs, args = weight_args(weights)
    spec = pltpu.PrefetchScalarGridSpec(
        num_scalar_prefetch=1,
        grid=(n // ROWS,),
        in_specs=[row] + specs,
        out_specs=row,
        scratch_shapes=[pltpu.VMEM((d, d), BF16), pltpu.SemaphoreType.DMA((1,))],
    )
    return pl.pallas_call(
        partial(q_kernel, weights),
        grid_spec=spec,
        out_shape=jax.ShapeDtypeStruct((n, d), BF16),
        compiler_params=params(32),
        cost_estimate=cost(2 * n * d * d, 2 * d * d + 4 * n * d),
        name="q_proj",
    )(place, h, *args)


def stack_heads(block):
    lane = lax.broadcasted_iota(jnp.int32, block.shape, 1) // HEAD_DIM
    zero = jnp.zeros_like(block)
    return jnp.concatenate([jnp.where(lane == h, block, zero) for h in range(GROUP)], axis=0)


def head_cols(value, h, width):
    return value[:, h * width : (h + 1) * width]


def head_rows(value, h):
    return value[h * HEAD_DIM : (h + 1) * HEAD_DIM, :]


def attend_kernel(bq, bk, tab, q_ref, ko_ref, vo_ref, kp_ref, vp_ref, sq_ref, so_ref, sp_ref, o_ref, lse_ref):
    i = pl.program_id(1)
    stacked = stack_heads(q_ref[...])
    seg_q = jnp.concatenate([sq_ref[0]] * GROUP, axis=1)

    def over(k_ref, v_ref, s_ref, first, count, state):
        def step(j, carry):
            top, total, acc = carry
            at = pl.multiple_of((first + j) * bk, bk)
            scores = dot_nt(k_ref[0, pl.ds(at, bk), :], stacked)
            scores = jnp.where(s_ref[pl.ds(at, bk), :] == seg_q, scores, NEG)
            new_top = jnp.maximum(top, jnp.max(scores, axis=0, keepdims=True))
            decay = jnp.exp(top - new_top)
            probs = jnp.exp(scores - new_top)
            total = total * decay + jnp.sum(probs, axis=0, keepdims=True)
            low = probs.astype(BF16)
            values = v_ref[0, pl.ds(at, bk), :].T
            acc = tuple(
                acc[h] * head_cols(decay, h, bq) + dot_nn(head_rows(values, h), head_cols(low, h, bq))
                for h in range(GROUP)
            )
            return new_top, total, acc

        return lax.fori_loop(0, count, step, state)

    state = (
        jnp.full((1, GROUP * bq), -jnp.inf, F32),
        jnp.zeros((1, GROUP * bq), F32),
        tuple(jnp.zeros((HEAD_DIM, bq), F32) for _ in range(GROUP)),
    )
    state = over(ko_ref, vo_ref, so_ref, tab[4 * i], tab[4 * i + 1], state)
    top, total, acc = over(kp_ref, vp_ref, sp_ref, tab[4 * i + 2], tab[4 * i + 3], state)
    out = jnp.concatenate([acc[h] / head_cols(total, h, bq) for h in range(GROUP)], axis=0)
    o_ref[...] = out.T.astype(BF16)
    lse_ref[0, 0] = top + jnp.log(total)


def attend_call(tab, q, own, other, seg_q, seg_own, seg_other, bq, bk, first, groups):
    n, d = q.shape
    blocks = n // bq
    query = pl.BlockSpec((bq, GROUP_WIDTH), lambda g, i, *_: (i, g + first))

    def half(which):
        return pl.BlockSpec((1, n, GROUP_WIDTH), lambda g, i, *_: (which, 0, g + first))

    column = pl.BlockSpec((n, 1), lambda g, i, *_: (0, 0))
    spec = pltpu.PrefetchScalarGridSpec(
        num_scalar_prefetch=1,
        grid=(groups, blocks),
        in_specs=[
            query,
            half(0),
            half(1),
            half(0),
            half(1),
            pl.BlockSpec((1, 1, bq), lambda g, i, *_: (i, 0, 0)),
            column,
            column,
        ],
        out_specs=[
            pl.BlockSpec((bq, GROUP_WIDTH), lambda g, i, *_: (i, g)),
            pl.BlockSpec((1, 1, 1, GROUP * bq), lambda g, i, *_: (g, i, 0, 0)),
        ],
    )
    return pl.pallas_call(
        partial(attend_kernel, bq, bk),
        grid_spec=spec,
        out_shape=[
            jax.ShapeDtypeStruct((n, groups * GROUP_WIDTH), BF16),
            jax.ShapeDtypeStruct((groups, blocks, 1, GROUP * bq), F32),
        ],
        compiler_params=params(56),
        cost_estimate=cost(8_000_000_000 * groups, 3 * groups * n * d),
        name="attend",
    )(tab, q, own, own, other, other, seg_q, seg_own, seg_other)


def attend_back_kernel(
    bq, bk, tab, q_ref, go_ref, o_ref, ko_ref, vo_ref, kp_ref, vp_ref, sq_ref, so_ref, sp_ref, lse_ref,
    dq_ref, down_ref, dpart_ref, dko, dvo, dkp, dvp,
):
    i = pl.program_id(1)

    @pl.when(i == 0)
    def _():
        for ref in (dko, dvo, dkp, dvp):
            ref[...] = jnp.zeros_like(ref)

    stacked = stack_heads(q_ref[...])
    grad = go_ref[...]
    stacked_grad = stack_heads(grad)
    product = (grad.astype(F32) * o_ref[...].astype(F32)).T
    inner = jnp.concatenate(
        [jnp.sum(head_rows(product, h), axis=0, keepdims=True) for h in range(GROUP)], axis=1
    )
    seg_q = jnp.concatenate([sq_ref[0]] * GROUP, axis=1)
    lse = lse_ref[0, 0]

    def over(k_ref, v_ref, s_ref, dk, dv, first, count, state):
        def step(j, acc):
            at = pl.multiple_of((first + j) * bk, bk)
            keys = k_ref[0, pl.ds(at, bk), :]
            scores = dot_nt(keys, stacked)
            scores = jnp.where(s_ref[pl.ds(at, bk), :] == seg_q, scores, NEG)
            probs = jnp.exp(scores - lse)
            grad_probs = dot_nt(v_ref[0, pl.ds(at, bk), :], stacked_grad)
            grad_scores = (probs * (grad_probs - inner)).astype(BF16)
            dv[pl.ds(at, bk), :] += dot_nn(probs.astype(BF16), stacked_grad)
            dk[pl.ds(at, bk), :] += dot_nn(grad_scores, stacked)
            keys_t = keys.T
            return tuple(
                acc[h] + dot_nn(head_rows(keys_t, h), head_cols(grad_scores, h, bq)) for h in range(GROUP)
            )

        return lax.fori_loop(0, count, step, state)

    state = tuple(jnp.zeros((HEAD_DIM, bq), F32) for _ in range(GROUP))
    state = over(ko_ref, vo_ref, so_ref, dko, dvo, tab[4 * i], tab[4 * i + 1], state)
    state = over(kp_ref, vp_ref, sp_ref, dkp, dvp, tab[4 * i + 2], tab[4 * i + 3], state)
    dq_ref[...] = (jnp.concatenate(state, axis=0).T * 0.125).astype(BF16)

    @pl.when(i == pl.num_programs(1) - 1)
    def _():
        down_ref[0] = dko[...].astype(BF16)
        down_ref[1] = dvo[...].astype(BF16)
        dpart_ref[0] = dkp[...].astype(BF16)
        dpart_ref[1] = dvp[...].astype(BF16)


def attend_back_call(tab, q, grad, out, own, other, seg_q, seg_own, seg_other, lse, bq, bk, first, groups, out_first):
    n, d = q.shape
    blocks = n // bq
    query = pl.BlockSpec((bq, GROUP_WIDTH), lambda g, i, *_: (i, g + first))

    def half(which):
        return pl.BlockSpec((1, n, GROUP_WIDTH), lambda g, i, *_: (which, 0, g + first))

    column = pl.BlockSpec((n, 1), lambda *_: (0, 0))
    pair = pl.BlockSpec((2, n, GROUP_WIDTH), lambda g, i, *_: (0, 0, g))
    spec = pltpu.PrefetchScalarGridSpec(
        num_scalar_prefetch=1,
        grid=(groups, blocks),
        in_specs=[
            query,
            query,
            pl.BlockSpec((bq, GROUP_WIDTH), lambda g, i, *_: (i, g + out_first)),
            half(0),
            half(1),
            half(0),
            half(1),
            pl.BlockSpec((1, 1, bq), lambda g, i, *_: (i, 0, 0)),
            column,
            column,
            pl.BlockSpec((1, 1, 1, GROUP * bq), lambda g, i, *_: (g + out_first, i, 0, 0)),
        ],
        out_specs=[pl.BlockSpec((bq, GROUP_WIDTH), lambda g, i, *_: (i, g)), pair, pair],
        scratch_shapes=[pltpu.VMEM((n, GROUP_WIDTH), F32)] * 4,
    )
    width = groups * GROUP_WIDTH
    return pl.pallas_call(
        partial(attend_back_kernel, bq, bk),
        grid_spec=spec,
        out_shape=[
            jax.ShapeDtypeStruct((n, width), BF16),
            jax.ShapeDtypeStruct((2, n, width), BF16),
            jax.ShapeDtypeStruct((2, n, width), BF16),
        ],
        compiler_params=params(56),
        cost_estimate=cost(12_000_000_000 * groups, 6 * groups * n * d),
        name="attend_back",
    )(tab, q, grad, out, own, own, other, other, seg_q, seg_own, seg_other, lse)


def mid_kernel(weights, count, place, x_ref, gain_ref, bias_ref, *refs):
    outs, refs = refs[:count], refs[count:]
    parts, refs = cut(refs, weights)
    r_ref, h_ref, wo, sem = refs
    load_all(weights, parts, place, (wo,), sem)
    mid = x_ref[...].astype(F32) + dot_nn(jnp.concatenate([o[...] for o in outs], axis=1), wo[...])
    r_ref[...] = mid
    hat, _ = normed(mid)
    h_ref[...] = (hat * gain_ref[...] + bias_ref[...]).astype(BF16)


def mid_call(place, x, outs, weights, gain, bias):
    n, d = x.shape
    row = pl.BlockSpec((ROWS, d), lambda i, *_: (i, 0))
    specs, args = weight_args(weights)
    spec = pltpu.PrefetchScalarGridSpec(
        num_scalar_prefetch=1,
        grid=(n // ROWS,),
        in_specs=[row, resident((1, d)), resident((1, d))]
        + [pl.BlockSpec((ROWS, o.shape[1]), lambda i, *_: (i, 0)) for o in outs]
        + specs,
        out_specs=[row, row],
        scratch_shapes=[pltpu.VMEM((d, d), BF16), pltpu.SemaphoreType.DMA((1,))],
    )
    return pl.pallas_call(
        partial(mid_kernel, weights, len(outs)),
        grid_spec=spec,
        out_shape=[jax.ShapeDtypeStruct((n, d), F32), jax.ShapeDtypeStruct((n, d), BF16)],
        compiler_params=params(32),
        cost_estimate=cost(2 * n * d * d, 2 * d * d + 10 * n * d),
        name="out_proj",
    )(place, x, gain, bias, *outs, *args)


def mid_back_kernel(weights, count, place, gh_ref, r_ref, g_ref, gain_ref, *refs):
    outs, refs = refs[:count], refs[count:]
    parts, refs = cut(refs, weights)
    gr_ref, go_ref, keep_ref, send_ref, dln_ref, acc, wo, sem = refs
    load_all(weights, parts, place, (wo,), sem)
    i = pl.program_id(0)
    hat, scale = normed(r_ref[...])
    grad = gh_ref[...]
    total = g_ref[...].astype(F32) + norm_back(grad, gain_ref[...], hat, scale)
    gr_ref[...] = total
    low = total.astype(BF16)
    go_ref[...] = dot_nt(low, wo[...]).astype(BF16)
    part = dot_tn(jnp.concatenate([o[...] for o in outs], axis=1), low)
    dgain = jnp.sum(grad * hat, axis=0, keepdims=True)
    dbias = jnp.sum(grad, axis=0, keepdims=True)

    @pl.when(i == 0)
    def _():
        acc[...] = part
        dln_ref[0:1, :] = dgain
        dln_ref[1:2, :] = dbias

    @pl.when(i > 0)
    def _():
        acc[...] += part
        dln_ref[0:1, :] += dgain
        dln_ref[1:2, :] += dbias

    @pl.when(i == pl.num_programs(0) - 1)
    def _():
        lanes = keep_ref.shape[3]
        for ref, value in zip(
            (keep_ref, send_ref), split_pairs(acc[...].astype(BF16), keep_ref.shape[1], place[1]), strict=True
        ):
            for t in range(ref.shape[0]):
                ref[t] = value[:, :, t * lanes : (t + 1) * lanes]


def mid_back_call(place, grad, mid, cot, outs, weights, gain, groups):
    n, d = mid.shape
    row = pl.BlockSpec((ROWS, d), lambda i, *_: (i, 0))
    share = (d // GROUP_WIDTH, groups, d // (2 * groups), GROUP_WIDTH)
    specs, args = weight_args(weights)
    spec = pltpu.PrefetchScalarGridSpec(
        num_scalar_prefetch=1,
        grid=(n // ROWS,),
        in_specs=[row, row, row, resident((1, d))]
        + [pl.BlockSpec((ROWS, o.shape[1]), lambda i, *_: (i, 0)) for o in outs]
        + specs,
        out_specs=[
            row,
            row,
            pl.BlockSpec(share, lambda *_: (0, 0, 0, 0)),
            pl.BlockSpec(share, lambda *_: (0, 0, 0, 0)),
            pl.BlockSpec((2, d), lambda *_: (0, 0)),
        ],
        scratch_shapes=[
            pltpu.VMEM((d, d), F32),
            pltpu.VMEM((d, d), BF16),
            pltpu.SemaphoreType.DMA((1,)),
        ],
    )
    return pl.pallas_call(
        partial(mid_back_kernel, weights, len(outs)),
        grid_spec=spec,
        out_shape=[
            jax.ShapeDtypeStruct((n, d), F32),
            jax.ShapeDtypeStruct((n, d), BF16),
            jax.ShapeDtypeStruct(share, BF16),
            jax.ShapeDtypeStruct(share, BF16),
            jax.ShapeDtypeStruct((2, d), F32),
        ],
        compiler_params=params(48),
        cost_estimate=cost(4 * n * d * d, 4 * d * d + 18 * n * d),
        name="out_proj_back",
    )(place, grad, mid, cot, gain, *outs, *args)


def split_pairs(value, groups, my_index):
    rows = value.shape[0] // (2 * groups)
    pairs = value.reshape(groups, 2, rows, value.shape[1])
    even, odd = pairs[:, 0], pairs[:, 1]
    first = my_index == 0
    return jnp.where(first, even, odd), jnp.where(first, odd, even)


def ffn_grads(h, grad, wu, wd):
    up = dot_nn(h, wu)
    cdf = 0.5 * (1.0 + lax.erf(up * 0.7071067811865476))
    act = (up * cdf).astype(BF16)
    slope = cdf + up * (jnp.exp(-0.5 * up * up) * 0.3989422804014327)
    gu = (dot_nt(grad, wd) * slope).astype(BF16)
    return act, gu, dot_tn(h, gu).astype(BF16), dot_tn(act, grad).astype(BF16)


def ffn_sums(j, act, gu, wu, wd, mid_ref, mixed_ref, gh_ref, acc):
    @pl.when(j == 0)
    def _():
        acc[...] = mid_ref[...] + dot_nn(act, wd)
        gh_ref[...] = dot_nt(gu, wu)

    @pl.when(j > 0)
    def _():
        acc[...] += dot_nn(act, wd)
        gh_ref[...] += dot_nt(gu, wu)

    @pl.when(j == pl.num_programs(0) - 1)
    def _():
        mixed_ref[...] = acc[...].astype(BF16)


def ffn_kernel(ups, downs, aligned, place, h_ref, g_ref, mid_ref, *refs):
    parts, refs = cut(refs, ups + downs)
    mixed_ref, gh_ref = refs[:2]
    grads = refs[2:6] if aligned else refs[2:4]
    wu_s, wd_s, acc, sem = refs[-4:]
    j, steps = pl.program_id(0), pl.num_programs(0)
    per_tile = h_ref.shape[1] // FF_COLS
    group = FF_COLS // sum(w.block for w in downs)

    def fetch(step, slot):
        column = pl.ds(pl.multiple_of((step % per_tile) * FF_COLS, FF_COLS), FF_COLS)
        for t, up in enumerate(ups):

            @pl.when(step // per_tile == t)
            def _(t=t, up=up):
                up.start(parts[t], place, wu_s.at[slot], sem.at[slot, 0], column)

        at = 0
        for i, down in enumerate(downs):
            count = group * down.block
            down.start_rows(
                parts[len(ups) + i], place, wd_s.at[slot, pl.ds(at, count), :], sem.at[slot, 1], step * group, group
            )
            at += count

    @pl.when(j == 0)
    def _():
        fetch(j, 0)

    @pl.when(j + 1 < steps)
    def _():
        fetch(j + 1, (j + 1) % 2)

    slot = j % 2
    arrived(wu_s.at[slot], sem.at[slot, 0])
    arrived(wd_s.at[slot], sem.at[slot, 1])
    wu, wd = wu_s[slot], wd_s[slot]
    if len(downs) > 1:
        width = wd.shape[1]
        stack, at = [], 0
        for down in downs:
            count = group * down.block
            stack.append(wd[at : at + count].reshape(group, down.block, width))
            at += count
        wd = jnp.concatenate(stack, axis=1).reshape(FF_COLS, width)
    act, gu, dwu, dwd = ffn_grads(h_ref[...], g_ref[...], wu, wd)
    if aligned:
        grads[0][...], grads[1][...] = split_pairs(dwu, grads[0].shape[0], place[1])
        for ref, value in zip(grads[2:], split_pairs(dwd, grads[2].shape[1], place[1]), strict=True):
            for t in range(ref.shape[0]):
                ref[t] = value[:, t * ref.shape[2] : (t + 1) * ref.shape[2]]
    else:
        grads[0][...] = dwu
        grads[1][...] = dwd
    ffn_sums(j, act, gu, wu, wd, mid_ref, mixed_ref, gh_ref, acc)


def ffn_call(place, h, cot, ups, downs, mid, grad_specs, hidden, aligned):
    n, d = h.shape
    full = resident((n, d))
    const = pl.BlockSpec((n, d), lambda j, *_: (0, 0))
    specs, args = weight_args(ups + downs)
    spec = pltpu.PrefetchScalarGridSpec(
        num_scalar_prefetch=1,
        grid=(hidden // FF_COLS,),
        in_specs=[full, full, full] + specs,
        out_specs=[const, const] + [g[0] for g in grad_specs],
        scratch_shapes=[
            pltpu.VMEM((2, d, FF_COLS), BF16),
            pltpu.VMEM((2, FF_COLS, d), BF16),
            pltpu.VMEM((n, d), F32),
            pltpu.SemaphoreType.DMA((2, 2)),
        ],
    )
    return pl.pallas_call(
        partial(ffn_kernel, ups, downs, aligned),
        grid_spec=spec,
        out_shape=[jax.ShapeDtypeStruct((n, d), BF16), jax.ShapeDtypeStruct((n, d), F32)]
        + [g[1] for g in grad_specs],
        compiler_params=params(60),
        cost_estimate=cost(12 * n * d * hidden, 8 * d * hidden + 14 * n * d),
        name="ffn",
    )(place, h, cot, mid, *args)


def qkv_grad_kernel(groups, place, h_ref, dq_ref, dkv_ref, rkv_ref, keep_ref, send_ref, sum_ref):
    h = h_ref[...]
    my_index = place[1]
    keep_ref[0], send_ref[0] = split_pairs(dot_tn(h, dq_ref[...]).astype(BF16), groups, my_index)
    for t in range(2):
        grad = (dkv_ref[t].astype(F32) + rkv_ref[t].astype(F32)).astype(BF16)
        sum_ref[t] = grad
        keep_ref[t + 1], send_ref[t + 1] = split_pairs(dot_tn(h, grad).astype(BF16), groups, my_index)


def qkv_grad_call(place, h, dq, dkv, rkv, groups):
    n, d = h.shape
    width = dq.shape[1]
    rows = d // (2 * groups)
    heads = width // GROUP_WIDTH
    pair = pl.BlockSpec((2, n, GROUP_WIDTH), lambda g, *_: (0, 0, g))
    share = pl.BlockSpec((3, groups, rows, GROUP_WIDTH), lambda g, *_: (g, 0, 0, 0))
    out = jax.ShapeDtypeStruct((3 * heads, groups, rows, GROUP_WIDTH), BF16)
    spec = pltpu.PrefetchScalarGridSpec(
        num_scalar_prefetch=1,
        grid=(heads,),
        in_specs=[resident((n, d)), pl.BlockSpec((n, GROUP_WIDTH), lambda g, *_: (0, g)), pair, pair],
        out_specs=[share, share, pair],
    )
    return pl.pallas_call(
        partial(qkv_grad_kernel, groups),
        grid_spec=spec,
        out_shape=[out, out, jax.ShapeDtypeStruct((2, n, width), BF16)],
        compiler_params=params(40),
        cost_estimate=cost(6 * n * d * width, 6 * d * width + 2 * n * d + 8 * n * width),
        name="qkv_grad",
    )(place, h, dq, dkv, rkv)


def head_back_kernel(weights, count, place, *refs):
    dqs, dkvs = refs[:count], refs[count : 2 * count]
    x_ref, gr_ref, gain_ref = refs[2 * count : 2 * count + 3]
    parts, refs = cut(refs[2 * count + 3 :], weights)
    tg_ref, dln_ref, wq, wk, wv, sem = refs
    load_all(weights, parts, place, (wq, wk, wv), sem)
    i = pl.program_id(0)
    dq = jnp.concatenate([r[...] for r in dqs], axis=1)
    dk = jnp.concatenate([r[0] for r in dkvs], axis=1)
    dv = jnp.concatenate([r[1] for r in dkvs], axis=1)
    grad = dot_nt(dq, wq[...]) + dot_nt(dk, wk[...]) + dot_nt(dv, wv[...])
    hat, scale = normed(x_ref[...].astype(F32))
    tg_ref[...] = (gr_ref[...] + norm_back(grad, gain_ref[...], hat, scale)).astype(BF16)
    dgain = jnp.sum(grad * hat, axis=0, keepdims=True)
    dbias = jnp.sum(grad, axis=0, keepdims=True)

    @pl.when(i == 0)
    def _():
        dln_ref[0:1, :] = dgain
        dln_ref[1:2, :] = dbias

    @pl.when(i > 0)
    def _():
        dln_ref[0:1, :] += dgain
        dln_ref[1:2, :] += dbias


def head_back_call(place, dqs, dkvs, x, gr, weights, gain):
    n, d = x.shape
    row = pl.BlockSpec((ROWS, d), lambda i, *_: (i, 0))
    specs, args = weight_args(weights)
    spec = pltpu.PrefetchScalarGridSpec(
        num_scalar_prefetch=1,
        grid=(n // ROWS,),
        in_specs=[pl.BlockSpec((ROWS, a.shape[1]), lambda i, *_: (i, 0)) for a in dqs]
        + [pl.BlockSpec((2, ROWS, a.shape[2]), lambda i, *_: (0, i, 0)) for a in dkvs]
        + [row, row, resident((1, d))]
        + specs,
        out_specs=[row, pl.BlockSpec((2, d), lambda *_: (0, 0))],
        scratch_shapes=[pltpu.VMEM((d, d), BF16)] * 3 + [pltpu.SemaphoreType.DMA((3,))],
    )
    return pl.pallas_call(
        partial(head_back_kernel, weights, len(dqs)),
        grid_spec=spec,
        out_shape=[jax.ShapeDtypeStruct((n, d), BF16), jax.ShapeDtypeStruct((2, d), F32)],
        compiler_params=params(48),
        cost_estimate=cost(6 * n * d * d, 6 * d * d + 14 * n * d),
        name="qkv_back",
    )(place, *dqs, *dkvs, x, gr, gain, *args)


class Term:
    def __init__(self, array, axes, first=0, count=None):
        self.array, self.axes, self.first = array, axes, first
        self.count = array.shape[0] if count is None else count
        self.whole = first % self.count != 0

    def spec(self, settled, flipped, open_bits, steps_bits):
        def index_map(step, mine):
            at = [0 if self.whole else self.first // self.count]
            for b in self.axes:
                if (flipped >> b) & 1:
                    at.append(1 - mine[b])
                elif b in settled:
                    at.append(mine[b])
                elif b in steps_bits:
                    at.append((step >> (len(steps_bits) - 1 - steps_bits.index(b))) & 1)
                else:
                    at.append(0)
            return (*at, 0, 0)

        lead = self.array.shape[0] if self.whole else self.count
        inner = tuple(2 if b in open_bits and b not in steps_bits else None for b in self.axes)
        return pl.BlockSpec((lead,) + inner + self.array.shape[-2:], index_map)

    def read(self, ref):
        start = self.first if self.whole else 0
        return ref[start : start + self.count].astype(F32)


class Cube:
    def __init__(self, dp, index, order):
        self.bits = dp.bit_length() - 1
        self.dp, self.order = dp, order
        self.mine = ((index >> jnp.arange(self.bits, dtype=jnp.int32)) & 1).astype(jnp.int32)

    def send(self, array, flip):
        return lax.ppermute(array, "dp", [(i, i ^ flip) for i in range(self.dp)])

    def far(self, low=2):
        return [f << low for f in range(1, 1 << (self.bits - low))]

    def terms(self, arrays, first=0, count=None):
        made = []
        for array in arrays:
            lead, _, rows, width = array.shape
            shape = (lead,) + (2,) * self.bits + (rows, width)
            made.append(Term(array.reshape(shape), list(range(self.bits))[::-1], first, count))
        return made

    def add(self, outputs, dtype):
        in_specs, args, plan, out_specs, out_shape = [], [], [], [], []
        for output in outputs:
            lead = 0
            for stream, settled, flipped in output:
                open_bits = [b for b in range(self.bits)[::-1] if b not in settled and not (flipped >> b) & 1]
                steps_bits = open_bits[:STEP_BITS]
                for term in stream:
                    in_specs.append(term.spec(settled, flipped, open_bits, steps_bits))
                    args.append(term.array)
                plan.append((len(out_specs), lead, list(stream)))
                lead += stream[0].count
            outer, inner = len(steps_bits), len(open_bits) - len(steps_bits)

            def out_map(step, mine, outer=outer, inner=inner):
                return (0, *[(step >> (outer - 1 - k)) & 1 for k in range(outer)], *[0] * inner, 0, 0)

            shape = output[0][0][0].array.shape[-2:]
            out_specs.append(pl.BlockSpec((lead,) + (None,) * outer + (2,) * inner + shape, out_map))
            out_shape.append(jax.ShapeDtypeStruct((lead,) + (2,) * (outer + inner) + shape, dtype))

        def kernel(mine, *refs):
            ins, outs = refs[: len(args)], refs[len(args) :]
            at = 0
            for out, first, stream in plan:
                total = stream[0].read(ins[at])
                for k in range(1, len(stream)):
                    total = total + stream[k].read(ins[at + k])
                outs[out][first : first + stream[0].count] = total.astype(dtype)
                at += len(stream)

        spec = pltpu.PrefetchScalarGridSpec(
            num_scalar_prefetch=1, grid=(2**outer,), in_specs=in_specs, out_specs=out_specs
        )
        size = sum(math.prod(o.shape) for o in out_shape)
        call = pl.pallas_call(
            kernel,
            grid_spec=spec,
            out_shape=out_shape,
            compiler_params=params(40),
            cost_estimate=cost(4 * size, 8 * size),
            name="add_terms",
        )
        return self.order.run(call, self.mine, *args)


def merge(arrays, outputs, *awaited):
    d = arrays[0].shape[-1]
    shapes = []
    for output in outputs:
        blocks = sum(arrays[i].shape[0] for i, _, _ in output)
        shapes.append(jax.ShapeDtypeStruct((blocks, output[0][2], d), BF16))

    def kernel(*refs):
        ins, outs = refs[: len(arrays)], refs[len(arrays) + len(awaited) :]
        for out, output in zip(outs, outputs, strict=True):
            at = 0
            for i, first, count in output:
                blocks = ins[i].shape[0]
                out[at : at + blocks] = ins[i][:, first : first + count]
                at += blocks

    whole = pl.BlockSpec(memory_space=pltpu.VMEM)
    size = sum(math.prod(shape.shape) for shape in shapes)
    return pl.pallas_call(
        kernel,
        in_specs=[whole] * len(arrays) + [HBM] * len(awaited),
        out_specs=[whole] * len(outputs),
        out_shape=shapes,
        compiler_params=params(40),
        cost_estimate=cost(size, 4 * size),
        name="merge",
    )(*arrays, *awaited)


class Side:
    def __init__(self, cube, order):
        self.cube, self.order = cube, order

    def hold(self, held, bit):
        self.held = held
        self.got = self.cube.send(held, 1 << bit)

    def parts_of(self):
        last = 1 << self.order[1]
        flips = [0] + self.cube.far()
        flips = flips + [f ^ (1 << self.order[0]) for f in flips]
        moved = [f ^ last for f in flips]
        return [(flips, 0), (moved, 0), (flips, 1), (moved, 1)]

    def index(self, flip):
        first, last = self.order
        return (flip >> 2) + (((flip >> first) & 1) << (self.cube.bits - 2)), (flip >> last) & 1


class Gather:
    def __init__(self, cube, order, exchange, one, two):
        self.cube, self.order, self.exchange = cube, order, exchange
        self.rows = one.shape[0]
        self.local = jnp.concatenate([one, two], axis=0)[None]
        self.sides = (Side(cube, (1, 0)), Side(cube, (0, 1)))

    def far(self):
        local = self.order.after(self.local)
        self.pieces = [local] + [self.cube.send(local, f) for f in self.cube.far()]
        self.order.note(local)

    def near(self, *awaited):
        total = self.local.shape[1]
        outputs = [
            [(i, first, count) for i in range(len(self.pieces))]
            for first, count in ((0, self.rows), (self.rows, total - self.rows))
        ]
        held = self.order.run(lambda first, *rest: merge((first, *rest), outputs, *awaited), *self.pieces)
        for s, array in zip(self.sides, held, strict=True):
            s.hold(array, s.order[0])

    def last(self, *awaited):
        arrays = [a for s in self.sides for a in (s.held, s.got)]
        outputs = [[(i, 0, arrays[i].shape[1]), (i + 1, 0, arrays[i].shape[1])] for i in (0, 2)]
        held = self.order.run(lambda first, *rest: merge((first, *rest), outputs, *awaited), *arrays)
        for s, array in zip(self.sides, held, strict=True):
            s.hold(array, s.order[1])
            s.other = self.exchange(s.held)

    def finish(self):
        for s in self.sides:
            s.buffers = [s.held, s.got, s.other, self.exchange(self.order.after(s.got))]
            s.parts = s.parts_of()


class Order:
    def __init__(self):
        self.token = ()

    def after(self, *values):
        if self.token:
            values = lax.optimization_barrier((values, self.token))[0]
        return values if len(values) > 1 else values[0]

    def note(self, *token):
        self.token = token

    def run(self, call, first, *rest):
        out = call(self.after(first), *rest)
        self.note(jax.tree.leaves(out)[0])
        return out


class Scatter:
    def __init__(self, cube, one, two):
        self.cube, self.sides, self.step = cube, (one, two), 0
        self.sent, self.last = [], []

    def advance(self):
        step, cube = self.step, self.cube
        if step < 2:
            flips = (1 << step, 1 << (1 - step))
            done = ([], []) if step == 0 else ([0], [1])
            self.sent = cube.add(
                [[(stream, done[s], flips[s]) for stream in self.sides[s]] for s in range(2)], BF16
            )
            self.last = []
            for s in range(2):
                got = cube.send(self.sent[s], flips[s])
                self.last.append(got)
                axes = [b for b in range(cube.bits)[::-1] if b not in done[s] and not (flips[s] >> b) & 1]
                at = 0
                for stream in self.sides[s]:
                    stream.append(Term(got, axes, at, stream[0].count))
                    at += stream[0].count
        else:
            streams = [stream for side in self.sides for stream in side]
            done = list(range(cube.bits))
            self.sent = cube.add([[(stream, done, f) for stream in streams] for f in cube.far()], BF16)
            self.last = [cube.send(sent, f) for sent, f in zip(self.sent, cube.far(), strict=True)]
            for got in self.last:
                at = 0
                for stream in streams:
                    stream.append(Term(got, [], at, stream[0].count))
                    at += stream[0].count
        self.step += 1
        return self

    def finish(self):
        while self.step < 3:
            self.advance()
        done = list(range(self.cube.bits))
        return self.cube.add([[(stream, done, 0)] for side in self.sides for stream in side], F32)


def gate(value, *others):
    return lax.optimization_barrier((value, others))[0]


def block_table(seg_full, seg_local, my_index, n, bq, bk):
    first, last = seg_local[::bq], seg_local[bq - 1 :: bq]
    low = jnp.sum((seg_full[None, :] < first[:, None]).astype(jnp.int32), axis=1)
    high = jnp.sum((seg_full[None, :] <= last[:, None]).astype(jnp.int32), axis=1)
    columns = []
    for index in (my_index, 1 - my_index):
        start = jnp.clip(low - index * n, 0, n)
        stop = jnp.clip(high - index * n, 0, n)
        block = start // bk
        columns += [block, jnp.where(stop > start, (stop + bk - 1) // bk - block, 0)]
    return jnp.stack(columns, axis=1).reshape(-1).astype(jnp.int32)


def body(
    tokens,
    segments,
    ln1_gain,
    ln1_bias,
    w_query,
    w_key,
    w_value,
    w_out,
    ln2_gain,
    ln2_bias,
    w_up,
    w_down,
    cotangent,
):
    x = tokens[0]
    n, d = x.shape
    cot = cotangent[0]
    rows = w_query.shape[0]
    devices = d // rows
    hidden = w_up.shape[1]
    per_device = hidden // devices
    my_index = lax.axis_index("seq")
    seg_full = segments[0]
    seg_local = lax.dynamic_slice_in_dim(seg_full, my_index * n, n)
    seg_other = lax.dynamic_slice_in_dim(seg_full, (1 - my_index) * n, n)
    tab = block_table(seg_full, seg_local, my_index, n, ATT_Q, ATT_K)
    seg_q = seg_local.reshape(n // ATT_Q, 1, ATT_Q)
    seg_own_col, seg_other_col = seg_local[:, None], seg_other[:, None]

    dp = devices // 2
    dp_index = lax.axis_index("dp")
    order = Order()
    cube = Cube(dp, dp_index, order)
    place = jnp.stack([dp_index, my_index]).astype(jnp.int32)
    swap = [(0, 1), (1, 0)]
    tiles = hidden // d

    def exchange(value):
        return lax.ppermute(value, "seq", swap)

    def halves(value, axis):
        keep = lax.dynamic_index_in_dim(value, my_index, axis, keepdims=False)
        send = lax.dynamic_index_in_dim(value, 1 - my_index, axis, keepdims=False)
        return keep, send

    vectors = jnp.concatenate([ln1_gain, ln1_bias, ln2_gain, ln2_bias]).astype(F32)
    vectors = jnp.broadcast_to(vectors[None], (devices, 4 * rows))
    vectors = lax.all_to_all(vectors, BOTH, 0, 0, tiled=True)
    ln = vectors.reshape(devices, 4, rows).transpose(1, 0, 2).reshape(4, 1, d)

    aligned = rows % 32 == 0
    groups = d // GROUP_WIDTH
    if aligned:
        cut_row, half_down = rows // 2, per_device // 2
        up_tiles = w_up.reshape(rows, tiles, d).transpose(1, 0, 2)
        half_up = tiles // 2 * rows
        low_up, high_up = (u.reshape(half_up, d) for u in (up_tiles[: tiles // 2], up_tiles[tiles // 2 :]))
        head = Gather(
            cube, order, exchange,
            jnp.concatenate([w_key, w_query[:cut_row]]), jnp.concatenate([w_value, w_query[cut_row:]]),
        )
        low = Gather(
            cube, order, exchange,
            jnp.concatenate([low_up, w_out[:cut_row]]), jnp.concatenate([w_down[:half_down], w_out[cut_row:]]),
        )
        high = Gather(cube, order, exchange, high_up, w_down[half_down:])
        head.far()
        head.near(vectors)
        low.far()
        head.last()
        order.note(*[side.got for side in head.sides])
        head.finish()
        low.near()
        high.far()
        key_w = Spread(rows, [(head.sides[0], 0, rows, 0)])
        value_w = Spread(rows, [(head.sides[1], 0, rows, 0)])
        query_w = Spread(rows, [(head.sides[0], rows, cut_row, 0), (head.sides[1], rows, cut_row, cut_row)])
    else:
        every = jnp.concatenate([w_query, w_key, w_value, w_out], axis=0).reshape(4, rows, d)
        every = lax.all_gather(every, BOTH, axis=1, tiled=True)
        query_w, key_w, value_w, out_w = (Plain(every[t], rows) for t in range(4))
        up_all = lax.all_gather(w_up, BOTH, axis=0, tiled=True)
        ups = [Plain(up_all[:, t * d : (t + 1) * d], rows) for t in range(tiles)]
        downs = [Plain(lax.all_gather(w_down, BOTH, axis=0, tiled=True), per_device)]

    h1, own = order.run(kv_call, place, x, ln[0], ln[1], [key_w, value_w])
    if aligned:
        low.last()
    other = exchange(order.after(own))
    q = order.run(q_call, place, h1, [query_w])
    outs, lses = [], []
    plan = [(0, 1), (1, 1), (2, 2)] if groups == 4 else [(g, 1) for g in range(groups)]
    for i, (start, count) in enumerate(plan):
        if aligned and i == 1:
            high.near(*[side.other for side in low.sides])
        if aligned and i == 2:
            high.last()
            low.finish()
        out, lse = order.run(
            attend_call, tab, q, own, other, seg_q, seg_own_col, seg_other_col, ATT_Q, ATT_K, start, count
        )
        outs.append(out)
        lses.append(lse)
    if aligned:
        out_w = Spread(
            rows, [(low.sides[0], half_up, cut_row, 0), (low.sides[1], half_down, cut_row, cut_row)]
        )
    mid, h2 = order.run(mid_call, place, x, outs, [out_w], ln[2], ln[3])
    if aligned:
        high.finish()

    up_rows = tiles * rows
    if aligned:
        ups = [
            Spread(rows, [((low, high)[t // (tiles // 2)].sides[0], t % (tiles // 2) * rows, rows, 0)])
            for t in range(tiles)
        ]
        downs = [Spread(half_down, [(r.sides[1], 0, half_down, 0)]) for r in (low, high)]
        per_tile = d // FF_COLS
        group = FF_COLS // per_device
        up_out = (
            pl.BlockSpec((None, dp, rows, FF_COLS), lambda j, *_: (j // per_tile, 0, 0, j % per_tile)),
            jax.ShapeDtypeStruct((tiles, dp, rows, d), BF16),
        )
        down_out = (
            pl.BlockSpec((tiles, group // 2, rows, d), lambda j, *_: (0, j, 0, 0)),
            jax.ShapeDtypeStruct((tiles, dp, rows, d), BF16),
        )
        grad_specs = [up_out, up_out, down_out, down_out]
    else:
        grad_specs = [
            (pl.BlockSpec((d, FF_COLS), lambda j, *_: (0, j)), jax.ShapeDtypeStruct((d, hidden), BF16)),
            (pl.BlockSpec((FF_COLS, d), lambda j, *_: (j, 0)), jax.ShapeDtypeStruct((hidden, d), BF16)),
        ]
    mixed, gmid, *grads = order.run(ffn_call, place, h2, cot, ups, downs, mid, grad_specs, hidden, aligned)
    if not aligned:
        dwu = grads[0].reshape(dp, 2, rows, tiles, d).transpose(3, 0, 1, 2, 4)
        dwd = grads[1].reshape(dp, 2, tiles, rows, d).transpose(2, 0, 1, 3, 4)
        grads = [*halves(dwu, 2), *halves(dwd, 2)]
    keep_up, send_up, keep_down, send_down = grads
    got_up, got_down = exchange(send_up), exchange(send_down)
    big = Scatter(cube, [cube.terms([keep_up, got_up])], [cube.terms([keep_down, got_down])])

    grad_mid, grad_att, keep_out, send_out, dln2 = order.run(
        mid_back_call, place, gmid, mid, cot, outs, [out_w], ln[2], dp
    )
    big.advance()
    got_out = exchange(order.after(send_out))
    dqs, dkvs = [], []

    def attend_back(g):
        which = [i for i, (start, _) in enumerate(plan) if start <= g][-1]
        return order.run(
            attend_back_call, tab, q, grad_att, outs[which], own, other, seg_q, seg_own_col, seg_other_col,
            lses[which], ATT_Q, ATT_K, g, 1, g - plan[which][0],
        )

    def finish_group(dq, dkv, got):
        keep, send, dkv = order.run(qkv_grad_call, place, h1, dq, dkv, got, dp)
        dqs.append(dq)
        dkvs.append(dkv)
        return keep, send

    dq_0, dkv_0, sent_0 = attend_back(0)
    dq_1, dkv_1, sent_1 = attend_back(1)
    got_0 = exchange(order.after(sent_0))
    big.advance()
    got_1 = exchange(order.after(sent_1))
    keep_0, send_0 = finish_group(dq_0, dkv_0, got_0)
    keep_1, send_1 = finish_group(dq_1, dkv_1, got_1)
    terms_0, terms_1 = [keep_0, exchange(order.after(send_0))], [keep_1, exchange(order.after(send_1))]
    dq_2, dkv_2, sent_2 = attend_back(2)
    big.advance()
    tail_one = Scatter(
        cube,
        [cube.terms(terms_0), cube.terms([keep_out, got_out], 0, 2)],
        [cube.terms(terms_1), cube.terms([keep_out, got_out], 2, 2)],
    )
    tail_one.advance()
    got_2 = exchange(order.after(sent_2))
    dq_3, dkv_3, sent_3 = attend_back(3)
    up_share, down_share = big.finish()
    tail_one.advance()
    got_3 = exchange(order.after(sent_3))
    keep_2, send_2 = finish_group(dq_2, dkv_2, got_2)
    keep_3, send_3 = finish_group(dq_3, dkv_3, got_3)
    tail_one.advance()
    terms_2, terms_3 = [keep_2, exchange(order.after(send_2))], [keep_3, exchange(order.after(send_3))]
    tail_two = Scatter(cube, [cube.terms(terms_2)], [cube.terms(terms_3)])
    tail_two.advance()
    token_grad, dln1 = order.run(
        head_back_call, place, dqs, dkvs, x, grad_mid, [query_w, key_w, value_w], ln[0]
    )
    tail_two.advance()
    one_a, out_a, one_b, out_b = tail_one.finish()
    dln = jnp.concatenate([dln1, order.after(dln2)], axis=0).reshape(4, devices, rows).transpose(1, 0, 2)
    dln = lax.all_to_all(dln.reshape(devices, 4 * rows), BOTH, 0, 0, tiled=True)
    dln = jnp.sum(dln.reshape(devices, 4, rows), axis=0)
    tail_two.advance()
    two_a, two_b = tail_two.finish()

    up_share = up_share.transpose(1, 0, 2).reshape(rows, hidden)
    down_share = down_share.reshape(per_device, d)
    qkv_share = jnp.concatenate([one_a, one_b, two_a, two_b], axis=-1)
    out_share = jnp.concatenate([out_a, out_b], axis=0).transpose(1, 0, 2).reshape(rows, d)
    return (
        mixed[None],
        token_grad[None],
        dln[0],
        dln[1],
        qkv_share[0],
        qkv_share[1],
        qkv_share[2],
        out_share,
        dln[2],
        dln[3],
        up_share,
        down_share,
    )


def solution(mesh):
    row, act, vec = P(BOTH, None), P("dp", "seq", None), P(BOTH)
    in_specs = (act, P("dp", None), vec, vec, row, row, row, row, vec, vec, row, row, act)
    out_specs = (act, act, vec, vec, row, row, row, row, vec, vec, row, row)
    return jax.shard_map(body, mesh=mesh, in_specs=in_specs, out_specs=out_specs, check_vma=False)
```

```python
import math
from functools import partial

import jax
import jax.numpy as jnp
from jax import lax
from jax.experimental import pallas as pl
from jax.experimental.pallas import tpu as pltpu
from jax.sharding import PartitionSpec as P

BF16 = jnp.bfloat16
F32 = jnp.float32
HEAD_DIM = 64
GROUP = 4
GROUP_WIDTH = GROUP * HEAD_DIM
NEG = -1000000000.0
BOTH = ("dp", "seq")
ATT_Q = 256
ATT_K = 512
ROW_ALIGN = 16
ROWS = 256
FF_COLS = 512
COST_SCALE = 100000
STEP_BITS = 1


def dot_nn(left, right):
    return lax.dot_general(left, right, (((1,), (0,)), ((), ())), preferred_element_type=F32)


def dot_nt(left, right):
    return lax.dot_general(left, right, (((1,), (1,)), ((), ())), preferred_element_type=F32)


def dot_tn(left, right):
    return lax.dot_general(left, right, (((0,), (0,)), ((), ())), preferred_element_type=F32)


def params(mib):
    return pltpu.CompilerParams(vmem_limit_bytes=mib << 20)


def cost(flops, nbytes, scale=None):
    if scale:
        return pl.CostEstimate(flops=scale * flops, bytes_accessed=scale * nbytes, transcendentals=0)
    return pl.CostEstimate(flops=flops // COST_SCALE, bytes_accessed=nbytes // COST_SCALE, transcendentals=0)


def normed(values):
    centre = values - jnp.mean(values, axis=-1, keepdims=True)
    scale = lax.rsqrt(jnp.mean(centre * centre, axis=-1, keepdims=True) + 1e-05)
    return centre * scale, scale


def norm_back(grad, gain_vec, hat, scale):
    inner = grad * gain_vec
    return scale * (
        inner
        - jnp.mean(inner, axis=-1, keepdims=True)
        - hat * jnp.mean(inner * hat, axis=-1, keepdims=True)
    )


def flat(ref):
    value = ref[...]
    return value.reshape(-1, value.shape[-1])


def resident(shape):
    zeros = (0,) * len(shape)
    return pl.BlockSpec(shape, lambda *_: zeros, pipeline_mode=pl.Buffered(1))


class Spread:
    def __init__(self, block, pieces):
        self.block, self.pieces = block, pieces
        self.args = [b for rounds, *_ in pieces for b in rounds.buffers]

    def start(self, refs, place, target, sem, columns=None):
        for i, (rounds, first, count, at) in enumerate(self.pieces):
            for ref, (flips, core) in zip(refs[4 * i : 4 * i + 4], rounds.parts, strict=True):
                for e, flip in enumerate(flips):
                    device = (place[0] ^ flip) * 2 + (place[1] ^ core)
                    row = pl.multiple_of(device * self.block + at, count)
                    source = ref.at[e, pl.ds(first, count)]
                    if columns is not None:
                        source = ref.at[e, pl.ds(first, count), columns]
                    pltpu.make_async_copy(source, target.at[pl.ds(row, count), :], sem).start()

    def start_rows(self, refs, place, target, sem, first, group):
        ((rounds, begin, count, _),) = self.pieces
        for k in range(group):
            device = first + k
            flip = (device // 2) ^ place[0]
            at, last = rounds.index(flip)
            core = (device % 2) ^ place[1]
            for i, ref in enumerate(refs):

                @pl.when((last == i % 2) & (core == i // 2))
                def _(ref=ref, at=at, k=k):
                    pltpu.make_async_copy(
                        ref.at[at, pl.ds(begin, count)], target.at[pl.ds(k * count, count), :], sem
                    ).start()


class Plain:
    def __init__(self, array, block):
        self.args, self.block = [array], block

    def start(self, refs, place, target, sem, columns=None):
        source = refs[0] if columns is None else refs[0].at[:, columns]
        pltpu.make_async_copy(source, target, sem).start()

    def start_rows(self, refs, place, target, sem, first, group):
        pltpu.make_async_copy(refs[0].at[pl.ds(first * self.block, group * self.block), :], target, sem).start()


def arrived(target, sem):
    pltpu.make_async_copy(target, target, sem).wait()


def cut(refs, weights):
    parts = []
    for weight in weights:
        parts.append(refs[: len(weight.args)])
        refs = refs[len(weight.args) :]
    return parts, refs


def load_all(weights, parts, place, targets, sem):
    @pl.when(pl.program_id(0) == 0)
    def _():
        for i, weight in enumerate(weights):
            weight.start(parts[i], place, targets[i], sem.at[i])
        for i in range(len(weights)):
            arrived(targets[i], sem.at[i])


HBM = pl.BlockSpec(memory_space=pl.ANY)


def weight_args(weights):
    args = [a for w in weights for a in w.args]
    return [HBM] * len(args), args


def kv_kernel(weights, place, x_ref, gain_ref, bias_ref, *refs):
    parts, refs = cut(refs, weights)
    h_ref, kv_ref, wk, wv, sem = refs
    load_all(weights, parts, place, (wk, wv), sem)
    hat, _ = normed(x_ref[...].astype(F32))
    low = (hat * gain_ref[...] + bias_ref[...]).astype(BF16)
    h_ref[...] = low
    kv_ref[0] = dot_nn(low, wk[...]).astype(BF16)
    kv_ref[1] = dot_nn(low, wv[...]).astype(BF16)


def kv_call(place, x, gain, bias, weights):
    n, d = x.shape
    row = pl.BlockSpec((ROWS, d), lambda i, *_: (i, 0))
    specs, args = weight_args(weights)
    spec = pltpu.PrefetchScalarGridSpec(
        num_scalar_prefetch=1,
        grid=(n // ROWS,),
        in_specs=[row, resident((1, d)), resident((1, d))] + specs,
        out_specs=[row, pl.BlockSpec((2, ROWS, d), lambda i, *_: (0, i, 0))],
        scratch_shapes=[pltpu.VMEM((d, d), BF16)] * 2 + [pltpu.SemaphoreType.DMA((2,))],
    )
    return pl.pallas_call(
        partial(kv_kernel, weights),
        grid_spec=spec,
        out_shape=[jax.ShapeDtypeStruct((n, d), BF16), jax.ShapeDtypeStruct((2, n, d), BF16)],
        compiler_params=params(40),
        cost_estimate=cost(4 * n * d * d, 4 * d * d + 8 * n * d),
        name="kv_proj",
    )(place, x, gain, bias, *args)


def q_kernel(weights, place, h_ref, *refs):
    parts, refs = cut(refs, weights)
    q_ref, wq, sem = refs
    load_all(weights, parts, place, (wq,), sem)
    q_ref[...] = (dot_nn(h_ref[...], wq[...]).astype(BF16).astype(F32) * 0.125).astype(BF16)


def q_call(place, h, weights):
    n, d = h.shape
    row = pl.BlockSpec((ROWS, d), lambda i, *_: (i, 0))
    specs, args = weight_args(weights)
    spec = pltpu.PrefetchScalarGridSpec(
        num_scalar_prefetch=1,
        grid=(n // ROWS,),
        in_specs=[row] + specs,
        out_specs=row,
        scratch_shapes=[pltpu.VMEM((d, d), BF16), pltpu.SemaphoreType.DMA((1,))],
    )
    return pl.pallas_call(
        partial(q_kernel, weights),
        grid_spec=spec,
        out_shape=jax.ShapeDtypeStruct((n, d), BF16),
        compiler_params=params(32),
        cost_estimate=cost(2 * n * d * d, 2 * d * d + 4 * n * d),
        name="q_proj",
    )(place, h, *args)


def stack_heads(block):
    lane = lax.broadcasted_iota(jnp.int32, block.shape, 1) // HEAD_DIM
    zero = jnp.zeros_like(block)
    return jnp.concatenate([jnp.where(lane == h, block, zero) for h in range(GROUP)], axis=0)


def head_cols(value, h, width):
    return value[:, h * width : (h + 1) * width]


def head_rows(value, h):
    return value[h * HEAD_DIM : (h + 1) * HEAD_DIM, :]


def line_up(target, own_ref, other_ref, which, mine):
    n = own_ref.shape[1]
    target[pl.ds(pl.multiple_of(mine * n, n), n), :] = own_ref[which]
    target[pl.ds(pl.multiple_of((1 - mine) * n, n), n), :] = other_ref[which]
    target[2 * n :, :] = jnp.zeros((target.shape[0] - 2 * n, target.shape[1]), target.dtype)


def attend_kernel(bq, bk, tab, q_ref, own_ref, other_ref, sq_ref, s_ref, o_ref, lse_ref, k_s, v_s):
    i = pl.program_id(1)

    @pl.when(i == 0)
    def _():
        mine = tab[2 * pl.num_programs(1)]
        line_up(k_s, own_ref, other_ref, 0, mine)
        line_up(v_s, own_ref, other_ref, 1, mine)

    stacked = stack_heads(q_ref[...])
    seg_q = jnp.concatenate([sq_ref[0]] * GROUP, axis=1)
    first = tab[2 * i]

    def step(j, carry):
        top, total, acc = carry
        at = pl.multiple_of(first + j * bk, ROW_ALIGN)
        scores = dot_nt(k_s[pl.ds(at, bk), :], stacked)
        scores = jnp.where(s_ref[pl.ds(at, bk), :] == seg_q, scores, NEG)
        new_top = jnp.maximum(top, jnp.max(scores, axis=0, keepdims=True))
        decay = jnp.exp(top - new_top)
        probs = jnp.exp(scores - new_top)
        total = total * decay + jnp.sum(probs, axis=0, keepdims=True)
        low = probs.astype(BF16)
        values = v_s[pl.ds(at, bk), :].T
        acc = tuple(
            acc[h] * head_cols(decay, h, bq) + dot_nn(head_rows(values, h), head_cols(low, h, bq))
            for h in range(GROUP)
        )
        return new_top, total, acc

    state = (
        jnp.full((1, GROUP * bq), -jnp.inf, F32),
        jnp.zeros((1, GROUP * bq), F32),
        tuple(jnp.zeros((HEAD_DIM, bq), F32) for _ in range(GROUP)),
    )
    top, total, acc = lax.fori_loop(0, tab[2 * i + 1], step, state)
    out = jnp.concatenate([acc[h] / head_cols(total, h, bq) for h in range(GROUP)], axis=0)
    o_ref[...] = out.T.astype(BF16)
    lse_ref[0, 0] = top + jnp.log(total)


def attend_specs(n, bq, padded, first):
    def half(_):
        return pl.BlockSpec((2, n, GROUP_WIDTH), lambda g, i, *_: (0, 0, g + first))

    return [
        half(0),
        half(1),
        pl.BlockSpec((1, 1, bq), lambda g, i, *_: (i, 0, 0)),
        pl.BlockSpec((padded, 1), lambda *_: (0, 0)),
    ]


def attend_call(tab, q, own, other, seg_q, seg_col, bq, bk, first, groups):
    n, d = q.shape
    blocks = n // bq
    padded = seg_col.shape[0]
    spec = pltpu.PrefetchScalarGridSpec(
        num_scalar_prefetch=1,
        grid=(groups, blocks),
        in_specs=[pl.BlockSpec((bq, GROUP_WIDTH), lambda g, i, *_: (i, g + first))]
        + attend_specs(n, bq, padded, first),
        out_specs=[
            pl.BlockSpec((bq, GROUP_WIDTH), lambda g, i, *_: (i, g)),
            pl.BlockSpec((1, 1, 1, GROUP * bq), lambda g, i, *_: (g, i, 0, 0)),
        ],
        scratch_shapes=[pltpu.VMEM((padded, GROUP_WIDTH), BF16)] * 2,
    )
    return pl.pallas_call(
        partial(attend_kernel, bq, bk),
        grid_spec=spec,
        out_shape=[
            jax.ShapeDtypeStruct((n, groups * GROUP_WIDTH), BF16),
            jax.ShapeDtypeStruct((groups, blocks, 1, GROUP * bq), F32),
        ],
        compiler_params=params(56),
        cost_estimate=cost(8_000_000_000 * groups, 3 * groups * n * d),
        name="attend",
    )(tab, q, own, other, seg_q, seg_col)


def attend_back_kernel(
    bq, bk, tab, q_ref, go_ref, o_ref, lse_ref, own_ref, other_ref, sq_ref, s_ref,
    dq_ref, down_ref, dpart_ref, k_s, v_s, dk_s, dv_s,
):
    i = pl.program_id(1)
    mine = tab[2 * pl.num_programs(1)]

    @pl.when(i == 0)
    def _():
        line_up(k_s, own_ref, other_ref, 0, mine)
        line_up(v_s, own_ref, other_ref, 1, mine)
        dk_s[...] = jnp.zeros_like(dk_s)
        dv_s[...] = jnp.zeros_like(dv_s)

    stacked = stack_heads(q_ref[...])
    grad = go_ref[...]
    stacked_grad = stack_heads(grad)
    product = (grad.astype(F32) * o_ref[...].astype(F32)).T
    inner = jnp.concatenate(
        [jnp.sum(head_rows(product, h), axis=0, keepdims=True) for h in range(GROUP)], axis=1
    )
    seg_q = jnp.concatenate([sq_ref[0]] * GROUP, axis=1)
    lse = lse_ref[0, 0]
    first = tab[2 * i]

    def step(j, acc):
        at = pl.multiple_of(first + j * bk, ROW_ALIGN)
        keys = k_s[pl.ds(at, bk), :]
        scores = dot_nt(keys, stacked)
        scores = jnp.where(s_ref[pl.ds(at, bk), :] == seg_q, scores, NEG)
        probs = jnp.exp(scores - lse)
        grad_probs = dot_nt(v_s[pl.ds(at, bk), :], stacked_grad)
        grad_scores = (probs * (grad_probs - inner)).astype(BF16)
        dv_s[pl.ds(at, bk), :] += dot_nn(probs.astype(BF16), stacked_grad)
        dk_s[pl.ds(at, bk), :] += dot_nn(grad_scores, stacked)
        keys_t = keys.T
        return tuple(
            acc[h] + dot_nn(head_rows(keys_t, h), head_cols(grad_scores, h, bq)) for h in range(GROUP)
        )

    state = tuple(jnp.zeros((HEAD_DIM, bq), F32) for _ in range(GROUP))
    state = lax.fori_loop(0, tab[2 * i + 1], step, state)
    dq_ref[...] = (jnp.concatenate(state, axis=0).T * 0.125).astype(BF16)

    @pl.when(i == pl.num_programs(1) - 1)
    def _():
        n = down_ref.shape[1]
        for ref, half in ((down_ref, mine), (dpart_ref, 1 - mine)):
            rows = pl.ds(pl.multiple_of(half * n, n), n)
            ref[0] = dk_s[rows, :].astype(BF16)
            ref[1] = dv_s[rows, :].astype(BF16)


def attend_back_call(tab, q, grad, out, own, other, seg_q, seg_col, lse, bq, bk, first, groups, out_first):
    n, d = q.shape
    blocks = n // bq
    padded = seg_col.shape[0]
    query = pl.BlockSpec((bq, GROUP_WIDTH), lambda g, i, *_: (i, g + first))
    pair = pl.BlockSpec((2, n, GROUP_WIDTH), lambda g, i, *_: (0, 0, g))
    spec = pltpu.PrefetchScalarGridSpec(
        num_scalar_prefetch=1,
        grid=(groups, blocks),
        in_specs=[
            query,
            query,
            pl.BlockSpec((bq, GROUP_WIDTH), lambda g, i, *_: (i, g + out_first)),
            pl.BlockSpec((1, 1, 1, GROUP * bq), lambda g, i, *_: (g + out_first, i, 0, 0)),
        ]
        + attend_specs(n, bq, padded, first),
        out_specs=[pl.BlockSpec((bq, GROUP_WIDTH), lambda g, i, *_: (i, g)), pair, pair],
        scratch_shapes=[pltpu.VMEM((padded, GROUP_WIDTH), BF16)] * 2
        + [pltpu.VMEM((padded, GROUP_WIDTH), F32)] * 2,
    )
    width = groups * GROUP_WIDTH
    return pl.pallas_call(
        partial(attend_back_kernel, bq, bk),
        grid_spec=spec,
        out_shape=[
            jax.ShapeDtypeStruct((n, width), BF16),
            jax.ShapeDtypeStruct((2, n, width), BF16),
            jax.ShapeDtypeStruct((2, n, width), BF16),
        ],
        compiler_params=params(56),
        cost_estimate=cost(12_000_000_000 * groups, 6 * groups * n * d),
        name="attend_back",
    )(tab, q, grad, out, lse, own, other, seg_q, seg_col)


def mid_kernel(weights, count, place, x_ref, gain_ref, bias_ref, *refs):
    outs, refs = refs[:count], refs[count:]
    parts, refs = cut(refs, weights)
    r_ref, h_ref, wo, sem = refs
    load_all(weights, parts, place, (wo,), sem)
    mid = x_ref[...].astype(F32) + dot_nn(jnp.concatenate([o[...] for o in outs], axis=1), wo[...])
    r_ref[...] = mid
    hat, _ = normed(mid)
    h_ref[...] = (hat * gain_ref[...] + bias_ref[...]).astype(BF16)


def mid_call(place, x, outs, weights, gain, bias):
    n, d = x.shape
    row = pl.BlockSpec((ROWS, d), lambda i, *_: (i, 0))
    specs, args = weight_args(weights)
    spec = pltpu.PrefetchScalarGridSpec(
        num_scalar_prefetch=1,
        grid=(n // ROWS,),
        in_specs=[row, resident((1, d)), resident((1, d))]
        + [pl.BlockSpec((ROWS, o.shape[1]), lambda i, *_: (i, 0)) for o in outs]
        + specs,
        out_specs=[row, row],
        scratch_shapes=[pltpu.VMEM((d, d), BF16), pltpu.SemaphoreType.DMA((1,))],
    )
    return pl.pallas_call(
        partial(mid_kernel, weights, len(outs)),
        grid_spec=spec,
        out_shape=[jax.ShapeDtypeStruct((n, d), F32), jax.ShapeDtypeStruct((n, d), BF16)],
        compiler_params=params(32),
        cost_estimate=cost(2 * n * d * d, 2 * d * d + 10 * n * d),
        name="out_proj",
    )(place, x, gain, bias, *outs, *args)


def mid_back_kernel(weights, count, place, gh_ref, r_ref, g_ref, gain_ref, *refs):
    outs, refs = refs[:count], refs[count:]
    parts, refs = cut(refs, weights)
    gr_ref, go_ref, keep_ref, send_ref, dln_ref, acc, wo, sem = refs
    load_all(weights, parts, place, (wo,), sem)
    i = pl.program_id(0)
    hat, scale = normed(r_ref[...])
    grad = gh_ref[...]
    total = g_ref[...].astype(F32) + norm_back(grad, gain_ref[...], hat, scale)
    gr_ref[...] = total
    low = total.astype(BF16)
    go_ref[...] = dot_nt(low, wo[...]).astype(BF16)
    part = dot_tn(jnp.concatenate([o[...] for o in outs], axis=1), low)
    dgain = jnp.sum(grad * hat, axis=0, keepdims=True)
    dbias = jnp.sum(grad, axis=0, keepdims=True)

    @pl.when(i == 0)
    def _():
        acc[...] = part
        dln_ref[0:1, :] = dgain
        dln_ref[1:2, :] = dbias

    @pl.when(i > 0)
    def _():
        acc[...] += part
        dln_ref[0:1, :] += dgain
        dln_ref[1:2, :] += dbias

    @pl.when(i == pl.num_programs(0) - 1)
    def _():
        lanes = keep_ref.shape[3]
        for ref, value in zip(
            (keep_ref, send_ref), split_pairs(acc[...].astype(BF16), keep_ref.shape[1], place[1]), strict=True
        ):
            for t in range(ref.shape[0]):
                ref[t] = value[:, :, t * lanes : (t + 1) * lanes]


def mid_back_call(place, grad, mid, cot, outs, weights, gain, groups):
    n, d = mid.shape
    row = pl.BlockSpec((ROWS, d), lambda i, *_: (i, 0))
    share = (d // GROUP_WIDTH, groups, d // (2 * groups), GROUP_WIDTH)
    specs, args = weight_args(weights)
    spec = pltpu.PrefetchScalarGridSpec(
        num_scalar_prefetch=1,
        grid=(n // ROWS,),
        in_specs=[row, row, row, resident((1, d))]
        + [pl.BlockSpec((ROWS, o.shape[1]), lambda i, *_: (i, 0)) for o in outs]
        + specs,
        out_specs=[
            row,
            row,
            pl.BlockSpec(share, lambda *_: (0, 0, 0, 0)),
            pl.BlockSpec(share, lambda *_: (0, 0, 0, 0)),
            pl.BlockSpec((2, d), lambda *_: (0, 0)),
        ],
        scratch_shapes=[
            pltpu.VMEM((d, d), F32),
            pltpu.VMEM((d, d), BF16),
            pltpu.SemaphoreType.DMA((1,)),
        ],
    )
    return pl.pallas_call(
        partial(mid_back_kernel, weights, len(outs)),
        grid_spec=spec,
        out_shape=[
            jax.ShapeDtypeStruct((n, d), F32),
            jax.ShapeDtypeStruct((n, d), BF16),
            jax.ShapeDtypeStruct(share, BF16),
            jax.ShapeDtypeStruct(share, BF16),
            jax.ShapeDtypeStruct((2, d), F32),
        ],
        compiler_params=params(48),
        cost_estimate=cost(4 * n * d * d, 4 * d * d + 18 * n * d),
        name="out_proj_back",
    )(place, grad, mid, cot, gain, *outs, *args)


def split_pairs(value, groups, my_index):
    rows = value.shape[0] // (2 * groups)
    pairs = value.reshape(groups, 2, rows, value.shape[1])
    even, odd = pairs[:, 0], pairs[:, 1]
    first = my_index == 0
    return jnp.where(first, even, odd), jnp.where(first, odd, even)


def ffn_grads(h, grad, wu, wd):
    up = dot_nn(h, wu)
    cdf = 0.5 * (1.0 + lax.erf(up * 0.7071067811865476))
    act = (up * cdf).astype(BF16)
    slope = cdf + up * (jnp.exp(-0.5 * up * up) * 0.3989422804014327)
    gu = (dot_nt(grad, wd) * slope).astype(BF16)
    return act, gu, dot_tn(h, gu).astype(BF16), dot_tn(act, grad).astype(BF16)


def ffn_sums(j, act, gu, wu, wd, mid_ref, mixed_ref, gh_ref, acc):
    @pl.when(j == 0)
    def _():
        acc[...] = mid_ref[...] + dot_nn(act, wd)
        gh_ref[...] = dot_nt(gu, wu)

    @pl.when(j > 0)
    def _():
        acc[...] += dot_nn(act, wd)
        gh_ref[...] += dot_nt(gu, wu)

    @pl.when(j == pl.num_programs(0) - 1)
    def _():
        mixed_ref[...] = acc[...].astype(BF16)


def ffn_kernel(ups, downs, aligned, place, h_ref, g_ref, mid_ref, *refs):
    parts, refs = cut(refs, ups + downs)
    mixed_ref, gh_ref = refs[:2]
    grads = refs[2:6] if aligned else refs[2:4]
    wu_s, wd_s, acc, sem = refs[-4:]
    j, steps = pl.program_id(0), pl.num_programs(0)
    per_tile = h_ref.shape[1] // FF_COLS
    group = FF_COLS // sum(w.block for w in downs)

    def fetch(step, slot):
        column = pl.ds(pl.multiple_of((step % per_tile) * FF_COLS, FF_COLS), FF_COLS)
        for t, up in enumerate(ups):

            @pl.when(step // per_tile == t)
            def _(t=t, up=up):
                up.start(parts[t], place, wu_s.at[slot], sem.at[slot, 0], column)

        at = 0
        for i, down in enumerate(downs):
            count = group * down.block
            down.start_rows(
                parts[len(ups) + i], place, wd_s.at[slot, pl.ds(at, count), :], sem.at[slot, 1], step * group, group
            )
            at += count

    @pl.when(j == 0)
    def _():
        fetch(j, 0)

    @pl.when(j + 1 < steps)
    def _():
        fetch(j + 1, (j + 1) % 2)

    slot = j % 2
    arrived(wu_s.at[slot], sem.at[slot, 0])
    arrived(wd_s.at[slot], sem.at[slot, 1])
    wu, wd = wu_s[slot], wd_s[slot]
    if len(downs) > 1:
        width = wd.shape[1]
        stack, at = [], 0
        for down in downs:
            count = group * down.block
            stack.append(wd[at : at + count].reshape(group, down.block, width))
            at += count
        wd = jnp.concatenate(stack, axis=1).reshape(FF_COLS, width)
    act, gu, dwu, dwd = ffn_grads(h_ref[...], g_ref[...], wu, wd)
    if aligned:
        grads[0][...], grads[1][...] = split_pairs(dwu, grads[0].shape[0], place[1])
        for ref, value in zip(grads[2:], split_pairs(dwd, grads[2].shape[1], place[1]), strict=True):
            for t in range(ref.shape[0]):
                ref[t] = value[:, t * ref.shape[2] : (t + 1) * ref.shape[2]]
    else:
        grads[0][...] = dwu
        grads[1][...] = dwd
    ffn_sums(j, act, gu, wu, wd, mid_ref, mixed_ref, gh_ref, acc)


def ffn_call(place, h, cot, ups, downs, mid, grad_specs, hidden, aligned):
    n, d = h.shape
    full = resident((n, d))
    const = pl.BlockSpec((n, d), lambda j, *_: (0, 0))
    specs, args = weight_args(ups + downs)
    spec = pltpu.PrefetchScalarGridSpec(
        num_scalar_prefetch=1,
        grid=(hidden // FF_COLS,),
        in_specs=[full, full, full] + specs,
        out_specs=[const, const] + [g[0] for g in grad_specs],
        scratch_shapes=[
            pltpu.VMEM((2, d, FF_COLS), BF16),
            pltpu.VMEM((2, FF_COLS, d), BF16),
            pltpu.VMEM((n, d), F32),
            pltpu.SemaphoreType.DMA((2, 2)),
        ],
    )
    return pl.pallas_call(
        partial(ffn_kernel, ups, downs, aligned),
        grid_spec=spec,
        out_shape=[jax.ShapeDtypeStruct((n, d), BF16), jax.ShapeDtypeStruct((n, d), F32)]
        + [g[1] for g in grad_specs],
        compiler_params=params(60),
        cost_estimate=cost(12 * n * d * hidden, 8 * d * hidden + 14 * n * d),
        name="ffn",
    )(place, h, cot, mid, *args)


def qkv_grad_kernel(groups, place, h_ref, dq_ref, dkv_ref, rkv_ref, keep_ref, send_ref, sum_ref):
    h = h_ref[...]
    my_index = place[1]
    keep_ref[0], send_ref[0] = split_pairs(dot_tn(h, dq_ref[...]).astype(BF16), groups, my_index)
    for t in range(2):
        grad = (dkv_ref[t].astype(F32) + rkv_ref[t].astype(F32)).astype(BF16)
        sum_ref[t] = grad
        keep_ref[t + 1], send_ref[t + 1] = split_pairs(dot_tn(h, grad).astype(BF16), groups, my_index)


def qkv_grad_call(place, h, dq, dkv, rkv, groups):
    n, d = h.shape
    width = dq.shape[1]
    rows = d // (2 * groups)
    heads = width // GROUP_WIDTH
    pair = pl.BlockSpec((2, n, GROUP_WIDTH), lambda g, *_: (0, 0, g))
    share = pl.BlockSpec((3, groups, rows, GROUP_WIDTH), lambda g, *_: (g, 0, 0, 0))
    out = jax.ShapeDtypeStruct((3 * heads, groups, rows, GROUP_WIDTH), BF16)
    spec = pltpu.PrefetchScalarGridSpec(
        num_scalar_prefetch=1,
        grid=(heads,),
        in_specs=[resident((n, d)), pl.BlockSpec((n, GROUP_WIDTH), lambda g, *_: (0, g)), pair, pair],
        out_specs=[share, share, pair],
    )
    return pl.pallas_call(
        partial(qkv_grad_kernel, groups),
        grid_spec=spec,
        out_shape=[out, out, jax.ShapeDtypeStruct((2, n, width), BF16)],
        compiler_params=params(40),
        cost_estimate=cost(6 * n * d * width, 6 * d * width + 2 * n * d + 8 * n * width),
        name="qkv_grad",
    )(place, h, dq, dkv, rkv)


def head_back_kernel(weights, count, place, *refs):
    dqs, dkvs = refs[:count], refs[count : 2 * count]
    x_ref, gr_ref, gain_ref = refs[2 * count : 2 * count + 3]
    parts, refs = cut(refs[2 * count + 3 :], weights)
    tg_ref, dln_ref, wq, wk, wv, sem = refs
    load_all(weights, parts, place, (wq, wk, wv), sem)
    i = pl.program_id(0)
    dq = jnp.concatenate([r[...] for r in dqs], axis=1)
    dk = jnp.concatenate([r[0] for r in dkvs], axis=1)
    dv = jnp.concatenate([r[1] for r in dkvs], axis=1)
    grad = dot_nt(dq, wq[...]) + dot_nt(dk, wk[...]) + dot_nt(dv, wv[...])
    hat, scale = normed(x_ref[...].astype(F32))
    tg_ref[...] = (gr_ref[...] + norm_back(grad, gain_ref[...], hat, scale)).astype(BF16)
    dgain = jnp.sum(grad * hat, axis=0, keepdims=True)
    dbias = jnp.sum(grad, axis=0, keepdims=True)

    @pl.when(i == 0)
    def _():
        dln_ref[0:1, :] = dgain
        dln_ref[1:2, :] = dbias

    @pl.when(i > 0)
    def _():
        dln_ref[0:1, :] += dgain
        dln_ref[1:2, :] += dbias


def head_back_call(place, dqs, dkvs, x, gr, weights, gain):
    n, d = x.shape
    row = pl.BlockSpec((ROWS, d), lambda i, *_: (i, 0))
    specs, args = weight_args(weights)
    spec = pltpu.PrefetchScalarGridSpec(
        num_scalar_prefetch=1,
        grid=(n // ROWS,),
        in_specs=[pl.BlockSpec((ROWS, a.shape[1]), lambda i, *_: (i, 0)) for a in dqs]
        + [pl.BlockSpec((2, ROWS, a.shape[2]), lambda i, *_: (0, i, 0)) for a in dkvs]
        + [row, row, resident((1, d))]
        + specs,
        out_specs=[row, pl.BlockSpec((2, d), lambda *_: (0, 0))],
        scratch_shapes=[pltpu.VMEM((d, d), BF16)] * 3 + [pltpu.SemaphoreType.DMA((3,))],
    )
    return pl.pallas_call(
        partial(head_back_kernel, weights, len(dqs)),
        grid_spec=spec,
        out_shape=[jax.ShapeDtypeStruct((n, d), BF16), jax.ShapeDtypeStruct((2, d), F32)],
        compiler_params=params(48),
        cost_estimate=cost(6 * n * d * d, 6 * d * d + 14 * n * d),
        name="qkv_back",
    )(place, *dqs, *dkvs, x, gr, gain, *args)


class Term:
    def __init__(self, array, axes, first=0, count=None):
        self.array, self.axes, self.first = array, axes, first
        self.count = array.shape[0] if count is None else count
        self.whole = first % self.count != 0

    def spec(self, settled, flipped, open_bits, steps_bits):
        def index_map(step, mine):
            at = [0 if self.whole else self.first // self.count]
            for b in self.axes:
                if (flipped >> b) & 1:
                    at.append(1 - mine[b])
                elif b in settled:
                    at.append(mine[b])
                elif b in steps_bits:
                    at.append((step >> (len(steps_bits) - 1 - steps_bits.index(b))) & 1)
                else:
                    at.append(0)
            return (*at, 0, 0)

        lead = self.array.shape[0] if self.whole else self.count
        inner = tuple(2 if b in open_bits and b not in steps_bits else None for b in self.axes)
        return pl.BlockSpec((lead,) + inner + self.array.shape[-2:], index_map)

    def read(self, ref):
        start = self.first if self.whole else 0
        return ref[start : start + self.count].astype(F32)


class Cube:
    def __init__(self, dp, index, order):
        self.bits = dp.bit_length() - 1
        self.dp, self.order = dp, order
        self.mine = ((index >> jnp.arange(self.bits, dtype=jnp.int32)) & 1).astype(jnp.int32)

    def send(self, array, flip):
        return lax.ppermute(array, "dp", [(i, i ^ flip) for i in range(self.dp)])

    def far(self, low=2):
        return [f << low for f in range(1, 1 << (self.bits - low))]

    def terms(self, arrays, first=0, count=None):
        made = []
        for array in arrays:
            lead, _, rows, width = array.shape
            shape = (lead,) + (2,) * self.bits + (rows, width)
            made.append(Term(array.reshape(shape), list(range(self.bits))[::-1], first, count))
        return made

    def add(self, outputs, dtype):
        in_specs, args, plan, out_specs, out_shape = [], [], [], [], []
        for output in outputs:
            lead = 0
            for stream, settled, flipped in output:
                open_bits = [b for b in range(self.bits)[::-1] if b not in settled and not (flipped >> b) & 1]
                steps_bits = open_bits[:STEP_BITS]
                for term in stream:
                    in_specs.append(term.spec(settled, flipped, open_bits, steps_bits))
                    args.append(term.array)
                plan.append((len(out_specs), lead, list(stream)))
                lead += stream[0].count
            outer, inner = len(steps_bits), len(open_bits) - len(steps_bits)

            def out_map(step, mine, outer=outer, inner=inner):
                return (0, *[(step >> (outer - 1 - k)) & 1 for k in range(outer)], *[0] * inner, 0, 0)

            shape = output[0][0][0].array.shape[-2:]
            out_specs.append(pl.BlockSpec((lead,) + (None,) * outer + (2,) * inner + shape, out_map))
            out_shape.append(jax.ShapeDtypeStruct((lead,) + (2,) * (outer + inner) + shape, dtype))

        def kernel(mine, *refs):
            ins, outs = refs[: len(args)], refs[len(args) :]
            at = 0
            for out, first, stream in plan:
                total = stream[0].read(ins[at])
                for k in range(1, len(stream)):
                    total = total + stream[k].read(ins[at + k])
                outs[out][first : first + stream[0].count] = total.astype(dtype)
                at += len(stream)

        spec = pltpu.PrefetchScalarGridSpec(
            num_scalar_prefetch=1, grid=(2**outer,), in_specs=in_specs, out_specs=out_specs
        )
        size = sum(math.prod(o.shape) for o in out_shape)
        call = pl.pallas_call(
            kernel,
            grid_spec=spec,
            out_shape=out_shape,
            compiler_params=params(40),
            cost_estimate=cost(4 * size, 8 * size),
            name="add_terms",
        )
        return self.order.run(call, self.mine, *args)


def merge(arrays, outputs, *awaited):
    d = arrays[0].shape[-1]
    shapes = []
    for output in outputs:
        blocks = sum(arrays[i].shape[0] for i, _, _ in output)
        shapes.append(jax.ShapeDtypeStruct((blocks, output[0][2], d), BF16))

    def kernel(*refs):
        ins, outs = refs[: len(arrays)], refs[len(arrays) + len(awaited) :]
        for out, output in zip(outs, outputs, strict=True):
            at = 0
            for i, first, count in output:
                blocks = ins[i].shape[0]
                out[at : at + blocks] = ins[i][:, first : first + count]
                at += blocks

    whole = pl.BlockSpec(memory_space=pltpu.VMEM)
    size = sum(math.prod(shape.shape) for shape in shapes)
    return pl.pallas_call(
        kernel,
        in_specs=[whole] * len(arrays) + [HBM] * len(awaited),
        out_specs=[whole] * len(outputs),
        out_shape=shapes,
        compiler_params=params(40),
        cost_estimate=cost(size, 4 * size),
        name="merge",
    )(*arrays, *awaited)


class Side:
    def __init__(self, cube, order):
        self.cube, self.order = cube, order

    def hold(self, held, bit):
        self.held = held
        self.got = self.cube.send(held, 1 << bit)

    def parts_of(self):
        last = 1 << self.order[1]
        flips = [0] + self.cube.far()
        flips = flips + [f ^ (1 << self.order[0]) for f in flips]
        moved = [f ^ last for f in flips]
        return [(flips, 0), (moved, 0), (flips, 1), (moved, 1)]

    def index(self, flip):
        first, last = self.order
        return (flip >> 2) + (((flip >> first) & 1) << (self.cube.bits - 2)), (flip >> last) & 1


class Gather:
    def __init__(self, cube, order, exchange, one, two):
        self.cube, self.order, self.exchange = cube, order, exchange
        self.rows = one.shape[0]
        self.local = jnp.concatenate([one, two], axis=0)[None]
        self.sides = (Side(cube, (1, 0)), Side(cube, (0, 1)))

    def far(self):
        local = self.order.after(self.local)
        self.pieces = [local] + [self.cube.send(local, f) for f in self.cube.far()]
        self.order.note(local)

    def near(self, *awaited):
        total = self.local.shape[1]
        outputs = [
            [(i, first, count) for i in range(len(self.pieces))]
            for first, count in ((0, self.rows), (self.rows, total - self.rows))
        ]
        held = self.order.run(lambda first, *rest: merge((first, *rest), outputs, *awaited), *self.pieces)
        for s, array in zip(self.sides, held, strict=True):
            s.hold(array, s.order[0])

    def last(self, *awaited):
        arrays = [a for s in self.sides for a in (s.held, s.got)]
        outputs = [[(i, 0, arrays[i].shape[1]), (i + 1, 0, arrays[i].shape[1])] for i in (0, 2)]
        held = self.order.run(lambda first, *rest: merge((first, *rest), outputs, *awaited), *arrays)
        for s, array in zip(self.sides, held, strict=True):
            s.hold(array, s.order[1])

    def cross(self):
        for s in self.sides:
            s.other = self.exchange(self.order.after(s.held))

    def finish(self):
        for s in self.sides:
            s.rest = self.exchange(self.order.after(s.got))

    def ready(self):
        for s in self.sides:
            s.buffers = [s.held, s.got, s.other, s.rest]
            s.parts = s.parts_of()


class Order:
    def __init__(self):
        self.token = ()

    def after(self, *values):
        if self.token:
            values = lax.optimization_barrier((values, self.token))[0]
        return values if len(values) > 1 else values[0]

    def note(self, *token):
        self.token = token

    def run(self, call, first, *rest):
        out = call(self.after(first), *rest)
        self.note(jax.tree.leaves(out)[0])
        return out


class Scatter:
    def __init__(self, cube, one, two, direct):
        self.cube, self.sides, self.step, self.direct = cube, (one, two), 0, direct
        self.sent, self.last = [], []

    def advance(self):
        step, cube = self.step, self.cube
        if step < 2:
            flips = (1 << step, 1 << (1 - step))
            done = ([], []) if step == 0 else ([0], [1])
            self.sent = cube.add(
                [[(stream, done[s], flips[s]) for stream in self.sides[s]] for s in range(2)], BF16
            )
            self.last = []
            for s in range(2):
                got = cube.send(self.sent[s], flips[s])
                self.last.append(got)
                axes = [b for b in range(cube.bits)[::-1] if b not in done[s] and not (flips[s] >> b) & 1]
                at = 0
                for stream in self.sides[s]:
                    stream.append(Term(got, axes, at, stream[0].count))
                    at += stream[0].count
        else:
            streams = [stream for side in self.sides for stream in side]
            if self.direct:
                done, flips = list(range(cube.bits)), cube.far()
            else:
                done, flips = list(range(step)), [1 << step]
            self.sent = cube.add([[(stream, done, f) for stream in streams] for f in flips], BF16)
            self.last = [cube.send(sent, f) for sent, f in zip(self.sent, flips, strict=True)]
            axes = [] if self.direct else list(range(step + 1, cube.bits))[::-1]
            for got in self.last:
                at = 0
                for stream in streams:
                    stream.append(Term(got, axes, at, stream[0].count))
                    at += stream[0].count
        self.step += 1
        return self

    def finish(self):
        while self.step < (3 if self.direct else self.cube.bits):
            self.advance()
        done = list(range(self.cube.bits))
        return self.cube.add([[(stream, done, 0)] for side in self.sides for stream in side], F32)


def gate(value, *others):
    return lax.optimization_barrier((value, others))[0]


def block_table(seg_full, seg_local, my_index, bq, bk):
    first, last = seg_local[::bq], seg_local[bq - 1 :: bq]
    low = jnp.sum((seg_full[None, :] < first[:, None]).astype(jnp.int32), axis=1)
    high = jnp.sum((seg_full[None, :] <= last[:, None]).astype(jnp.int32), axis=1)
    start = low // ROW_ALIGN * ROW_ALIGN
    table = jnp.stack([start, (high - start + bk - 1) // bk], axis=1).reshape(-1)
    return jnp.concatenate([table, my_index[None]]).astype(jnp.int32)


def body(
    tokens,
    segments,
    ln1_gain,
    ln1_bias,
    w_query,
    w_key,
    w_value,
    w_out,
    ln2_gain,
    ln2_bias,
    w_up,
    w_down,
    cotangent,
):
    x = tokens[0]
    n, d = x.shape
    cot = cotangent[0]
    rows = w_query.shape[0]
    devices = d // rows
    hidden = w_up.shape[1]
    per_device = hidden // devices
    my_index = lax.axis_index("seq")
    seg_full = segments[0]
    seg_local = lax.dynamic_slice_in_dim(seg_full, my_index * n, n)
    tab = block_table(seg_full, seg_local, my_index, ATT_Q, ATT_K)
    seg_q = seg_local.reshape(n // ATT_Q, 1, ATT_Q)
    seg_col = jnp.pad(seg_full, (0, ATT_K), constant_values=-1)[:, None]

    dp = devices // 2
    dp_index = lax.axis_index("dp")
    order = Order()
    cube = Cube(dp, dp_index, order)
    place = jnp.stack([dp_index, my_index]).astype(jnp.int32)
    swap = [(0, 1), (1, 0)]
    tiles = hidden // d

    def exchange(value):
        return lax.ppermute(value, "seq", swap)

    def halves(value, axis):
        keep = lax.dynamic_index_in_dim(value, my_index, axis, keepdims=False)
        send = lax.dynamic_index_in_dim(value, 1 - my_index, axis, keepdims=False)
        return keep, send

    vectors = jnp.concatenate([ln1_gain, ln1_bias, ln2_gain, ln2_bias]).astype(F32)
    vectors = jnp.broadcast_to(vectors[None], (devices, 4 * rows))
    vectors = lax.all_to_all(vectors, BOTH, 0, 0, tiled=True)
    ln = vectors.reshape(devices, 4, rows).transpose(1, 0, 2).reshape(4, 1, d)

    aligned = rows % 32 == 0
    groups = d // GROUP_WIDTH
    if aligned:
        cut_row, half_down = rows // 2, per_device // 2
        up_tiles = w_up.reshape(rows, tiles, d).transpose(1, 0, 2)
        half_up = tiles // 2 * rows
        low_up, high_up = (u.reshape(half_up, d) for u in (up_tiles[: tiles // 2], up_tiles[tiles // 2 :]))
        head = Gather(
            cube, order, exchange,
            jnp.concatenate([w_key, w_query[:cut_row]]), jnp.concatenate([w_value, w_query[cut_row:]]),
        )
        low = Gather(
            cube, order, exchange,
            jnp.concatenate([low_up, w_out[:cut_row]]), jnp.concatenate([w_down[:half_down], w_out[cut_row:]]),
        )
        high = Gather(cube, order, exchange, high_up, w_down[half_down:])
        head.far()
        head.near(vectors)
        low.far()
        head.last()
        head.cross()
        order.note(*[side.got for side in head.sides])
        head.finish()
        head.ready()
        key_w = Spread(rows, [(head.sides[0], 0, rows, 0)])
        value_w = Spread(rows, [(head.sides[1], 0, rows, 0)])
        query_w = Spread(rows, [(head.sides[0], rows, cut_row, 0), (head.sides[1], rows, cut_row, cut_row)])
    else:
        every = jnp.concatenate([w_query, w_key, w_value, w_out], axis=0).reshape(4, rows, d)
        every = lax.all_gather(every, BOTH, axis=1, tiled=True)
        query_w, key_w, value_w, out_w = (Plain(every[t], rows) for t in range(4))
        up_all = lax.all_gather(w_up, BOTH, axis=0, tiled=True)
        ups = [Plain(up_all[:, t * d : (t + 1) * d], rows) for t in range(tiles)]
        downs = [Plain(lax.all_gather(w_down, BOTH, axis=0, tiled=True), per_device)]

    h1, own = order.run(kv_call, place, x, ln[0], ln[1], [key_w, value_w])
    if aligned:
        low.near()
    other = exchange(order.after(own))
    q = order.run(q_call, place, h1, [query_w])
    if aligned:
        low.last()
        high.far()
    outs, lses = [], []
    plan = [(0, 2), (2, 1), (3, 1)] if groups == 4 else [(g, 1) for g in range(groups)]
    for i, (start, count) in enumerate(plan):
        if aligned and i == 1:
            high.near()
            low.finish()
        if aligned and i == 2:
            high.last(*[side.rest for side in low.sides])
            low.cross()
        out, lse = order.run(
            attend_call, tab, q, own, other, seg_q, seg_col, ATT_Q, ATT_K, start, count
        )
        outs.append(out)
        lses.append(lse)
    if aligned:
        low.ready()
        high.cross()
        out_w = Spread(
            rows, [(low.sides[0], half_up, cut_row, 0), (low.sides[1], half_down, cut_row, cut_row)]
        )
    mid, h2 = order.run(mid_call, place, x, outs, [out_w], ln[2], ln[3])
    if aligned:
        high.finish()
        high.ready()

    up_rows = tiles * rows
    if aligned:
        ups = [
            Spread(rows, [((low, high)[t // (tiles // 2)].sides[0], t % (tiles // 2) * rows, rows, 0)])
            for t in range(tiles)
        ]
        downs = [Spread(half_down, [(r.sides[1], 0, half_down, 0)]) for r in (low, high)]
        per_tile = d // FF_COLS
        group = FF_COLS // per_device
        up_out = (
            pl.BlockSpec((None, dp, rows, FF_COLS), lambda j, *_: (j // per_tile, 0, 0, j % per_tile)),
            jax.ShapeDtypeStruct((tiles, dp, rows, d), BF16),
        )
        down_out = (
            pl.BlockSpec((tiles, group // 2, rows, d), lambda j, *_: (0, j, 0, 0)),
            jax.ShapeDtypeStruct((tiles, dp, rows, d), BF16),
        )
        grad_specs = [up_out, up_out, down_out, down_out]
    else:
        grad_specs = [
            (pl.BlockSpec((d, FF_COLS), lambda j, *_: (0, j)), jax.ShapeDtypeStruct((d, hidden), BF16)),
            (pl.BlockSpec((FF_COLS, d), lambda j, *_: (j, 0)), jax.ShapeDtypeStruct((hidden, d), BF16)),
        ]
    mixed, gmid, *grads = order.run(ffn_call, place, h2, cot, ups, downs, mid, grad_specs, hidden, aligned)
    if not aligned:
        dwu = grads[0].reshape(dp, 2, rows, tiles, d).transpose(3, 0, 1, 2, 4)
        dwd = grads[1].reshape(dp, 2, tiles, rows, d).transpose(2, 0, 1, 3, 4)
        grads = [*halves(dwu, 2), *halves(dwd, 2)]
    keep_up, send_up, keep_down, send_down = grads
    got_up, got_down = exchange(send_up), exchange(send_down)
    big = Scatter(cube, [cube.terms([keep_up, got_up])], [cube.terms([keep_down, got_down])], False)

    grad_mid, grad_att, keep_out, send_out, dln2 = order.run(
        mid_back_call, place, gmid, mid, cot, outs, [out_w], ln[2], dp
    )
    big.advance()
    got_out = exchange(order.after(send_out))
    dqs, dkvs = [], []

    def attend_back(g):
        which = [i for i, (start, _) in enumerate(plan) if start <= g][-1]
        return order.run(
            attend_back_call, tab, q, grad_att, outs[which], own, other, seg_q, seg_col,
            lses[which], ATT_Q, ATT_K, g, 1, g - plan[which][0],
        )

    def finish_group(dq, dkv, got):
        keep, send, dkv = order.run(qkv_grad_call, place, h1, dq, dkv, got, dp)
        dqs.append(dq)
        dkvs.append(dkv)
        return keep, send

    dq_0, dkv_0, sent_0 = attend_back(0)
    dq_1, dkv_1, sent_1 = attend_back(1)
    got_0 = exchange(order.after(sent_0))
    big.advance()
    got_1 = exchange(order.after(sent_1))
    keep_0, send_0 = finish_group(dq_0, dkv_0, got_0)
    keep_1, send_1 = finish_group(dq_1, dkv_1, got_1)
    terms_0, terms_1 = [keep_0, exchange(order.after(send_0))], [keep_1, exchange(order.after(send_1))]
    dq_2, dkv_2, sent_2 = attend_back(2)
    big.advance()
    tail_one = Scatter(
        cube,
        [cube.terms(terms_0), cube.terms([keep_out, got_out], 0, 2)],
        [cube.terms(terms_1), cube.terms([keep_out, got_out], 2, 2)],
        False,
    )
    tail_one.advance()
    got_2 = exchange(order.after(sent_2))
    dq_3, dkv_3, sent_3 = attend_back(3)
    big.advance()
    tail_one.advance()
    got_3 = exchange(order.after(sent_3))
    keep_2, send_2 = finish_group(dq_2, dkv_2, got_2)
    keep_3, send_3 = finish_group(dq_3, dkv_3, got_3)
    tail_one.advance()
    terms_2, terms_3 = [keep_2, exchange(order.after(send_2))], [keep_3, exchange(order.after(send_3))]
    tail_two = Scatter(cube, [cube.terms(terms_2)], [cube.terms(terms_3)], True)
    tail_two.advance()
    token_grad, dln1 = order.run(
        head_back_call, place, dqs, dkvs, x, grad_mid, [query_w, key_w, value_w], ln[0]
    )
    tail_two.advance()
    tail_one.advance()
    up_share, down_share = big.finish()
    dln = jnp.concatenate([dln1, order.after(dln2)], axis=0).reshape(4, devices, rows).transpose(1, 0, 2)
    dln = lax.all_to_all(dln.reshape(devices, 4 * rows), BOTH, 0, 0, tiled=True)
    dln = jnp.sum(dln.reshape(devices, 4, rows), axis=0)
    tail_two.advance()
    one_a, out_a, one_b, out_b = tail_one.finish()
    two_a, two_b = tail_two.finish()

    up_share = up_share.transpose(1, 0, 2).reshape(rows, hidden)
    down_share = down_share.reshape(per_device, d)
    qkv_share = jnp.concatenate([one_a, one_b, two_a, two_b], axis=-1)
    out_share = jnp.concatenate([out_a, out_b], axis=0).transpose(1, 0, 2).reshape(rows, d)
    return (
        mixed[None],
        token_grad[None],
        dln[0],
        dln[1],
        qkv_share[0],
        qkv_share[1],
        qkv_share[2],
        out_share,
        dln[2],
        dln[3],
        up_share,
        down_share,
    )


def solution(mesh):
    row, act, vec = P(BOTH, None), P("dp", "seq", None), P(BOTH)
    in_specs = (act, P("dp", None), vec, vec, row, row, row, row, vec, vec, row, row, act)
    out_specs = (act, act, vec, vec, row, row, row, row, vec, vec, row, row)
    return jax.shard_map(body, mesh=mesh, in_specs=in_specs, out_specs=out_specs, check_vma=False)
```

```python
import math
from functools import partial

import jax
import jax.numpy as jnp
from jax import lax
from jax.experimental import pallas as pl
from jax.experimental.pallas import tpu as pltpu
from jax.sharding import PartitionSpec as P

BF16 = jnp.bfloat16
F32 = jnp.float32
HEAD_DIM = 64
GROUP = 4
GROUP_WIDTH = GROUP * HEAD_DIM
NEG = -1000000000.0
BOTH = ("dp", "seq")
ATT_Q = 256
ATT_K = 512
ROW_ALIGN = 16
ROWS = 256
FF_COLS = 512
COST_SCALE = 100000
STEP_BITS = 1


def dot_nn(left, right):
    return lax.dot_general(left, right, (((1,), (0,)), ((), ())), preferred_element_type=F32)


def dot_nt(left, right):
    return lax.dot_general(left, right, (((1,), (1,)), ((), ())), preferred_element_type=F32)


def dot_tn(left, right):
    return lax.dot_general(left, right, (((0,), (0,)), ((), ())), preferred_element_type=F32)


def params(mib):
    return pltpu.CompilerParams(vmem_limit_bytes=mib << 20)


def cost(flops, nbytes, scale=None):
    if scale:
        return pl.CostEstimate(flops=scale * flops, bytes_accessed=scale * nbytes, transcendentals=0)
    return pl.CostEstimate(flops=flops // COST_SCALE, bytes_accessed=nbytes // COST_SCALE, transcendentals=0)


def normed(values):
    centre = values - jnp.mean(values, axis=-1, keepdims=True)
    scale = lax.rsqrt(jnp.mean(centre * centre, axis=-1, keepdims=True) + 1e-05)
    return centre * scale, scale


def norm_back(grad, gain_vec, hat, scale):
    inner = grad * gain_vec
    return scale * (
        inner
        - jnp.mean(inner, axis=-1, keepdims=True)
        - hat * jnp.mean(inner * hat, axis=-1, keepdims=True)
    )


def flat(ref):
    value = ref[...]
    return value.reshape(-1, value.shape[-1])


def resident(shape):
    zeros = (0,) * len(shape)
    return pl.BlockSpec(shape, lambda *_: zeros, pipeline_mode=pl.Buffered(1))


class Spread:
    def __init__(self, block, pieces):
        self.block, self.pieces = block, pieces
        self.args = [b for rounds, *_ in pieces for b in rounds.buffers]

    def start(self, refs, place, target, sem, columns=None):
        for i, (rounds, first, count, at) in enumerate(self.pieces):
            for ref, (flips, core) in zip(refs[4 * i : 4 * i + 4], rounds.parts, strict=True):
                for e, flip in enumerate(flips):
                    device = (place[0] ^ flip) * 2 + (place[1] ^ core)
                    row = pl.multiple_of(device * self.block + at, count)
                    source = ref.at[e, pl.ds(first, count)]
                    if columns is not None:
                        source = ref.at[e, pl.ds(first, count), columns]
                    pltpu.make_async_copy(source, target.at[pl.ds(row, count), :], sem).start()

    def start_rows(self, refs, place, target, sem, first, group):
        ((rounds, begin, count, _),) = self.pieces
        for k in range(group):
            device = first + k
            flip = (device // 2) ^ place[0]
            at, last = rounds.index(flip)
            core = (device % 2) ^ place[1]
            for i, ref in enumerate(refs):

                @pl.when((last == i % 2) & (core == i // 2))
                def _(ref=ref, at=at, k=k):
                    pltpu.make_async_copy(
                        ref.at[at, pl.ds(begin, count)], target.at[pl.ds(k * count, count), :], sem
                    ).start()


class Plain:
    def __init__(self, array, block):
        self.args, self.block = [array], block

    def start(self, refs, place, target, sem, columns=None):
        source = refs[0] if columns is None else refs[0].at[:, columns]
        pltpu.make_async_copy(source, target, sem).start()

    def start_rows(self, refs, place, target, sem, first, group):
        pltpu.make_async_copy(refs[0].at[pl.ds(first * self.block, group * self.block), :], target, sem).start()


def arrived(target, sem):
    pltpu.make_async_copy(target, target, sem).wait()


def cut(refs, weights):
    parts = []
    for weight in weights:
        parts.append(refs[: len(weight.args)])
        refs = refs[len(weight.args) :]
    return parts, refs


def load_all(weights, parts, place, targets, sem, wait=True):
    @pl.when(pl.program_id(0) == 0)
    def _():
        for i, weight in enumerate(weights):
            weight.start(parts[i], place, targets[i], sem.at[i])
        if wait:
            for i in range(len(weights)):
                arrived(targets[i], sem.at[i])


def loaded(targets, sem, i):
    @pl.when(pl.program_id(0) == 0)
    def _():
        arrived(targets[i], sem.at[i])

    return targets[i][...]


HBM = pl.BlockSpec(memory_space=pltpu.HBM)


def weight_args(weights):
    args = [a for w in weights for a in w.args]
    return [HBM] * len(args), args


def kv_kernel(weights, place, x_ref, gain_ref, bias_ref, *refs):
    parts, refs = cut(refs, weights)
    h_ref, kv_ref, wk, wv, sem = refs
    load_all(weights, parts, place, (wk, wv), sem)
    hat, _ = normed(x_ref[...].astype(F32))
    low = (hat * gain_ref[...] + bias_ref[...]).astype(BF16)
    h_ref[...] = low
    kv_ref[0] = dot_nn(low, wk[...]).astype(BF16)
    kv_ref[1] = dot_nn(low, wv[...]).astype(BF16)


def kv_call(place, x, gain, bias, weights):
    n, d = x.shape
    row = pl.BlockSpec((ROWS, d), lambda i, *_: (i, 0))
    specs, args = weight_args(weights)
    spec = pltpu.PrefetchScalarGridSpec(
        num_scalar_prefetch=1,
        grid=(n // ROWS,),
        in_specs=[row, resident((1, d)), resident((1, d))] + specs,
        out_specs=[row, pl.BlockSpec((2, ROWS, d), lambda i, *_: (0, i, 0))],
        scratch_shapes=[pltpu.VMEM((d, d), BF16)] * 2 + [pltpu.SemaphoreType.DMA((2,))],
    )
    return pl.pallas_call(
        partial(kv_kernel, weights),
        grid_spec=spec,
        out_shape=[jax.ShapeDtypeStruct((n, d), BF16), jax.ShapeDtypeStruct((2, n, d), BF16)],
        compiler_params=params(40),
        cost_estimate=cost(4 * n * d * d, 4 * d * d + 8 * n * d),
        name="kv_proj",
    )(place, x, gain, bias, *args)


def q_kernel(weights, place, h_ref, *refs):
    parts, refs = cut(refs, weights)
    q_ref, wq, sem = refs
    load_all(weights, parts, place, (wq,), sem)
    q_ref[...] = (dot_nn(h_ref[...], wq[...]).astype(BF16).astype(F32) * 0.125).astype(BF16)


def q_call(place, h, weights):
    n, d = h.shape
    row = pl.BlockSpec((ROWS, d), lambda i, *_: (i, 0))
    specs, args = weight_args(weights)
    spec = pltpu.PrefetchScalarGridSpec(
        num_scalar_prefetch=1,
        grid=(n // ROWS,),
        in_specs=[row] + specs,
        out_specs=row,
        scratch_shapes=[pltpu.VMEM((d, d), BF16), pltpu.SemaphoreType.DMA((1,))],
    )
    return pl.pallas_call(
        partial(q_kernel, weights),
        grid_spec=spec,
        out_shape=jax.ShapeDtypeStruct((n, d), BF16),
        compiler_params=params(32),
        cost_estimate=cost(2 * n * d * d, 2 * d * d + 4 * n * d),
        name="q_proj",
    )(place, h, *args)


def stack_heads(block):
    lane = lax.broadcasted_iota(jnp.int32, block.shape, 1) // HEAD_DIM
    zero = jnp.zeros_like(block)
    return jnp.concatenate([jnp.where(lane == h, block, zero) for h in range(GROUP)], axis=0)


def head_cols(value, h, width):
    return value[:, h * width : (h + 1) * width]


def head_rows(value, h):
    return value[h * HEAD_DIM : (h + 1) * HEAD_DIM, :]


def line_up(target, own_ref, other_ref, which, mine):
    n = own_ref.shape[1]
    target[pl.ds(pl.multiple_of(mine * n, n), n), :] = own_ref[which]
    target[pl.ds(pl.multiple_of((1 - mine) * n, n), n), :] = other_ref[which]
    target[2 * n :, :] = jnp.zeros((target.shape[0] - 2 * n, target.shape[1]), target.dtype)


def attend_kernel(bq, bk, tab, q_ref, own_ref, other_ref, sq_ref, s_ref, o_ref, lse_ref, k_s, v_s):
    i = pl.program_id(1)

    @pl.when(i == 0)
    def _():
        mine = tab[2 * pl.num_programs(1)]
        line_up(k_s, own_ref, other_ref, 0, mine)
        line_up(v_s, own_ref, other_ref, 1, mine)

    stacked = stack_heads(q_ref[...])
    seg_q = jnp.concatenate([sq_ref[0]] * GROUP, axis=1)
    first = tab[2 * i]

    def step(j, carry):
        top, total, acc = carry
        at = pl.multiple_of(first + j * bk, ROW_ALIGN)
        scores = dot_nt(k_s[pl.ds(at, bk), :], stacked)
        scores = jnp.where(s_ref[pl.ds(at, bk), :] == seg_q, scores, NEG)
        new_top = jnp.maximum(top, jnp.max(scores, axis=0, keepdims=True))
        decay = jnp.exp(top - new_top)
        probs = jnp.exp(scores - new_top)
        total = total * decay + jnp.sum(probs, axis=0, keepdims=True)
        low = probs.astype(BF16)
        values = v_s[pl.ds(at, bk), :].T
        acc = tuple(
            acc[h] * head_cols(decay, h, bq) + dot_nn(head_rows(values, h), head_cols(low, h, bq))
            for h in range(GROUP)
        )
        return new_top, total, acc

    state = (
        jnp.full((1, GROUP * bq), -jnp.inf, F32),
        jnp.zeros((1, GROUP * bq), F32),
        tuple(jnp.zeros((HEAD_DIM, bq), F32) for _ in range(GROUP)),
    )
    top, total, acc = lax.fori_loop(0, tab[2 * i + 1], step, state)
    out = jnp.concatenate([acc[h] / head_cols(total, h, bq) for h in range(GROUP)], axis=0)
    o_ref[...] = out.T.astype(BF16)
    lse_ref[0, 0] = top + jnp.log(total)


def attend_specs(n, bq, padded, first):
    def half(_):
        return pl.BlockSpec((2, n, GROUP_WIDTH), lambda g, i, *_: (0, 0, g + first))

    return [
        half(0),
        half(1),
        pl.BlockSpec((1, 1, bq), lambda g, i, *_: (i, 0, 0)),
        pl.BlockSpec((padded, 1), lambda *_: (0, 0)),
    ]


def attend_call(tab, q, own, other, seg_q, seg_col, bq, bk, first, groups):
    n, d = q.shape
    blocks = n // bq
    padded = seg_col.shape[0]
    spec = pltpu.PrefetchScalarGridSpec(
        num_scalar_prefetch=1,
        grid=(groups, blocks),
        in_specs=[pl.BlockSpec((bq, GROUP_WIDTH), lambda g, i, *_: (i, g + first))]
        + attend_specs(n, bq, padded, first),
        out_specs=[
            pl.BlockSpec((bq, GROUP_WIDTH), lambda g, i, *_: (i, g)),
            pl.BlockSpec((1, 1, 1, GROUP * bq), lambda g, i, *_: (g, i, 0, 0)),
        ],
        scratch_shapes=[pltpu.VMEM((padded, GROUP_WIDTH), BF16)] * 2,
    )
    return pl.pallas_call(
        partial(attend_kernel, bq, bk),
        grid_spec=spec,
        out_shape=[
            jax.ShapeDtypeStruct((n, groups * GROUP_WIDTH), BF16),
            jax.ShapeDtypeStruct((groups, blocks, 1, GROUP * bq), F32),
        ],
        compiler_params=params(56),
        cost_estimate=cost(8_000_000_000 * groups, 3 * groups * n * d),
        name="attend",
    )(tab, q, own, other, seg_q, seg_col)


def attend_back_kernel(
    bq, bk, tab, q_ref, go_ref, o_ref, lse_ref, own_ref, other_ref, sq_ref, s_ref,
    dq_ref, down_ref, dpart_ref, k_s, v_s, dk_s, dv_s,
):
    i = pl.program_id(1)
    mine = tab[2 * pl.num_programs(1)]

    @pl.when(i == 0)
    def _():
        line_up(k_s, own_ref, other_ref, 0, mine)
        line_up(v_s, own_ref, other_ref, 1, mine)
        dk_s[...] = jnp.zeros_like(dk_s)
        dv_s[...] = jnp.zeros_like(dv_s)

    stacked = stack_heads(q_ref[...])
    grad = go_ref[...]
    stacked_grad = stack_heads(grad)
    product = (grad.astype(F32) * o_ref[...].astype(F32)).T
    inner = jnp.concatenate(
        [jnp.sum(head_rows(product, h), axis=0, keepdims=True) for h in range(GROUP)], axis=1
    )
    seg_q = jnp.concatenate([sq_ref[0]] * GROUP, axis=1)
    lse = lse_ref[0, 0]
    first = tab[2 * i]

    def step(j, acc):
        at = pl.multiple_of(first + j * bk, ROW_ALIGN)
        keys = k_s[pl.ds(at, bk), :]
        scores = dot_nt(keys, stacked)
        scores = jnp.where(s_ref[pl.ds(at, bk), :] == seg_q, scores, NEG)
        probs = jnp.exp(scores - lse)
        grad_probs = dot_nt(v_s[pl.ds(at, bk), :], stacked_grad)
        grad_scores = (probs * (grad_probs - inner)).astype(BF16)
        dv_s[pl.ds(at, bk), :] += dot_nn(probs.astype(BF16), stacked_grad)
        dk_s[pl.ds(at, bk), :] += dot_nn(grad_scores, stacked)
        keys_t = keys.T
        return tuple(
            acc[h] + dot_nn(head_rows(keys_t, h), head_cols(grad_scores, h, bq)) for h in range(GROUP)
        )

    state = tuple(jnp.zeros((HEAD_DIM, bq), F32) for _ in range(GROUP))
    state = lax.fori_loop(0, tab[2 * i + 1], step, state)
    dq_ref[...] = (jnp.concatenate(state, axis=0).T * 0.125).astype(BF16)

    @pl.when(i == pl.num_programs(1) - 1)
    def _():
        n = down_ref.shape[1]
        for ref, half in ((down_ref, mine), (dpart_ref, 1 - mine)):
            rows = pl.ds(pl.multiple_of(half * n, n), n)
            ref[0] = dk_s[rows, :].astype(BF16)
            ref[1] = dv_s[rows, :].astype(BF16)


def attend_back_call(tab, q, grad, out, own, other, seg_q, seg_col, lse, bq, bk, first, groups, out_first):
    n, d = q.shape
    blocks = n // bq
    padded = seg_col.shape[0]
    query = pl.BlockSpec((bq, GROUP_WIDTH), lambda g, i, *_: (i, g + first))
    pair = pl.BlockSpec((2, n, GROUP_WIDTH), lambda g, i, *_: (0, 0, g))
    spec = pltpu.PrefetchScalarGridSpec(
        num_scalar_prefetch=1,
        grid=(groups, blocks),
        in_specs=[
            query,
            query,
            pl.BlockSpec((bq, GROUP_WIDTH), lambda g, i, *_: (i, g + out_first)),
            pl.BlockSpec((1, 1, 1, GROUP * bq), lambda g, i, *_: (g + out_first, i, 0, 0)),
        ]
        + attend_specs(n, bq, padded, first),
        out_specs=[pl.BlockSpec((bq, GROUP_WIDTH), lambda g, i, *_: (i, g)), pair, pair],
        scratch_shapes=[pltpu.VMEM((padded, GROUP_WIDTH), BF16)] * 2
        + [pltpu.VMEM((padded, GROUP_WIDTH), F32)] * 2,
    )
    width = groups * GROUP_WIDTH
    return pl.pallas_call(
        partial(attend_back_kernel, bq, bk),
        grid_spec=spec,
        out_shape=[
            jax.ShapeDtypeStruct((n, width), BF16),
            jax.ShapeDtypeStruct((2, n, width), BF16),
            jax.ShapeDtypeStruct((2, n, width), BF16),
        ],
        compiler_params=params(56),
        cost_estimate=cost(12_000_000_000 * groups, 6 * groups * n * d),
        name="attend_back",
    )(tab, q, grad, out, lse, own, other, seg_q, seg_col)


def mid_kernel(weights, count, place, x_ref, gain_ref, bias_ref, *refs):
    outs, refs = refs[:count], refs[count:]
    parts, refs = cut(refs, weights)
    r_ref, h_ref, wo, sem = refs
    load_all(weights, parts, place, (wo,), sem)
    mid = x_ref[...].astype(F32) + dot_nn(jnp.concatenate([o[...] for o in outs], axis=1), wo[...])
    r_ref[...] = mid
    hat, _ = normed(mid)
    h_ref[...] = (hat * gain_ref[...] + bias_ref[...]).astype(BF16)


def mid_call(place, x, outs, weights, gain, bias):
    n, d = x.shape
    row = pl.BlockSpec((ROWS, d), lambda i, *_: (i, 0))
    specs, args = weight_args(weights)
    spec = pltpu.PrefetchScalarGridSpec(
        num_scalar_prefetch=1,
        grid=(n // ROWS,),
        in_specs=[row, resident((1, d)), resident((1, d))]
        + [pl.BlockSpec((ROWS, o.shape[1]), lambda i, *_: (i, 0)) for o in outs]
        + specs,
        out_specs=[row, row],
        scratch_shapes=[pltpu.VMEM((d, d), BF16), pltpu.SemaphoreType.DMA((1,))],
    )
    return pl.pallas_call(
        partial(mid_kernel, weights, len(outs)),
        grid_spec=spec,
        out_shape=[jax.ShapeDtypeStruct((n, d), F32), jax.ShapeDtypeStruct((n, d), BF16)],
        compiler_params=params(32),
        cost_estimate=cost(2 * n * d * d, 2 * d * d + 10 * n * d),
        name="out_proj",
    )(place, x, gain, bias, *outs, *args)


def mid_back_kernel(weights, count, place, gh_ref, r_ref, g_ref, gain_ref, *refs):
    outs, refs = refs[:count], refs[count:]
    parts, refs = cut(refs, weights)
    gr_ref, go_ref, keep_ref, send_ref, dln_ref, acc, wo, sem = refs
    load_all(weights, parts, place, (wo,), sem, wait=False)
    i = pl.program_id(0)
    hat, scale = normed(r_ref[...])
    grad = gh_ref[...]
    total = g_ref[...].astype(F32) + norm_back(grad, gain_ref[...], hat, scale)
    gr_ref[...] = total
    low = total.astype(BF16)
    part = dot_tn(jnp.concatenate([o[...] for o in outs], axis=1), low)
    go_ref[...] = dot_nt(low, loaded((wo,), sem, 0)).astype(BF16)
    dgain = jnp.sum(grad * hat, axis=0, keepdims=True)
    dbias = jnp.sum(grad, axis=0, keepdims=True)

    @pl.when(i == 0)
    def _():
        acc[...] = part
        dln_ref[0:1, :] = dgain
        dln_ref[1:2, :] = dbias

    @pl.when(i > 0)
    def _():
        acc[...] += part
        dln_ref[0:1, :] += dgain
        dln_ref[1:2, :] += dbias

    @pl.when(i == pl.num_programs(0) - 1)
    def _():
        lanes = keep_ref.shape[3]
        for ref, value in zip(
            (keep_ref, send_ref), split_pairs(acc[...].astype(BF16), keep_ref.shape[1], place[1]), strict=True
        ):
            for t in range(ref.shape[0]):
                ref[t] = value[:, :, t * lanes : (t + 1) * lanes]


def mid_back_call(place, grad, mid, cot, outs, weights, gain, groups):
    n, d = mid.shape
    row = pl.BlockSpec((ROWS, d), lambda i, *_: (i, 0))
    share = (d // GROUP_WIDTH, groups, d // (2 * groups), GROUP_WIDTH)
    specs, args = weight_args(weights)
    spec = pltpu.PrefetchScalarGridSpec(
        num_scalar_prefetch=1,
        grid=(n // ROWS,),
        in_specs=[row, row, row, resident((1, d))]
        + [pl.BlockSpec((ROWS, o.shape[1]), lambda i, *_: (i, 0)) for o in outs]
        + specs,
        out_specs=[
            row,
            row,
            pl.BlockSpec(share, lambda *_: (0, 0, 0, 0)),
            pl.BlockSpec(share, lambda *_: (0, 0, 0, 0)),
            pl.BlockSpec((2, d), lambda *_: (0, 0)),
        ],
        scratch_shapes=[
            pltpu.VMEM((d, d), F32),
            pltpu.VMEM((d, d), BF16),
            pltpu.SemaphoreType.DMA((1,)),
        ],
    )
    return pl.pallas_call(
        partial(mid_back_kernel, weights, len(outs)),
        grid_spec=spec,
        out_shape=[
            jax.ShapeDtypeStruct((n, d), F32),
            jax.ShapeDtypeStruct((n, d), BF16),
            jax.ShapeDtypeStruct(share, BF16),
            jax.ShapeDtypeStruct(share, BF16),
            jax.ShapeDtypeStruct((2, d), F32),
        ],
        compiler_params=params(48),
        cost_estimate=cost(4 * n * d * d, 4 * d * d + 18 * n * d),
        name="out_proj_back",
    )(place, grad, mid, cot, gain, *outs, *args)


def split_pairs(value, groups, my_index):
    rows = value.shape[0] // (2 * groups)
    pairs = value.reshape(groups, 2, rows, value.shape[1])
    even, odd = pairs[:, 0], pairs[:, 1]
    first = my_index == 0
    return jnp.where(first, even, odd), jnp.where(first, odd, even)


def ffn_grads(h, grad, wu, wd):
    up = dot_nn(h, wu)
    cdf = 0.5 * (1.0 + lax.erf(up * 0.7071067811865476))
    act = (up * cdf).astype(BF16)
    slope = cdf + up * (jnp.exp(-0.5 * up * up) * 0.3989422804014327)
    gu = (dot_nt(grad, wd) * slope).astype(BF16)
    return act, gu, dot_tn(h, gu).astype(BF16), dot_tn(act, grad).astype(BF16)


def ffn_sums(j, act, gu, wu, wd, mid_ref, mixed_ref, gh_ref, acc):
    @pl.when(j == 0)
    def _():
        acc[...] = mid_ref[...] + dot_nn(act, wd)
        gh_ref[...] = dot_nt(gu, wu)

    @pl.when(j > 0)
    def _():
        acc[...] += dot_nn(act, wd)
        gh_ref[...] += dot_nt(gu, wu)

    @pl.when(j == pl.num_programs(0) - 1)
    def _():
        mixed_ref[...] = acc[...].astype(BF16)


def ffn_kernel(ups, downs, aligned, place, h_ref, g_ref, mid_ref, *refs):
    parts, refs = cut(refs, ups + downs)
    mixed_ref, gh_ref = refs[:2]
    grads = refs[2:6] if aligned else refs[2:4]
    wu_s, wd_s, acc, sem = refs[-4:]
    j, steps = pl.program_id(0), pl.num_programs(0)
    per_tile = h_ref.shape[1] // FF_COLS
    group = FF_COLS // sum(w.block for w in downs)

    def fetch(step, slot):
        column = pl.ds(pl.multiple_of((step % per_tile) * FF_COLS, FF_COLS), FF_COLS)
        for t, up in enumerate(ups):

            @pl.when(step // per_tile == t)
            def _(t=t, up=up):
                up.start(parts[t], place, wu_s.at[slot], sem.at[slot, 0], column)

        at = 0
        for i, down in enumerate(downs):
            count = group * down.block
            down.start_rows(
                parts[len(ups) + i], place, wd_s.at[slot, pl.ds(at, count), :], sem.at[slot, 1], step * group, group
            )
            at += count

    @pl.when(j == 0)
    def _():
        fetch(j, 0)

    @pl.when(j + 1 < steps)
    def _():
        fetch(j + 1, (j + 1) % 2)

    slot = j % 2
    arrived(wu_s.at[slot], sem.at[slot, 0])
    arrived(wd_s.at[slot], sem.at[slot, 1])
    wu, wd = wu_s[slot], wd_s[slot]
    if len(downs) > 1:
        width = wd.shape[1]
        stack, at = [], 0
        for down in downs:
            count = group * down.block
            stack.append(wd[at : at + count].reshape(group, down.block, width))
            at += count
        wd = jnp.concatenate(stack, axis=1).reshape(FF_COLS, width)
    act, gu, dwu, dwd = ffn_grads(h_ref[...], g_ref[...], wu, wd)
    if aligned:
        grads[0][...], grads[1][...] = split_pairs(dwu, grads[0].shape[0], place[1])
        for ref, value in zip(grads[2:], split_pairs(dwd, grads[2].shape[1], place[1]), strict=True):
            for t in range(ref.shape[0]):
                ref[t] = value[:, t * ref.shape[2] : (t + 1) * ref.shape[2]]
    else:
        grads[0][...] = dwu
        grads[1][...] = dwd
    ffn_sums(j, act, gu, wu, wd, mid_ref, mixed_ref, gh_ref, acc)


def ffn_call(place, h, cot, ups, downs, mid, grad_specs, hidden, aligned):
    n, d = h.shape
    full = resident((n, d))
    const = pl.BlockSpec((n, d), lambda j, *_: (0, 0))
    specs, args = weight_args(ups + downs)
    spec = pltpu.PrefetchScalarGridSpec(
        num_scalar_prefetch=1,
        grid=(hidden // FF_COLS,),
        in_specs=[full, full, full] + specs,
        out_specs=[const, const] + [g[0] for g in grad_specs],
        scratch_shapes=[
            pltpu.VMEM((2, d, FF_COLS), BF16),
            pltpu.VMEM((2, FF_COLS, d), BF16),
            pltpu.VMEM((n, d), F32),
            pltpu.SemaphoreType.DMA((2, 2)),
        ],
    )
    return pl.pallas_call(
        partial(ffn_kernel, ups, downs, aligned),
        grid_spec=spec,
        out_shape=[jax.ShapeDtypeStruct((n, d), BF16), jax.ShapeDtypeStruct((n, d), F32)]
        + [g[1] for g in grad_specs],
        compiler_params=params(60),
        cost_estimate=cost(12 * n * d * hidden, 8 * d * hidden + 14 * n * d),
        name="ffn",
    )(place, h, cot, mid, *args)


def qkv_grad_kernel(groups, place, h_ref, dq_ref, dkv_ref, rkv_ref, keep_ref, send_ref, sum_ref):
    h = h_ref[...]
    my_index = place[1]
    keep_ref[0], send_ref[0] = split_pairs(dot_tn(h, dq_ref[...]).astype(BF16), groups, my_index)
    for t in range(2):
        grad = (dkv_ref[t].astype(F32) + rkv_ref[t].astype(F32)).astype(BF16)
        sum_ref[t] = grad
        keep_ref[t + 1], send_ref[t + 1] = split_pairs(dot_tn(h, grad).astype(BF16), groups, my_index)


def qkv_grad_call(place, h, dq, dkv, rkv, groups):
    n, d = h.shape
    width = dq.shape[1]
    rows = d // (2 * groups)
    heads = width // GROUP_WIDTH
    pair = pl.BlockSpec((2, n, GROUP_WIDTH), lambda g, *_: (0, 0, g))
    share = pl.BlockSpec((3, groups, rows, GROUP_WIDTH), lambda g, *_: (g, 0, 0, 0))
    out = jax.ShapeDtypeStruct((3 * heads, groups, rows, GROUP_WIDTH), BF16)
    spec = pltpu.PrefetchScalarGridSpec(
        num_scalar_prefetch=1,
        grid=(heads,),
        in_specs=[resident((n, d)), pl.BlockSpec((n, GROUP_WIDTH), lambda g, *_: (0, g)), pair, pair],
        out_specs=[share, share, pair],
    )
    return pl.pallas_call(
        partial(qkv_grad_kernel, groups),
        grid_spec=spec,
        out_shape=[out, out, jax.ShapeDtypeStruct((2, n, width), BF16)],
        compiler_params=params(40),
        cost_estimate=cost(6 * n * d * width, 6 * d * width + 2 * n * d + 8 * n * width),
        name="qkv_grad",
    )(place, h, dq, dkv, rkv)


def head_back_kernel(weights, count, place, *refs):
    dqs, dkvs = refs[:count], refs[count : 2 * count]
    x_ref, gr_ref, gain_ref = refs[2 * count : 2 * count + 3]
    parts, refs = cut(refs[2 * count + 3 :], weights)
    tg_ref, dln_ref, wq, wk, wv, sem = refs
    load_all(weights, parts, place, (wq, wk, wv), sem)
    i = pl.program_id(0)
    dq = jnp.concatenate([r[...] for r in dqs], axis=1)
    dk = jnp.concatenate([r[0] for r in dkvs], axis=1)
    dv = jnp.concatenate([r[1] for r in dkvs], axis=1)
    grad = dot_nt(dq, wq[...]) + dot_nt(dk, wk[...]) + dot_nt(dv, wv[...])
    hat, scale = normed(x_ref[...].astype(F32))
    tg_ref[...] = (gr_ref[...] + norm_back(grad, gain_ref[...], hat, scale)).astype(BF16)
    dgain = jnp.sum(grad * hat, axis=0, keepdims=True)
    dbias = jnp.sum(grad, axis=0, keepdims=True)

    @pl.when(i == 0)
    def _():
        dln_ref[0:1, :] = dgain
        dln_ref[1:2, :] = dbias

    @pl.when(i > 0)
    def _():
        dln_ref[0:1, :] += dgain
        dln_ref[1:2, :] += dbias


def head_back_call(place, dqs, dkvs, x, gr, weights, gain):
    n, d = x.shape
    row = pl.BlockSpec((ROWS, d), lambda i, *_: (i, 0))
    specs, args = weight_args(weights)
    spec = pltpu.PrefetchScalarGridSpec(
        num_scalar_prefetch=1,
        grid=(n // ROWS,),
        in_specs=[pl.BlockSpec((ROWS, a.shape[1]), lambda i, *_: (i, 0)) for a in dqs]
        + [pl.BlockSpec((2, ROWS, a.shape[2]), lambda i, *_: (0, i, 0)) for a in dkvs]
        + [row, row, resident((1, d))]
        + specs,
        out_specs=[row, pl.BlockSpec((2, d), lambda *_: (0, 0))],
        scratch_shapes=[pltpu.VMEM((d, d), BF16)] * 3 + [pltpu.SemaphoreType.DMA((3,))],
    )
    return pl.pallas_call(
        partial(head_back_kernel, weights, len(dqs)),
        grid_spec=spec,
        out_shape=[jax.ShapeDtypeStruct((n, d), BF16), jax.ShapeDtypeStruct((2, d), F32)],
        compiler_params=params(48),
        cost_estimate=cost(6 * n * d * d, 6 * d * d + 14 * n * d),
        name="qkv_back",
    )(place, *dqs, *dkvs, x, gr, gain, *args)


class Term:
    def __init__(self, array, axes, first=0, count=None):
        self.array, self.axes, self.first = array, axes, first
        self.count = array.shape[0] if count is None else count
        self.whole = first % self.count != 0

    def spec(self, settled, flipped, open_bits, steps_bits):
        def index_map(step, mine):
            at = [0 if self.whole else self.first // self.count]
            for b in self.axes:
                if (flipped >> b) & 1:
                    at.append(1 - mine[b])
                elif b in settled:
                    at.append(mine[b])
                elif b in steps_bits:
                    at.append((step >> (len(steps_bits) - 1 - steps_bits.index(b))) & 1)
                else:
                    at.append(0)
            return (*at, 0, 0)

        lead = self.array.shape[0] if self.whole else self.count
        inner = tuple(2 if b in open_bits and b not in steps_bits else None for b in self.axes)
        return pl.BlockSpec((lead,) + inner + self.array.shape[-2:], index_map)

    def read(self, ref):
        start = self.first if self.whole else 0
        return ref[start : start + self.count].astype(F32)


class Cube:
    def __init__(self, dp, index, order):
        self.bits = dp.bit_length() - 1
        self.dp, self.order, self.mib = dp, order, 40
        self.mine = ((index >> jnp.arange(self.bits, dtype=jnp.int32)) & 1).astype(jnp.int32)

    def send(self, array, flip):
        return lax.ppermute(array, "dp", [(i, i ^ flip) for i in range(self.dp)])

    def far(self, low=2):
        return [f << low for f in range(1, 1 << (self.bits - low))]

    def terms(self, arrays, first=0, count=None):
        made = []
        for array in arrays:
            lead, _, rows, width = array.shape
            shape = (lead,) + (2,) * self.bits + (rows, width)
            made.append(Term(array.reshape(shape), list(range(self.bits))[::-1], first, count))
        return made

    def add(self, outputs, dtype):
        in_specs, args, plan, out_specs, out_shape = [], [], [], [], []
        for output in outputs:
            lead = 0
            for stream, settled, flipped in output:
                open_bits = [b for b in range(self.bits)[::-1] if b not in settled and not (flipped >> b) & 1]
                steps_bits = open_bits[:STEP_BITS]
                for term in stream:
                    in_specs.append(term.spec(settled, flipped, open_bits, steps_bits))
                    args.append(term.array)
                plan.append((len(out_specs), lead, list(stream)))
                lead += stream[0].count
            outer, inner = len(steps_bits), len(open_bits) - len(steps_bits)

            def out_map(step, mine, outer=outer, inner=inner):
                return (0, *[(step >> (outer - 1 - k)) & 1 for k in range(outer)], *[0] * inner, 0, 0)

            shape = output[0][0][0].array.shape[-2:]
            out_specs.append(pl.BlockSpec((lead,) + (None,) * outer + (2,) * inner + shape, out_map))
            out_shape.append(jax.ShapeDtypeStruct((lead,) + (2,) * (outer + inner) + shape, dtype))

        def kernel(mine, *refs):
            ins, outs = refs[: len(args)], refs[len(args) :]
            at = 0
            for out, first, stream in plan:
                total = stream[0].read(ins[at])
                for k in range(1, len(stream)):
                    total = total + stream[k].read(ins[at + k])
                outs[out][first : first + stream[0].count] = total.astype(dtype)
                at += len(stream)

        spec = pltpu.PrefetchScalarGridSpec(
            num_scalar_prefetch=1, grid=(2**outer,), in_specs=in_specs, out_specs=out_specs
        )
        size = sum(math.prod(o.shape) for o in out_shape)
        call = pl.pallas_call(
            kernel,
            grid_spec=spec,
            out_shape=out_shape,
            compiler_params=params(self.mib),
            cost_estimate=cost(4 * size, 8 * size),
            name="add_terms",
        )
        return self.order.run(call, self.mine, *args)


def merge(arrays, outputs, *awaited):
    d = arrays[0].shape[-1]
    shapes = []
    for output in outputs:
        blocks = sum(arrays[i].shape[0] for i, _, _ in output)
        shapes.append(jax.ShapeDtypeStruct((blocks, output[0][2], d), BF16))

    def kernel(*refs):
        ins, outs = refs[: len(arrays)], refs[len(arrays) + len(awaited) :]
        for out, output in zip(outs, outputs, strict=True):
            at = 0
            for i, first, count in output:
                blocks = ins[i].shape[0]
                out[at : at + blocks] = ins[i][:, first : first + count]
                at += blocks

    whole = pl.BlockSpec(memory_space=pltpu.VMEM)
    size = sum(math.prod(shape.shape) for shape in shapes)
    return pl.pallas_call(
        kernel,
        in_specs=[whole] * len(arrays) + [HBM] * len(awaited),
        out_specs=[whole] * len(outputs),
        out_shape=shapes,
        compiler_params=params(40),
        cost_estimate=cost(size, 4 * size),
        name="merge",
    )(*arrays, *awaited)


class Side:
    def __init__(self, cube, order):
        self.cube, self.order = cube, order

    def hold(self, held, bit):
        self.held = held
        self.got = self.cube.send(held, 1 << bit)

    def parts_of(self):
        last = 1 << self.order[1]
        flips = [0] + self.cube.far()
        flips = flips + [f ^ (1 << self.order[0]) for f in flips]
        moved = [f ^ last for f in flips]
        return [(flips, 0), (moved, 0), (flips, 1), (moved, 1)]

    def index(self, flip):
        first, last = self.order
        return (flip >> 2) + (((flip >> first) & 1) << (self.cube.bits - 2)), (flip >> last) & 1


class Gather:
    def __init__(self, cube, order, exchange, one, two):
        self.cube, self.order, self.exchange = cube, order, exchange
        self.rows = one.shape[0]
        self.local = jnp.concatenate([one, two], axis=0)[None]
        self.sides = (Side(cube, (1, 0)), Side(cube, (0, 1)))

    def far(self):
        local = self.order.after(self.local)
        self.pieces = [local] + [self.cube.send(local, f) for f in self.cube.far()]
        self.order.note(local)

    def near(self, *awaited):
        total = self.local.shape[1]
        outputs = [
            [(i, first, count) for i in range(len(self.pieces))]
            for first, count in ((0, self.rows), (self.rows, total - self.rows))
        ]
        held = self.order.run(lambda first, *rest: merge((first, *rest), outputs, *awaited), *self.pieces)
        for s, array in zip(self.sides, held, strict=True):
            s.hold(array, s.order[0])

    def last(self, *awaited):
        arrays = [a for s in self.sides for a in (s.held, s.got)]
        outputs = [[(i, 0, arrays[i].shape[1]), (i + 1, 0, arrays[i].shape[1])] for i in (0, 2)]
        held = self.order.run(lambda first, *rest: merge((first, *rest), outputs, *awaited), *arrays)
        for s, array in zip(self.sides, held, strict=True):
            s.hold(array, s.order[1])

    def cross(self):
        for s in self.sides:
            s.other = self.exchange(self.order.after(s.held))

    def finish(self):
        for s in self.sides:
            s.rest = self.exchange(self.order.after(s.got))

    def ready(self):
        for s in self.sides:
            s.buffers = [s.held, s.got, s.other, s.rest]
            s.parts = s.parts_of()


class Order:
    def __init__(self):
        self.token = ()

    def after(self, *values):
        if self.token:
            values = lax.optimization_barrier((values, self.token))[0]
        return values if len(values) > 1 else values[0]

    def note(self, *token):
        self.token = token

    def run(self, call, first, *rest):
        out = call(self.after(first), *rest)
        self.note(jax.tree.leaves(out)[0])
        return out


class Scatter:
    def __init__(self, cube, one, two, direct):
        self.cube, self.sides, self.step, self.direct = cube, (one, two), 0, direct
        self.sent, self.last = [], []

    def advance(self):
        step, cube = self.step, self.cube
        if step < 2:
            flips = (1 << step, 1 << (1 - step))
            done = ([], []) if step == 0 else ([0], [1])
            self.sent = cube.add(
                [[(stream, done[s], flips[s]) for stream in self.sides[s]] for s in range(2)], BF16
            )
            self.last = []
            for s in range(2):
                got = cube.send(self.sent[s], flips[s])
                self.last.append(got)
                axes = [b for b in range(cube.bits)[::-1] if b not in done[s] and not (flips[s] >> b) & 1]
                at = 0
                for stream in self.sides[s]:
                    stream.append(Term(got, axes, at, stream[0].count))
                    at += stream[0].count
        else:
            streams = [stream for side in self.sides for stream in side]
            if self.direct:
                done, flips = list(range(cube.bits)), cube.far()
            else:
                done, flips = list(range(step)), [1 << step]
            self.sent = cube.add([[(stream, done, f) for stream in streams] for f in flips], BF16)
            self.last = [cube.send(sent, f) for sent, f in zip(self.sent, flips, strict=True)]
            axes = [] if self.direct else list(range(step + 1, cube.bits))[::-1]
            for got in self.last:
                at = 0
                for stream in streams:
                    stream.append(Term(got, axes, at, stream[0].count))
                    at += stream[0].count
        self.step += 1
        return self

    def finish(self):
        while self.step < (3 if self.direct else self.cube.bits):
            self.advance()
        done = list(range(self.cube.bits))
        return self.cube.add([[(stream, done, 0)] for side in self.sides for stream in side], F32)


def gate(value, *others):
    return lax.optimization_barrier((value, others))[0]


def block_table(seg_full, seg_local, my_index, bq, bk):
    first, last = seg_local[::bq], seg_local[bq - 1 :: bq]
    low = jnp.sum((seg_full[None, :] < first[:, None]).astype(jnp.int32), axis=1)
    high = jnp.sum((seg_full[None, :] <= last[:, None]).astype(jnp.int32), axis=1)
    start = low // ROW_ALIGN * ROW_ALIGN
    table = jnp.stack([start, (high - start + bk - 1) // bk], axis=1).reshape(-1)
    return jnp.concatenate([table, my_index[None]]).astype(jnp.int32)


def body(
    tokens,
    segments,
    ln1_gain,
    ln1_bias,
    w_query,
    w_key,
    w_value,
    w_out,
    ln2_gain,
    ln2_bias,
    w_up,
    w_down,
    cotangent,
):
    x = tokens[0]
    n, d = x.shape
    cot = cotangent[0]
    rows = w_query.shape[0]
    devices = d // rows
    hidden = w_up.shape[1]
    per_device = hidden // devices
    my_index = lax.axis_index("seq")
    seg_full = segments[0]
    seg_local = lax.dynamic_slice_in_dim(seg_full, my_index * n, n)
    tab = block_table(seg_full, seg_local, my_index, ATT_Q, ATT_K)
    seg_q = seg_local.reshape(n // ATT_Q, 1, ATT_Q)
    seg_col = jnp.pad(seg_full, (0, ATT_K), constant_values=-1)[:, None]

    dp = devices // 2
    dp_index = lax.axis_index("dp")
    order = Order()
    cube = Cube(dp, dp_index, order)
    place = jnp.stack([dp_index, my_index]).astype(jnp.int32)
    swap = [(0, 1), (1, 0)]
    tiles = hidden // d

    def exchange(value):
        return lax.ppermute(value, "seq", swap)

    def halves(value, axis):
        keep = lax.dynamic_index_in_dim(value, my_index, axis, keepdims=False)
        send = lax.dynamic_index_in_dim(value, 1 - my_index, axis, keepdims=False)
        return keep, send

    vectors = jnp.concatenate([ln1_gain, ln1_bias, ln2_gain, ln2_bias]).astype(F32)
    vectors = jnp.broadcast_to(vectors[None], (devices, 4 * rows))
    vectors = lax.all_to_all(vectors, BOTH, 0, 0, tiled=True)
    ln = vectors.reshape(devices, 4, rows).transpose(1, 0, 2).reshape(4, 1, d)

    aligned = rows % 32 == 0
    groups = d // GROUP_WIDTH
    if aligned:
        cut_row, half_down = rows // 2, per_device // 2
        up_tiles = w_up.reshape(rows, tiles, d).transpose(1, 0, 2)
        half_up = tiles // 2 * rows
        low_up, high_up = (u.reshape(half_up, d) for u in (up_tiles[: tiles // 2], up_tiles[tiles // 2 :]))
        head = Gather(
            cube, order, exchange,
            jnp.concatenate([w_key, w_query[:cut_row]]), jnp.concatenate([w_value, w_query[cut_row:]]),
        )
        low = Gather(
            cube, order, exchange,
            jnp.concatenate([low_up, w_out[:cut_row]]), jnp.concatenate([w_down[:half_down], w_out[cut_row:]]),
        )
        high = Gather(cube, order, exchange, high_up, w_down[half_down:])
        head.far()
        head.near(vectors, seg_col, seg_q, tab)
        low.far()
        head.last()
        head.cross()
        order.note(*[side.got for side in head.sides])
        head.finish()
        head.ready()
        low.near()
        key_w = Spread(rows, [(head.sides[0], 0, rows, 0)])
        value_w = Spread(rows, [(head.sides[1], 0, rows, 0)])
        query_w = Spread(rows, [(head.sides[0], rows, cut_row, 0), (head.sides[1], rows, cut_row, cut_row)])
    else:
        every = jnp.concatenate([w_query, w_key, w_value, w_out], axis=0).reshape(4, rows, d)
        every = lax.all_gather(every, BOTH, axis=1, tiled=True)
        query_w, key_w, value_w, out_w = (Plain(every[t], rows) for t in range(4))
        up_all = lax.all_gather(w_up, BOTH, axis=0, tiled=True)
        ups = [Plain(up_all[:, t * d : (t + 1) * d], rows) for t in range(tiles)]
        downs = [Plain(lax.all_gather(w_down, BOTH, axis=0, tiled=True), per_device)]

    h1, own = order.run(kv_call, place, x, ln[0], ln[1], [key_w, value_w])
    if aligned:
        low.last()
    other = exchange(order.after(own))
    q = order.run(q_call, place, h1, [query_w])
    if aligned:
        high.far()
    outs, lses = [], []
    plan = [(0, 2), (2, 1), (3, 1)] if groups == 4 else [(g, 1) for g in range(groups)]
    for i, (start, count) in enumerate(plan):
        if aligned and i == 1:
            high.near()
            low.finish()
        if aligned and i == 2:
            high.last(*[side.rest for side in low.sides])
            low.cross()
        out, lse = order.run(
            attend_call, tab, q, own, other, seg_q, seg_col, ATT_Q, ATT_K, start, count
        )
        outs.append(out)
        lses.append(lse)
    if aligned:
        low.ready()
        high.cross()
        out_w = Spread(
            rows, [(low.sides[0], half_up, cut_row, 0), (low.sides[1], half_down, cut_row, cut_row)]
        )
    mid, h2 = order.run(mid_call, place, x, outs, [out_w], ln[2], ln[3])
    if aligned:
        high.finish()
        high.ready()

    up_rows = tiles * rows
    if aligned:
        ups = [
            Spread(rows, [((low, high)[t // (tiles // 2)].sides[0], t % (tiles // 2) * rows, rows, 0)])
            for t in range(tiles)
        ]
        downs = [Spread(half_down, [(r.sides[1], 0, half_down, 0)]) for r in (low, high)]
        per_tile = d // FF_COLS
        group = FF_COLS // per_device
        up_out = (
            pl.BlockSpec((None, dp, rows, FF_COLS), lambda j, *_: (j // per_tile, 0, 0, j % per_tile)),
            jax.ShapeDtypeStruct((tiles, dp, rows, d), BF16),
        )
        down_out = (
            pl.BlockSpec((tiles, group // 2, rows, d), lambda j, *_: (0, j, 0, 0)),
            jax.ShapeDtypeStruct((tiles, dp, rows, d), BF16),
        )
        grad_specs = [up_out, up_out, down_out, down_out]
    else:
        grad_specs = [
            (pl.BlockSpec((d, FF_COLS), lambda j, *_: (0, j)), jax.ShapeDtypeStruct((d, hidden), BF16)),
            (pl.BlockSpec((FF_COLS, d), lambda j, *_: (j, 0)), jax.ShapeDtypeStruct((hidden, d), BF16)),
        ]
    mixed, gmid, *grads = order.run(ffn_call, place, h2, cot, ups, downs, mid, grad_specs, hidden, aligned)
    if not aligned:
        dwu = grads[0].reshape(dp, 2, rows, tiles, d).transpose(3, 0, 1, 2, 4)
        dwd = grads[1].reshape(dp, 2, tiles, rows, d).transpose(2, 0, 1, 3, 4)
        grads = [*halves(dwu, 2), *halves(dwd, 2)]
    keep_up, send_up, keep_down, send_down = grads
    got_up, got_down = exchange(send_up), exchange(send_down)
    big = Scatter(cube, [cube.terms([keep_up, got_up])], [cube.terms([keep_down, got_down])], False)

    grad_mid, grad_att, keep_out, send_out, dln2 = order.run(
        mid_back_call, place, gmid, mid, cot, outs, [out_w], ln[2], dp
    )
    big.advance()
    got_out = exchange(order.after(send_out))
    dqs, dkvs = [], []

    def attend_back(g):
        which = [i for i, (start, _) in enumerate(plan) if start <= g][-1]
        return order.run(
            attend_back_call, tab, q, grad_att, outs[which], own, other, seg_q, seg_col,
            lses[which], ATT_Q, ATT_K, g, 1, g - plan[which][0],
        )

    def finish_group(dq, dkv, got):
        keep, send, dkv = order.run(qkv_grad_call, place, h1, dq, dkv, got, dp)
        dqs.append(dq)
        dkvs.append(dkv)
        return keep, send

    dq_0, dkv_0, sent_0 = attend_back(0)
    got_0 = exchange(sent_0)
    dq_1, dkv_1, sent_1 = attend_back(1)
    keep_0, send_0 = finish_group(dq_0, dkv_0, got_0)
    big.advance()
    got_1 = exchange(order.after(sent_1))
    keep_1, send_1 = finish_group(dq_1, dkv_1, got_1)
    terms_0, terms_1 = [keep_0, exchange(order.after(send_0))], [keep_1, exchange(order.after(send_1))]
    dq_2, dkv_2, sent_2 = attend_back(2)
    big.advance()
    tail_one = Scatter(
        cube,
        [cube.terms(terms_0), cube.terms([keep_out, got_out], 0, 2)],
        [cube.terms(terms_1), cube.terms([keep_out, got_out], 2, 2)],
        False,
    )
    tail_one.advance()
    got_2 = exchange(order.after(sent_2))
    dq_3, dkv_3, sent_3 = attend_back(3)
    big.advance()
    tail_one.advance()
    got_3 = exchange(order.after(sent_3))
    keep_2, send_2 = finish_group(dq_2, dkv_2, got_2)
    keep_3, send_3 = finish_group(dq_3, dkv_3, got_3)
    tail_one.advance()
    terms_2, terms_3 = [keep_2, exchange(order.after(send_2))], [keep_3, exchange(order.after(send_3))]
    tail_two = Scatter(cube, [cube.terms(terms_2)], [cube.terms(terms_3)], True)
    tail_two.advance()
    token_grad, dln1 = order.run(
        head_back_call, place, dqs, dkvs, x, grad_mid, [query_w, key_w, value_w], ln[0]
    )
    cube.mib = 62
    tail_two.advance()
    tail_one.advance()
    up_share, down_share = big.finish()
    tail_two.advance()
    dln = jnp.concatenate([dln1, order.after(dln2)], axis=0).reshape(4, devices, rows).transpose(1, 0, 2)
    dln = lax.all_to_all(dln.reshape(devices, 4 * rows), BOTH, 0, 0, tiled=True)
    dln = jnp.sum(dln.reshape(devices, 4, rows), axis=0)
    one_a, out_a, one_b, out_b = tail_one.finish()
    two_a, two_b = tail_two.finish()

    up_share = up_share.transpose(1, 0, 2).reshape(rows, hidden)
    down_share = down_share.reshape(per_device, d)
    qkv_share = jnp.concatenate([one_a, one_b, two_a, two_b], axis=-1)
    out_share = jnp.concatenate([out_a, out_b], axis=0).transpose(1, 0, 2).reshape(rows, d)
    return (
        mixed[None],
        token_grad[None],
        dln[0],
        dln[1],
        qkv_share[0],
        qkv_share[1],
        qkv_share[2],
        out_share,
        dln[2],
        dln[3],
        up_share,
        down_share,
    )


def solution(mesh):
    row, act, vec = P(BOTH, None), P("dp", "seq", None), P(BOTH)
    in_specs = (act, P("dp", None), vec, vec, row, row, row, row, vec, vec, row, row, act)
    out_specs = (act, act, vec, vec, row, row, row, row, vec, vec, row, row)
    return jax.shard_map(body, mesh=mesh, in_specs=in_specs, out_specs=out_specs, check_vma=False)
```

```python
import math
from functools import partial

import jax
import jax.numpy as jnp
from jax import lax
from jax.experimental import pallas as pl
from jax.experimental.pallas import tpu as pltpu
from jax.sharding import PartitionSpec as P

BF16 = jnp.bfloat16
F32 = jnp.float32
HEAD_DIM = 64
GROUP = 4
GROUP_WIDTH = GROUP * HEAD_DIM
NEG = -1000000000.0
BOTH = ("dp", "seq")
ATT_Q = 256
ATT_K = 512
BACK_K = 256
ROW_ALIGN = 16
ROWS = 256
FF_COLS = 512
COST_SCALE = 100000
STEP_BITS = 1


def dot_nn(left, right):
    return lax.dot_general(left, right, (((1,), (0,)), ((), ())), preferred_element_type=F32)


def dot_nt(left, right):
    return lax.dot_general(left, right, (((1,), (1,)), ((), ())), preferred_element_type=F32)


def dot_tn(left, right):
    return lax.dot_general(left, right, (((0,), (0,)), ((), ())), preferred_element_type=F32)


def params(mib):
    return pltpu.CompilerParams(vmem_limit_bytes=mib << 20)


def cost(flops, nbytes, scale=None):
    if scale:
        return pl.CostEstimate(flops=scale * flops, bytes_accessed=scale * nbytes, transcendentals=0)
    return pl.CostEstimate(flops=flops // COST_SCALE, bytes_accessed=nbytes // COST_SCALE, transcendentals=0)


def normed(values):
    centre = values - jnp.mean(values, axis=-1, keepdims=True)
    scale = lax.rsqrt(jnp.mean(centre * centre, axis=-1, keepdims=True) + 1e-05)
    return centre * scale, scale


def norm_back(grad, gain_vec, hat, scale):
    inner = grad * gain_vec
    return scale * (
        inner
        - jnp.mean(inner, axis=-1, keepdims=True)
        - hat * jnp.mean(inner * hat, axis=-1, keepdims=True)
    )


def flat(ref):
    value = ref[...]
    return value.reshape(-1, value.shape[-1])


def resident(shape):
    zeros = (0,) * len(shape)
    return pl.BlockSpec(shape, lambda *_: zeros, pipeline_mode=pl.Buffered(1))


class Spread:
    def __init__(self, block, pieces):
        self.block, self.pieces = block, pieces
        self.args = [b for rounds, *_ in pieces for b in rounds.buffers]

    def start(self, refs, place, target, sem, columns=None):
        for i, (rounds, first, count, at) in enumerate(self.pieces):
            for ref, (flips, core) in zip(refs[4 * i : 4 * i + 4], rounds.parts, strict=True):
                for e, flip in enumerate(flips):
                    device = (place[0] ^ flip) * 2 + (place[1] ^ core)
                    row = pl.multiple_of(device * self.block + at, count)
                    source = ref.at[e, pl.ds(first, count)]
                    if columns is not None:
                        source = ref.at[e, pl.ds(first, count), columns]
                    pltpu.make_async_copy(source, target.at[pl.ds(row, count), :], sem).start()

    def start_rows(self, refs, place, target, sem, first, group):
        ((rounds, begin, count, _),) = self.pieces
        for k in range(group):
            device = first + k
            flip = (device // 2) ^ place[0]
            at, last = rounds.index(flip)
            core = (device % 2) ^ place[1]
            for i, ref in enumerate(refs):

                @pl.when((last == i % 2) & (core == i // 2))
                def _(ref=ref, at=at, k=k):
                    pltpu.make_async_copy(
                        ref.at[at, pl.ds(begin, count)], target.at[pl.ds(k * count, count), :], sem
                    ).start()


class Plain:
    def __init__(self, array, block):
        self.args, self.block = [array], block

    def start(self, refs, place, target, sem, columns=None):
        source = refs[0] if columns is None else refs[0].at[:, columns]
        pltpu.make_async_copy(source, target, sem).start()

    def start_rows(self, refs, place, target, sem, first, group):
        pltpu.make_async_copy(refs[0].at[pl.ds(first * self.block, group * self.block), :], target, sem).start()


def arrived(target, sem):
    pltpu.make_async_copy(target, target, sem).wait()


def cut(refs, weights):
    parts = []
    for weight in weights:
        parts.append(refs[: len(weight.args)])
        refs = refs[len(weight.args) :]
    return parts, refs


def load_all(weights, parts, place, targets, sem, wait=True):
    @pl.when(pl.program_id(0) == 0)
    def _():
        for i, weight in enumerate(weights):
            weight.start(parts[i], place, targets[i], sem.at[i])
        if wait:
            for i in range(len(weights)):
                arrived(targets[i], sem.at[i])


def loaded(targets, sem, i):
    @pl.when(pl.program_id(0) == 0)
    def _():
        arrived(targets[i], sem.at[i])

    return targets[i][...]


HBM = pl.BlockSpec(memory_space=pltpu.HBM)


def weight_args(weights):
    args = [a for w in weights for a in w.args]
    return [HBM] * len(args), args


def kv_kernel(weights, place, x_ref, gain_ref, bias_ref, *refs):
    parts, refs = cut(refs, weights)
    h_ref, kv_ref, wk, wv, sem = refs
    load_all(weights, parts, place, (wk, wv), sem)
    hat, _ = normed(x_ref[...].astype(F32))
    low = (hat * gain_ref[...] + bias_ref[...]).astype(BF16)
    h_ref[...] = low
    kv_ref[0] = dot_nn(low, wk[...]).astype(BF16)
    kv_ref[1] = dot_nn(low, wv[...]).astype(BF16)


def kv_call(place, x, gain, bias, weights):
    n, d = x.shape
    row = pl.BlockSpec((ROWS, d), lambda i, *_: (i, 0))
    specs, args = weight_args(weights)
    spec = pltpu.PrefetchScalarGridSpec(
        num_scalar_prefetch=1,
        grid=(n // ROWS,),
        in_specs=[row, resident((1, d)), resident((1, d))] + specs,
        out_specs=[row, pl.BlockSpec((2, ROWS, d), lambda i, *_: (0, i, 0))],
        scratch_shapes=[pltpu.VMEM((d, d), BF16)] * 2 + [pltpu.SemaphoreType.DMA((2,))],
    )
    return pl.pallas_call(
        partial(kv_kernel, weights),
        grid_spec=spec,
        out_shape=[jax.ShapeDtypeStruct((n, d), BF16), jax.ShapeDtypeStruct((2, n, d), BF16)],
        compiler_params=params(40),
        cost_estimate=cost(4 * n * d * d, 4 * d * d + 8 * n * d),
        name="kv_proj",
    )(place, x, gain, bias, *args)


def q_kernel(weights, place, h_ref, *refs):
    parts, refs = cut(refs, weights)
    q_ref, wq, sem = refs
    load_all(weights, parts, place, (wq,), sem)
    q_ref[...] = (dot_nn(h_ref[...], wq[...]).astype(BF16).astype(F32) * 0.125).astype(BF16)


def q_call(place, h, weights):
    n, d = h.shape
    row = pl.BlockSpec((ROWS, d), lambda i, *_: (i, 0))
    specs, args = weight_args(weights)
    spec = pltpu.PrefetchScalarGridSpec(
        num_scalar_prefetch=1,
        grid=(n // ROWS,),
        in_specs=[row] + specs,
        out_specs=row,
        scratch_shapes=[pltpu.VMEM((d, d), BF16), pltpu.SemaphoreType.DMA((1,))],
    )
    return pl.pallas_call(
        partial(q_kernel, weights),
        grid_spec=spec,
        out_shape=jax.ShapeDtypeStruct((n, d), BF16),
        compiler_params=params(32),
        cost_estimate=cost(2 * n * d * d, 2 * d * d + 4 * n * d),
        name="q_proj",
    )(place, h, *args)


def stack_heads(block):
    lane = lax.broadcasted_iota(jnp.int32, block.shape, 1) // HEAD_DIM
    zero = jnp.zeros_like(block)
    return jnp.concatenate([jnp.where(lane == h, block, zero) for h in range(GROUP)], axis=0)


def head_cols(value, h, width):
    return value[:, h * width : (h + 1) * width]


def head_rows(value, h):
    return value[h * HEAD_DIM : (h + 1) * HEAD_DIM, :]


def line_up(target, own_ref, other_ref, which, mine):
    n = own_ref.shape[1]
    target[pl.ds(pl.multiple_of(mine * n, n), n), :] = own_ref[which]
    target[pl.ds(pl.multiple_of((1 - mine) * n, n), n), :] = other_ref[which]
    target[2 * n :, :] = jnp.zeros((target.shape[0] - 2 * n, target.shape[1]), target.dtype)


def attend_kernel(bq, bk, tab, q_ref, own_ref, other_ref, sq_ref, s_ref, o_ref, lse_ref, k_s, v_s):
    i = pl.program_id(1)

    @pl.when(i == 0)
    def _():
        mine = tab[2 * pl.num_programs(1)]
        line_up(k_s, own_ref, other_ref, 0, mine)
        line_up(v_s, own_ref, other_ref, 1, mine)

    stacked = stack_heads(q_ref[...])
    seg_q = jnp.concatenate([sq_ref[0]] * GROUP, axis=1)
    first = tab[2 * i]

    def step(j, carry):
        top, total, acc = carry
        at = pl.multiple_of(first + j * bk, ROW_ALIGN)
        scores = dot_nt(k_s[pl.ds(at, bk), :], stacked)
        scores = jnp.where(s_ref[pl.ds(at, bk), :] == seg_q, scores, NEG)
        new_top = jnp.maximum(top, jnp.max(scores, axis=0, keepdims=True))
        decay = jnp.exp(top - new_top)
        probs = jnp.exp(scores - new_top)
        total = total * decay + jnp.sum(probs, axis=0, keepdims=True)
        low = probs.astype(BF16)
        values = v_s[pl.ds(at, bk), :].T
        acc = tuple(
            acc[h] * head_cols(decay, h, bq) + dot_nn(head_rows(values, h), head_cols(low, h, bq))
            for h in range(GROUP)
        )
        return new_top, total, acc

    state = (
        jnp.full((1, GROUP * bq), -jnp.inf, F32),
        jnp.zeros((1, GROUP * bq), F32),
        tuple(jnp.zeros((HEAD_DIM, bq), F32) for _ in range(GROUP)),
    )
    top, total, acc = lax.fori_loop(0, tab[2 * i + 1], step, state)
    out = jnp.concatenate([acc[h] / head_cols(total, h, bq) for h in range(GROUP)], axis=0)
    o_ref[...] = out.T.astype(BF16)
    lse_ref[0, 0] = top + jnp.log(total)


def attend_specs(n, bq, padded, first):
    def half(_):
        return pl.BlockSpec((2, n, GROUP_WIDTH), lambda g, i, *_: (0, 0, g + first))

    return [
        half(0),
        half(1),
        pl.BlockSpec((1, 1, bq), lambda g, i, *_: (i, 0, 0)),
        pl.BlockSpec((padded, 1), lambda *_: (0, 0)),
    ]


def attend_call(tab, q, own, other, seg_q, seg_col, bq, bk, first, groups):
    n, d = q.shape
    blocks = n // bq
    padded = seg_col.shape[0]
    spec = pltpu.PrefetchScalarGridSpec(
        num_scalar_prefetch=1,
        grid=(groups, blocks),
        in_specs=[pl.BlockSpec((bq, GROUP_WIDTH), lambda g, i, *_: (i, g + first))]
        + attend_specs(n, bq, padded, first),
        out_specs=[
            pl.BlockSpec((bq, GROUP_WIDTH), lambda g, i, *_: (i, g)),
            pl.BlockSpec((1, 1, 1, GROUP * bq), lambda g, i, *_: (g, i, 0, 0)),
        ],
        scratch_shapes=[pltpu.VMEM((padded, GROUP_WIDTH), BF16)] * 2,
    )
    return pl.pallas_call(
        partial(attend_kernel, bq, bk),
        grid_spec=spec,
        out_shape=[
            jax.ShapeDtypeStruct((n, groups * GROUP_WIDTH), BF16),
            jax.ShapeDtypeStruct((groups, blocks, 1, GROUP * bq), F32),
        ],
        compiler_params=params(56),
        cost_estimate=cost(8_000_000_000 * groups, 3 * groups * n * d),
        name="attend",
    )(tab, q, own, other, seg_q, seg_col)


def attend_back_kernel(
    bq, bk, tab, q_ref, go_ref, o_ref, lse_ref, own_ref, other_ref, sq_ref, s_ref,
    dq_ref, down_ref, dpart_ref, k_s, v_s, dk_s, dv_s,
):
    i = pl.program_id(1)
    mine = tab[2 * pl.num_programs(1)]

    @pl.when(i == 0)
    def _():
        line_up(k_s, own_ref, other_ref, 0, mine)
        line_up(v_s, own_ref, other_ref, 1, mine)
        dk_s[...] = jnp.zeros_like(dk_s)
        dv_s[...] = jnp.zeros_like(dv_s)

    stacked = stack_heads(q_ref[...])
    grad = go_ref[...]
    stacked_grad = stack_heads(grad)
    product = (grad.astype(F32) * o_ref[...].astype(F32)).T
    inner = jnp.concatenate(
        [jnp.sum(head_rows(product, h), axis=0, keepdims=True) for h in range(GROUP)], axis=1
    )
    seg_q = jnp.concatenate([sq_ref[0]] * GROUP, axis=1)
    lse = lse_ref[0, 0]
    first = tab[2 * i]

    def step(j, acc):
        at = pl.multiple_of(first + j * bk, ROW_ALIGN)
        keys = k_s[pl.ds(at, bk), :]
        scores = dot_nt(keys, stacked)
        scores = jnp.where(s_ref[pl.ds(at, bk), :] == seg_q, scores, NEG)
        probs = jnp.exp(scores - lse)
        grad_probs = dot_nt(v_s[pl.ds(at, bk), :], stacked_grad)
        grad_scores = (probs * (grad_probs - inner)).astype(BF16)
        dv_s[pl.ds(at, bk), :] += dot_nn(probs.astype(BF16), stacked_grad)
        dk_s[pl.ds(at, bk), :] += dot_nn(grad_scores, stacked)
        keys_t = keys.T
        return tuple(
            acc[h] + dot_nn(head_rows(keys_t, h), head_cols(grad_scores, h, bq)) for h in range(GROUP)
        )

    state = tuple(jnp.zeros((HEAD_DIM, bq), F32) for _ in range(GROUP))
    state = lax.fori_loop(0, tab[2 * i + 1], step, state)
    dq_ref[...] = (jnp.concatenate(state, axis=0).T * 0.125).astype(BF16)

    @pl.when(i == pl.num_programs(1) - 1)
    def _():
        n = down_ref.shape[1]
        for ref, half in ((down_ref, mine), (dpart_ref, 1 - mine)):
            rows = pl.ds(pl.multiple_of(half * n, n), n)
            ref[0] = dk_s[rows, :].astype(BF16)
            ref[1] = dv_s[rows, :].astype(BF16)


def attend_back_call(tab, q, grad, out, own, other, seg_q, seg_col, lse, bq, bk, first, groups, out_first):
    n, d = q.shape
    blocks = n // bq
    padded = seg_col.shape[0]
    query = pl.BlockSpec((bq, GROUP_WIDTH), lambda g, i, *_: (i, g + first))
    pair = pl.BlockSpec((2, n, GROUP_WIDTH), lambda g, i, *_: (0, 0, g))
    spec = pltpu.PrefetchScalarGridSpec(
        num_scalar_prefetch=1,
        grid=(groups, blocks),
        in_specs=[
            query,
            query,
            pl.BlockSpec((bq, GROUP_WIDTH), lambda g, i, *_: (i, g + out_first)),
            pl.BlockSpec((1, 1, 1, GROUP * bq), lambda g, i, *_: (g + out_first, i, 0, 0)),
        ]
        + attend_specs(n, bq, padded, first),
        out_specs=[pl.BlockSpec((bq, GROUP_WIDTH), lambda g, i, *_: (i, g)), pair, pair],
        scratch_shapes=[pltpu.VMEM((padded, GROUP_WIDTH), BF16)] * 2
        + [pltpu.VMEM((padded, GROUP_WIDTH), F32)] * 2,
    )
    width = groups * GROUP_WIDTH
    return pl.pallas_call(
        partial(attend_back_kernel, bq, bk),
        grid_spec=spec,
        out_shape=[
            jax.ShapeDtypeStruct((n, width), BF16),
            jax.ShapeDtypeStruct((2, n, width), BF16),
            jax.ShapeDtypeStruct((2, n, width), BF16),
        ],
        compiler_params=params(56),
        cost_estimate=cost(12_000_000_000 * groups, 6 * groups * n * d),
        name="attend_back",
    )(tab, q, grad, out, lse, own, other, seg_q, seg_col)


def mid_kernel(weights, count, place, x_ref, gain_ref, bias_ref, *refs):
    outs, refs = refs[:count], refs[count:]
    parts, refs = cut(refs, weights)
    r_ref, h_ref, wo, sem = refs
    load_all(weights, parts, place, (wo,), sem)
    mid = x_ref[...].astype(F32) + dot_nn(jnp.concatenate([o[...] for o in outs], axis=1), wo[...])
    r_ref[...] = mid
    hat, _ = normed(mid)
    h_ref[...] = (hat * gain_ref[...] + bias_ref[...]).astype(BF16)


def mid_call(place, x, outs, weights, gain, bias):
    n, d = x.shape
    row = pl.BlockSpec((ROWS, d), lambda i, *_: (i, 0))
    specs, args = weight_args(weights)
    spec = pltpu.PrefetchScalarGridSpec(
        num_scalar_prefetch=1,
        grid=(n // ROWS,),
        in_specs=[row, resident((1, d)), resident((1, d))]
        + [pl.BlockSpec((ROWS, o.shape[1]), lambda i, *_: (i, 0)) for o in outs]
        + specs,
        out_specs=[row, row],
        scratch_shapes=[pltpu.VMEM((d, d), BF16), pltpu.SemaphoreType.DMA((1,))],
    )
    return pl.pallas_call(
        partial(mid_kernel, weights, len(outs)),
        grid_spec=spec,
        out_shape=[jax.ShapeDtypeStruct((n, d), F32), jax.ShapeDtypeStruct((n, d), BF16)],
        compiler_params=params(32),
        cost_estimate=cost(2 * n * d * d, 2 * d * d + 10 * n * d),
        name="out_proj",
    )(place, x, gain, bias, *outs, *args)


def mid_back_kernel(weights, count, place, gh_ref, r_ref, g_ref, gain_ref, *refs):
    outs, refs = refs[:count], refs[count:]
    parts, refs = cut(refs, weights)
    gr_ref, go_ref, keep_ref, send_ref, dln_ref, acc, wo, sem = refs
    load_all(weights, parts, place, (wo,), sem, wait=False)
    i = pl.program_id(0)
    hat, scale = normed(r_ref[...])
    grad = gh_ref[...]
    total = g_ref[...].astype(F32) + norm_back(grad, gain_ref[...], hat, scale)
    gr_ref[...] = total
    low = total.astype(BF16)
    part = dot_tn(jnp.concatenate([o[...] for o in outs], axis=1), low)
    go_ref[...] = dot_nt(low, loaded((wo,), sem, 0)).astype(BF16)
    dgain = jnp.sum(grad * hat, axis=0, keepdims=True)
    dbias = jnp.sum(grad, axis=0, keepdims=True)

    @pl.when(i == 0)
    def _():
        acc[...] = part
        dln_ref[0:1, :] = dgain
        dln_ref[1:2, :] = dbias

    @pl.when(i > 0)
    def _():
        acc[...] += part
        dln_ref[0:1, :] += dgain
        dln_ref[1:2, :] += dbias

    @pl.when(i == pl.num_programs(0) - 1)
    def _():
        lanes = keep_ref.shape[3]
        for ref, value in zip(
            (keep_ref, send_ref), split_pairs(acc[...].astype(BF16), keep_ref.shape[1], place[1]), strict=True
        ):
            for t in range(ref.shape[0]):
                ref[t] = value[:, :, t * lanes : (t + 1) * lanes]


def mid_back_call(place, grad, mid, cot, outs, weights, gain, groups):
    n, d = mid.shape
    row = pl.BlockSpec((ROWS, d), lambda i, *_: (i, 0))
    share = (d // GROUP_WIDTH, groups, d // (2 * groups), GROUP_WIDTH)
    specs, args = weight_args(weights)
    spec = pltpu.PrefetchScalarGridSpec(
        num_scalar_prefetch=1,
        grid=(n // ROWS,),
        in_specs=[row, row, row, resident((1, d))]
        + [pl.BlockSpec((ROWS, o.shape[1]), lambda i, *_: (i, 0)) for o in outs]
        + specs,
        out_specs=[
            row,
            row,
            pl.BlockSpec(share, lambda *_: (0, 0, 0, 0)),
            pl.BlockSpec(share, lambda *_: (0, 0, 0, 0)),
            pl.BlockSpec((2, d), lambda *_: (0, 0)),
        ],
        scratch_shapes=[
            pltpu.VMEM((d, d), F32),
            pltpu.VMEM((d, d), BF16),
            pltpu.SemaphoreType.DMA((1,)),
        ],
    )
    return pl.pallas_call(
        partial(mid_back_kernel, weights, len(outs)),
        grid_spec=spec,
        out_shape=[
            jax.ShapeDtypeStruct((n, d), F32),
            jax.ShapeDtypeStruct((n, d), BF16),
            jax.ShapeDtypeStruct(share, BF16),
            jax.ShapeDtypeStruct(share, BF16),
            jax.ShapeDtypeStruct((2, d), F32),
        ],
        compiler_params=params(48),
        cost_estimate=cost(4 * n * d * d, 4 * d * d + 18 * n * d),
        name="out_proj_back",
    )(place, grad, mid, cot, gain, *outs, *args)


def split_pairs(value, groups, my_index):
    rows = value.shape[0] // (2 * groups)
    pairs = value.reshape(groups, 2, rows, value.shape[1])
    even, odd = pairs[:, 0], pairs[:, 1]
    first = my_index == 0
    return jnp.where(first, even, odd), jnp.where(first, odd, even)


def ffn_grads(h, grad, wu, wd):
    up = dot_nn(h, wu)
    cdf = 0.5 * (1.0 + lax.erf(up * 0.7071067811865476))
    act = (up * cdf).astype(BF16)
    slope = cdf + up * (jnp.exp(-0.5 * up * up) * 0.3989422804014327)
    gu = (dot_nt(grad, wd) * slope).astype(BF16)
    return act, gu, dot_tn(h, gu).astype(BF16), dot_tn(act, grad).astype(BF16)


def ffn_sums(j, act, gu, wu, wd, mid_ref, mixed_ref, gh_ref, acc):
    @pl.when(j == 0)
    def _():
        acc[...] = mid_ref[...] + dot_nn(act, wd)
        gh_ref[...] = dot_nt(gu, wu)

    @pl.when(j > 0)
    def _():
        acc[...] += dot_nn(act, wd)
        gh_ref[...] += dot_nt(gu, wu)

    @pl.when(j == pl.num_programs(0) - 1)
    def _():
        mixed_ref[...] = acc[...].astype(BF16)


def ffn_kernel(ups, downs, aligned, place, h_ref, g_ref, mid_ref, *refs):
    parts, refs = cut(refs, ups + downs)
    mixed_ref, gh_ref = refs[:2]
    grads = refs[2:6] if aligned else refs[2:4]
    wu_s, wd_s, acc, sem = refs[-4:]
    j, steps = pl.program_id(0), pl.num_programs(0)
    per_tile = h_ref.shape[1] // FF_COLS
    group = FF_COLS // sum(w.block for w in downs)

    def fetch(step, slot):
        column = pl.ds(pl.multiple_of((step % per_tile) * FF_COLS, FF_COLS), FF_COLS)
        for t, up in enumerate(ups):

            @pl.when(step // per_tile == t)
            def _(t=t, up=up):
                up.start(parts[t], place, wu_s.at[slot], sem.at[slot, 0], column)

        at = 0
        for i, down in enumerate(downs):
            count = group * down.block
            down.start_rows(
                parts[len(ups) + i], place, wd_s.at[slot, pl.ds(at, count), :], sem.at[slot, 1], step * group, group
            )
            at += count

    @pl.when(j == 0)
    def _():
        fetch(j, 0)

    @pl.when(j + 1 < steps)
    def _():
        fetch(j + 1, (j + 1) % 2)

    slot = j % 2
    arrived(wu_s.at[slot], sem.at[slot, 0])
    arrived(wd_s.at[slot], sem.at[slot, 1])
    wu, wd = wu_s[slot], wd_s[slot]
    if len(downs) > 1:
        width = wd.shape[1]
        stack, at = [], 0
        for down in downs:
            count = group * down.block
            stack.append(wd[at : at + count].reshape(group, down.block, width))
            at += count
        wd = jnp.concatenate(stack, axis=1).reshape(FF_COLS, width)
    act, gu, dwu, dwd = ffn_grads(h_ref[...], g_ref[...], wu, wd)
    if aligned:
        grads[0][...], grads[1][...] = split_pairs(dwu, grads[0].shape[0], place[1])
        for ref, value in zip(grads[2:], split_pairs(dwd, grads[2].shape[1], place[1]), strict=True):
            for t in range(ref.shape[0]):
                ref[t] = value[:, t * ref.shape[2] : (t + 1) * ref.shape[2]]
    else:
        grads[0][...] = dwu
        grads[1][...] = dwd
    ffn_sums(j, act, gu, wu, wd, mid_ref, mixed_ref, gh_ref, acc)


def ffn_call(place, h, cot, ups, downs, mid, grad_specs, hidden, aligned):
    n, d = h.shape
    full = resident((n, d))
    const = pl.BlockSpec((n, d), lambda j, *_: (0, 0))
    specs, args = weight_args(ups + downs)
    spec = pltpu.PrefetchScalarGridSpec(
        num_scalar_prefetch=1,
        grid=(hidden // FF_COLS,),
        in_specs=[full, full, full] + specs,
        out_specs=[const, const] + [g[0] for g in grad_specs],
        scratch_shapes=[
            pltpu.VMEM((2, d, FF_COLS), BF16),
            pltpu.VMEM((2, FF_COLS, d), BF16),
            pltpu.VMEM((n, d), F32),
            pltpu.SemaphoreType.DMA((2, 2)),
        ],
    )
    return pl.pallas_call(
        partial(ffn_kernel, ups, downs, aligned),
        grid_spec=spec,
        out_shape=[jax.ShapeDtypeStruct((n, d), BF16), jax.ShapeDtypeStruct((n, d), F32)]
        + [g[1] for g in grad_specs],
        compiler_params=params(60),
        cost_estimate=cost(12 * n * d * hidden, 8 * d * hidden + 14 * n * d),
        name="ffn",
    )(place, h, cot, mid, *args)


def qkv_grad_kernel(groups, place, h_ref, dq_ref, dkv_ref, rkv_ref, keep_ref, send_ref, sum_ref):
    h = h_ref[...]
    my_index = place[1]
    keep_ref[0], send_ref[0] = split_pairs(dot_tn(h, dq_ref[...]).astype(BF16), groups, my_index)
    for t in range(2):
        grad = (dkv_ref[t].astype(F32) + rkv_ref[t].astype(F32)).astype(BF16)
        sum_ref[t] = grad
        keep_ref[t + 1], send_ref[t + 1] = split_pairs(dot_tn(h, grad).astype(BF16), groups, my_index)


def qkv_grad_call(place, h, dq, dkv, rkv, groups):
    n, d = h.shape
    width = dq.shape[1]
    rows = d // (2 * groups)
    heads = width // GROUP_WIDTH
    pair = pl.BlockSpec((2, n, GROUP_WIDTH), lambda g, *_: (0, 0, g))
    share = pl.BlockSpec((3, groups, rows, GROUP_WIDTH), lambda g, *_: (g, 0, 0, 0))
    out = jax.ShapeDtypeStruct((3 * heads, groups, rows, GROUP_WIDTH), BF16)
    spec = pltpu.PrefetchScalarGridSpec(
        num_scalar_prefetch=1,
        grid=(heads,),
        in_specs=[resident((n, d)), pl.BlockSpec((n, GROUP_WIDTH), lambda g, *_: (0, g)), pair, pair],
        out_specs=[share, share, pair],
    )
    return pl.pallas_call(
        partial(qkv_grad_kernel, groups),
        grid_spec=spec,
        out_shape=[out, out, jax.ShapeDtypeStruct((2, n, width), BF16)],
        compiler_params=params(40),
        cost_estimate=cost(6 * n * d * width, 6 * d * width + 2 * n * d + 8 * n * width),
        name="qkv_grad",
    )(place, h, dq, dkv, rkv)


def head_back_kernel(weights, count, place, *refs):
    dqs, dkvs = refs[:count], refs[count : 2 * count]
    x_ref, gr_ref, gain_ref = refs[2 * count : 2 * count + 3]
    parts, refs = cut(refs[2 * count + 3 :], weights)
    tg_ref, dln_ref, wq, wk, wv, sem = refs
    load_all(weights, parts, place, (wq, wk, wv), sem)
    i = pl.program_id(0)
    dq = jnp.concatenate([r[...] for r in dqs], axis=1)
    dk = jnp.concatenate([r[0] for r in dkvs], axis=1)
    dv = jnp.concatenate([r[1] for r in dkvs], axis=1)
    grad = dot_nt(dq, wq[...]) + dot_nt(dk, wk[...]) + dot_nt(dv, wv[...])
    hat, scale = normed(x_ref[...].astype(F32))
    tg_ref[...] = (gr_ref[...] + norm_back(grad, gain_ref[...], hat, scale)).astype(BF16)
    dgain = jnp.sum(grad * hat, axis=0, keepdims=True)
    dbias = jnp.sum(grad, axis=0, keepdims=True)

    @pl.when(i == 0)
    def _():
        dln_ref[0:1, :] = dgain
        dln_ref[1:2, :] = dbias

    @pl.when(i > 0)
    def _():
        dln_ref[0:1, :] += dgain
        dln_ref[1:2, :] += dbias


def head_back_call(place, dqs, dkvs, x, gr, weights, gain):
    n, d = x.shape
    row = pl.BlockSpec((ROWS, d), lambda i, *_: (i, 0))
    specs, args = weight_args(weights)
    spec = pltpu.PrefetchScalarGridSpec(
        num_scalar_prefetch=1,
        grid=(n // ROWS,),
        in_specs=[pl.BlockSpec((ROWS, a.shape[1]), lambda i, *_: (i, 0)) for a in dqs]
        + [pl.BlockSpec((2, ROWS, a.shape[2]), lambda i, *_: (0, i, 0)) for a in dkvs]
        + [row, row, resident((1, d))]
        + specs,
        out_specs=[row, pl.BlockSpec((2, d), lambda *_: (0, 0))],
        scratch_shapes=[pltpu.VMEM((d, d), BF16)] * 3 + [pltpu.SemaphoreType.DMA((3,))],
    )
    return pl.pallas_call(
        partial(head_back_kernel, weights, len(dqs)),
        grid_spec=spec,
        out_shape=[jax.ShapeDtypeStruct((n, d), BF16), jax.ShapeDtypeStruct((2, d), F32)],
        compiler_params=params(48),
        cost_estimate=cost(6 * n * d * d, 6 * d * d + 14 * n * d),
        name="qkv_back",
    )(place, *dqs, *dkvs, x, gr, gain, *args)


class Term:
    def __init__(self, array, axes, first=0, count=None):
        self.array, self.axes, self.first = array, axes, first
        self.count = array.shape[0] if count is None else count
        self.whole = first % self.count != 0

    def spec(self, settled, flipped, open_bits, steps_bits):
        def index_map(step, mine):
            at = [0 if self.whole else self.first // self.count]
            for b in self.axes:
                if (flipped >> b) & 1:
                    at.append(1 - mine[b])
                elif b in settled:
                    at.append(mine[b])
                elif b in steps_bits:
                    at.append((step >> (len(steps_bits) - 1 - steps_bits.index(b))) & 1)
                else:
                    at.append(0)
            return (*at, 0, 0)

        lead = self.array.shape[0] if self.whole else self.count
        inner = tuple(2 if b in open_bits and b not in steps_bits else None for b in self.axes)
        return pl.BlockSpec((lead,) + inner + self.array.shape[-2:], index_map)

    def read(self, ref):
        start = self.first if self.whole else 0
        return ref[start : start + self.count].astype(F32)


class Cube:
    def __init__(self, dp, index, order):
        self.bits = dp.bit_length() - 1
        self.dp, self.order, self.mib = dp, order, 40
        self.mine = ((index >> jnp.arange(self.bits, dtype=jnp.int32)) & 1).astype(jnp.int32)

    def send(self, array, flip):
        return lax.ppermute(array, "dp", [(i, i ^ flip) for i in range(self.dp)])

    def far(self, low=2):
        return [f << low for f in range(1, 1 << (self.bits - low))]

    def terms(self, arrays, first=0, count=None):
        made = []
        for array in arrays:
            lead, _, rows, width = array.shape
            shape = (lead,) + (2,) * self.bits + (rows, width)
            made.append(Term(array.reshape(shape), list(range(self.bits))[::-1], first, count))
        return made

    def add(self, outputs, dtype):
        in_specs, args, plan, out_specs, out_shape = [], [], [], [], []
        for output in outputs:
            lead = 0
            for stream, settled, flipped in output:
                open_bits = [b for b in range(self.bits)[::-1] if b not in settled and not (flipped >> b) & 1]
                steps_bits = open_bits[:STEP_BITS]
                for term in stream:
                    in_specs.append(term.spec(settled, flipped, open_bits, steps_bits))
                    args.append(term.array)
                plan.append((len(out_specs), lead, list(stream)))
                lead += stream[0].count
            outer, inner = len(steps_bits), len(open_bits) - len(steps_bits)

            def out_map(step, mine, outer=outer, inner=inner):
                return (0, *[(step >> (outer - 1 - k)) & 1 for k in range(outer)], *[0] * inner, 0, 0)

            shape = output[0][0][0].array.shape[-2:]
            out_specs.append(pl.BlockSpec((lead,) + (None,) * outer + (2,) * inner + shape, out_map))
            out_shape.append(jax.ShapeDtypeStruct((lead,) + (2,) * (outer + inner) + shape, dtype))

        def kernel(mine, *refs):
            ins, outs = refs[: len(args)], refs[len(args) :]
            at = 0
            for out, first, stream in plan:
                total = stream[0].read(ins[at])
                for k in range(1, len(stream)):
                    total = total + stream[k].read(ins[at + k])
                outs[out][first : first + stream[0].count] = total.astype(dtype)
                at += len(stream)

        spec = pltpu.PrefetchScalarGridSpec(
            num_scalar_prefetch=1, grid=(2**outer,), in_specs=in_specs, out_specs=out_specs
        )
        size = sum(math.prod(o.shape) for o in out_shape)
        call = pl.pallas_call(
            kernel,
            grid_spec=spec,
            out_shape=out_shape,
            compiler_params=params(self.mib),
            cost_estimate=cost(4 * size, 8 * size),
            name="add_terms",
        )
        return self.order.run(call, self.mine, *args)


def join(cube, parts, streams):
    done = list(range(cube.bits))
    count, rows, width = parts[0].shape
    terms = [term for stream in streams for term in stream]

    def kernel(mine, *refs):
        outs = refs[len(parts) + len(terms) :]
        for k in range(len(parts)):
            for t, out in enumerate(outs):
                out[:, k * width : (k + 1) * width] = refs[k][t]
        at = len(parts)
        for k, stream in enumerate(streams):
            total = stream[0].read(refs[at])
            for m in range(1, len(stream)):
                total = total + stream[m].read(refs[at + m])
            at += len(stream)
            column = (len(parts) + k) * width
            for t, out in enumerate(outs):
                out[:, column : column + width] = total[t]

    whole = (rows, (len(parts) + len(streams)) * width)
    spec = pltpu.PrefetchScalarGridSpec(
        num_scalar_prefetch=1,
        grid=(1,),
        in_specs=[pl.BlockSpec(p.shape, lambda *_: (0, 0, 0)) for p in parts]
        + [term.spec(done, 0, [], []) for term in terms],
        out_specs=[pl.BlockSpec(whole, lambda *_: (0, 0))] * count,
    )
    call = pl.pallas_call(
        kernel,
        grid_spec=spec,
        out_shape=[jax.ShapeDtypeStruct(whole, F32)] * count,
        compiler_params=params(62),
        cost_estimate=cost(4 * count * rows, 8 * count * rows),
        name="join_terms",
    )
    return cube.order.run(call, cube.mine, *parts, *[term.array for term in terms])


def merge(arrays, outputs, *awaited):
    d = arrays[0].shape[-1]
    shapes = []
    for output in outputs:
        blocks = sum(arrays[i].shape[0] for i, _, _ in output)
        shapes.append(jax.ShapeDtypeStruct((blocks, output[0][2], d), BF16))

    def kernel(*refs):
        ins, outs = refs[: len(arrays)], refs[len(arrays) + len(awaited) :]
        for out, output in zip(outs, outputs, strict=True):
            at = 0
            for i, first, count in output:
                blocks = ins[i].shape[0]
                out[at : at + blocks] = ins[i][:, first : first + count]
                at += blocks

    whole = pl.BlockSpec(memory_space=pltpu.VMEM)
    size = sum(math.prod(shape.shape) for shape in shapes)
    return pl.pallas_call(
        kernel,
        in_specs=[whole] * len(arrays) + [HBM] * len(awaited),
        out_specs=[whole] * len(outputs),
        out_shape=shapes,
        compiler_params=params(40),
        cost_estimate=cost(size, 4 * size),
        name="merge",
    )(*arrays, *awaited)


class Side:
    def __init__(self, cube, order):
        self.cube, self.order = cube, order

    def hold(self, held, bit):
        self.held = held
        self.got = self.cube.send(held, 1 << bit)

    def parts_of(self):
        last = 1 << self.order[1]
        flips = [0] + self.cube.far()
        flips = flips + [f ^ (1 << self.order[0]) for f in flips]
        moved = [f ^ last for f in flips]
        return [(flips, 0), (moved, 0), (flips, 1), (moved, 1)]

    def index(self, flip):
        first, last = self.order
        return (flip >> 2) + (((flip >> first) & 1) << (self.cube.bits - 2)), (flip >> last) & 1


class Gather:
    def __init__(self, cube, order, exchange, one, two):
        self.cube, self.order, self.exchange = cube, order, exchange
        self.rows = one.shape[0]
        self.local = jnp.concatenate([one, two], axis=0)[None]
        self.sides = (Side(cube, (1, 0)), Side(cube, (0, 1)))

    def far(self):
        local = self.order.after(self.local)
        self.pieces = [local] + [self.cube.send(local, f) for f in self.cube.far()]
        self.order.note(local)

    def near(self, *awaited):
        total = self.local.shape[1]
        outputs = [
            [(i, first, count) for i in range(len(self.pieces))]
            for first, count in ((0, self.rows), (self.rows, total - self.rows))
        ]
        held = self.order.run(lambda first, *rest: merge((first, *rest), outputs, *awaited), *self.pieces)
        for s, array in zip(self.sides, held, strict=True):
            s.hold(array, s.order[0])

    def last(self, *awaited):
        arrays = [a for s in self.sides for a in (s.held, s.got)]
        outputs = [[(i, 0, arrays[i].shape[1]), (i + 1, 0, arrays[i].shape[1])] for i in (0, 2)]
        held = self.order.run(lambda first, *rest: merge((first, *rest), outputs, *awaited), *arrays)
        for s, array in zip(self.sides, held, strict=True):
            s.hold(array, s.order[1])

    def cross(self):
        for s in self.sides:
            s.other = self.exchange(self.order.after(s.held))

    def finish(self):
        for s in self.sides:
            s.rest = self.exchange(self.order.after(s.got))

    def ready(self):
        for s in self.sides:
            s.buffers = [s.held, s.got, s.other, s.rest]
            s.parts = s.parts_of()


class Order:
    def __init__(self):
        self.token = ()

    def after(self, *values):
        if self.token:
            values = lax.optimization_barrier((values, self.token))[0]
        return values if len(values) > 1 else values[0]

    def note(self, *token):
        self.token = token

    def run(self, call, first, *rest):
        out = call(self.after(first), *rest)
        self.note(jax.tree.leaves(out)[0])
        return out


class Scatter:
    def __init__(self, cube, one, two, direct):
        self.cube, self.sides, self.step, self.direct = cube, (one, two), 0, direct
        self.sent, self.last = [], []

    def advance(self):
        step, cube = self.step, self.cube
        if step < 2:
            flips = (1 << step, 1 << (1 - step))
            done = ([], []) if step == 0 else ([0], [1])
            self.sent = cube.add(
                [[(stream, done[s], flips[s]) for stream in self.sides[s]] for s in range(2)], BF16
            )
            self.last = []
            for s in range(2):
                got = cube.send(self.sent[s], flips[s])
                self.last.append(got)
                axes = [b for b in range(cube.bits)[::-1] if b not in done[s] and not (flips[s] >> b) & 1]
                at = 0
                for stream in self.sides[s]:
                    stream.append(Term(got, axes, at, stream[0].count))
                    at += stream[0].count
        else:
            streams = [stream for side in self.sides for stream in side]
            if self.direct:
                done, flips = list(range(cube.bits)), cube.far()
            else:
                done, flips = list(range(step)), [1 << step]
            self.sent = cube.add([[(stream, done, f) for stream in streams] for f in flips], BF16)
            self.last = [cube.send(sent, f) for sent, f in zip(self.sent, flips, strict=True)]
            axes = [] if self.direct else list(range(step + 1, cube.bits))[::-1]
            for got in self.last:
                at = 0
                for stream in streams:
                    stream.append(Term(got, axes, at, stream[0].count))
                    at += stream[0].count
        self.step += 1
        return self

    def finish(self):
        while self.step < (3 if self.direct else self.cube.bits):
            self.advance()
        done = list(range(self.cube.bits))
        return self.cube.add([[(stream, done, 0)] for side in self.sides for stream in side], F32)


def gate(value, *others):
    return lax.optimization_barrier((value, others))[0]


def block_table(seg_full, seg_local, my_index, bq, bk):
    first, last = seg_local[::bq], seg_local[bq - 1 :: bq]
    low = jnp.sum((seg_full[None, :] < first[:, None]).astype(jnp.int32), axis=1)
    high = jnp.sum((seg_full[None, :] <= last[:, None]).astype(jnp.int32), axis=1)
    start = low // ROW_ALIGN * ROW_ALIGN
    table = jnp.stack([start, (high - start + bk - 1) // bk], axis=1).reshape(-1)
    return jnp.concatenate([table, my_index[None]]).astype(jnp.int32)


def body(
    tokens,
    segments,
    ln1_gain,
    ln1_bias,
    w_query,
    w_key,
    w_value,
    w_out,
    ln2_gain,
    ln2_bias,
    w_up,
    w_down,
    cotangent,
):
    x = tokens[0]
    n, d = x.shape
    cot = cotangent[0]
    rows = w_query.shape[0]
    devices = d // rows
    hidden = w_up.shape[1]
    per_device = hidden // devices
    my_index = lax.axis_index("seq")
    seg_full = segments[0]
    seg_local = lax.dynamic_slice_in_dim(seg_full, my_index * n, n)
    tab = block_table(seg_full, seg_local, my_index, ATT_Q, ATT_K)
    tab_back = block_table(seg_full, seg_local, my_index, ATT_Q, BACK_K)
    seg_q = seg_local.reshape(n // ATT_Q, 1, ATT_Q)
    seg_col = jnp.pad(seg_full, (0, max(ATT_K, BACK_K)), constant_values=-1)[:, None]

    dp = devices // 2
    dp_index = lax.axis_index("dp")
    order = Order()
    cube = Cube(dp, dp_index, order)
    place = jnp.stack([dp_index, my_index]).astype(jnp.int32)
    swap = [(0, 1), (1, 0)]
    tiles = hidden // d

    def exchange(value):
        return lax.ppermute(value, "seq", swap)

    def halves(value, axis):
        keep = lax.dynamic_index_in_dim(value, my_index, axis, keepdims=False)
        send = lax.dynamic_index_in_dim(value, 1 - my_index, axis, keepdims=False)
        return keep, send

    vectors = jnp.concatenate([ln1_gain, ln1_bias, ln2_gain, ln2_bias]).astype(F32)
    vectors = jnp.broadcast_to(vectors[None], (devices, 4 * rows))
    vectors = lax.all_to_all(vectors, BOTH, 0, 0, tiled=True)
    ln = vectors.reshape(devices, 4, rows).transpose(1, 0, 2).reshape(4, 1, d)

    aligned = rows % 32 == 0
    groups = d // GROUP_WIDTH
    if aligned:
        cut_row, half_down = rows // 2, per_device // 2
        up_tiles = w_up.reshape(rows, tiles, d).transpose(1, 0, 2)
        half_up = tiles // 2 * rows
        low_up, high_up = (u.reshape(half_up, d) for u in (up_tiles[: tiles // 2], up_tiles[tiles // 2 :]))
        head = Gather(
            cube, order, exchange,
            jnp.concatenate([w_key, w_query[:cut_row]]), jnp.concatenate([w_value, w_query[cut_row:]]),
        )
        low = Gather(
            cube, order, exchange,
            jnp.concatenate([low_up, w_out[:cut_row]]), jnp.concatenate([w_down[:half_down], w_out[cut_row:]]),
        )
        high = Gather(cube, order, exchange, high_up, w_down[half_down:])
        head.far()
        head.near(vectors, seg_col, seg_q, tab, tab_back)
        low.far()
        head.last()
        head.cross()
        order.note(*[side.got for side in head.sides])
        head.finish()
        head.ready()
        low.near()
        key_w = Spread(rows, [(head.sides[0], 0, rows, 0)])
        value_w = Spread(rows, [(head.sides[1], 0, rows, 0)])
        query_w = Spread(rows, [(head.sides[0], rows, cut_row, 0), (head.sides[1], rows, cut_row, cut_row)])
    else:
        every = jnp.concatenate([w_query, w_key, w_value, w_out], axis=0).reshape(4, rows, d)
        every = lax.all_gather(every, BOTH, axis=1, tiled=True)
        query_w, key_w, value_w, out_w = (Plain(every[t], rows) for t in range(4))
        up_all = lax.all_gather(w_up, BOTH, axis=0, tiled=True)
        ups = [Plain(up_all[:, t * d : (t + 1) * d], rows) for t in range(tiles)]
        downs = [Plain(lax.all_gather(w_down, BOTH, axis=0, tiled=True), per_device)]

    h1, own = order.run(kv_call, place, x, ln[0], ln[1], [key_w, value_w])
    if aligned:
        low.last()
    other = exchange(order.after(own))
    q = order.run(q_call, place, h1, [query_w])
    if aligned:
        high.far()
    outs, lses = [], []
    plan = [(0, 2), (2, 1), (3, 1)] if groups == 4 else [(g, 1) for g in range(groups)]
    for i, (start, count) in enumerate(plan):
        if aligned and i == 1:
            high.near()
            low.finish()
        if aligned and i == 2:
            high.last(*[side.rest for side in low.sides])
            low.cross()
        out, lse = order.run(
            attend_call, tab, q, own, other, seg_q, seg_col, ATT_Q, ATT_K, start, count
        )
        outs.append(out)
        lses.append(lse)
    if aligned:
        low.ready()
        high.cross()
        out_w = Spread(
            rows, [(low.sides[0], half_up, cut_row, 0), (low.sides[1], half_down, cut_row, cut_row)]
        )
    mid, h2 = order.run(mid_call, place, x, outs, [out_w], ln[2], ln[3])
    if aligned:
        high.finish()
        high.ready()

    up_rows = tiles * rows
    if aligned:
        ups = [
            Spread(rows, [((low, high)[t // (tiles // 2)].sides[0], t % (tiles // 2) * rows, rows, 0)])
            for t in range(tiles)
        ]
        downs = [Spread(half_down, [(r.sides[1], 0, half_down, 0)]) for r in (low, high)]
        per_tile = d // FF_COLS
        group = FF_COLS // per_device
        up_out = (
            pl.BlockSpec((None, dp, rows, FF_COLS), lambda j, *_: (j // per_tile, 0, 0, j % per_tile)),
            jax.ShapeDtypeStruct((tiles, dp, rows, d), BF16),
        )
        down_out = (
            pl.BlockSpec((tiles, group // 2, rows, d), lambda j, *_: (0, j, 0, 0)),
            jax.ShapeDtypeStruct((tiles, dp, rows, d), BF16),
        )
        grad_specs = [up_out, up_out, down_out, down_out]
    else:
        grad_specs = [
            (pl.BlockSpec((d, FF_COLS), lambda j, *_: (0, j)), jax.ShapeDtypeStruct((d, hidden), BF16)),
            (pl.BlockSpec((FF_COLS, d), lambda j, *_: (j, 0)), jax.ShapeDtypeStruct((hidden, d), BF16)),
        ]
    mixed, gmid, *grads = order.run(ffn_call, place, h2, cot, ups, downs, mid, grad_specs, hidden, aligned)
    if not aligned:
        dwu = grads[0].reshape(dp, 2, rows, tiles, d).transpose(3, 0, 1, 2, 4)
        dwd = grads[1].reshape(dp, 2, tiles, rows, d).transpose(2, 0, 1, 3, 4)
        grads = [*halves(dwu, 2), *halves(dwd, 2)]
    keep_up, send_up, keep_down, send_down = grads
    got_up, got_down = exchange(send_up), exchange(send_down)
    big = Scatter(cube, [cube.terms([keep_up, got_up])], [cube.terms([keep_down, got_down])], False)

    grad_mid, grad_att, keep_out, send_out, dln2 = order.run(
        mid_back_call, place, gmid, mid, cot, outs, [out_w], ln[2], dp
    )
    big.advance()
    got_out = exchange(order.after(send_out))
    dqs, dkvs = [], []

    def attend_back(g):
        which = [i for i, (start, _) in enumerate(plan) if start <= g][-1]
        return order.run(
            attend_back_call, tab_back, q, grad_att, outs[which], own, other, seg_q, seg_col,
            lses[which], ATT_Q, BACK_K, g, 1, g - plan[which][0],
        )

    def finish_group(dq, dkv, got):
        keep, send, dkv = order.run(qkv_grad_call, place, h1, dq, dkv, got, dp)
        dqs.append(dq)
        dkvs.append(dkv)
        return keep, send

    dq_0, dkv_0, sent_0 = attend_back(0)
    got_0 = exchange(sent_0)
    dq_1, dkv_1, sent_1 = attend_back(1)
    keep_0, send_0 = finish_group(dq_0, dkv_0, got_0)
    big.advance()
    got_1 = exchange(order.after(sent_1))
    keep_1, send_1 = finish_group(dq_1, dkv_1, got_1)
    terms_0, terms_1 = [keep_0, exchange(order.after(send_0))], [keep_1, exchange(order.after(send_1))]
    dq_2, dkv_2, sent_2 = attend_back(2)
    big.advance()
    tail_one = Scatter(
        cube,
        [cube.terms(terms_0), cube.terms([keep_out, got_out], 0, 2)],
        [cube.terms(terms_1), cube.terms([keep_out, got_out], 2, 2)],
        False,
    )
    tail_one.advance()
    got_2 = exchange(order.after(sent_2))
    dq_3, dkv_3, sent_3 = attend_back(3)
    big.advance()
    tail_one.advance()
    got_3 = exchange(order.after(sent_3))
    keep_2, send_2 = finish_group(dq_2, dkv_2, got_2)
    keep_3, send_3 = finish_group(dq_3, dkv_3, got_3)
    tail_one.advance()
    terms_2, terms_3 = [keep_2, exchange(order.after(send_2))], [keep_3, exchange(order.after(send_3))]
    tail_two = Scatter(cube, [cube.terms(terms_2)], [cube.terms(terms_3)], True)
    tail_two.advance()
    token_grad, dln1 = order.run(
        head_back_call, place, dqs, dkvs, x, grad_mid, [query_w, key_w, value_w], ln[0]
    )
    cube.mib = 62
    tail_two.advance()
    tail_one.advance()
    tail_two.advance()
    up_share, down_share = big.finish()
    one_a, out_a, one_b, out_b = tail_one.finish()
    dln = jnp.concatenate([dln1, gate(dln2, *tail_two.last)], axis=0).reshape(4, devices, rows).transpose(1, 0, 2)
    dln = lax.all_to_all(dln.reshape(devices, 4 * rows), BOTH, 0, 0, tiled=True)
    dln = jnp.sum(dln.reshape(devices, 4, rows), axis=0)
    qkv_share = join(cube, [one_a, one_b], [stream for side in tail_two.sides for stream in side])

    up_share = up_share.transpose(1, 0, 2).reshape(rows, hidden)
    down_share = down_share.reshape(per_device, d)
    out_share = jnp.concatenate([out_a, out_b], axis=0).transpose(1, 0, 2).reshape(rows, d)
    return (
        mixed[None],
        token_grad[None],
        dln[0],
        dln[1],
        qkv_share[0],
        qkv_share[1],
        qkv_share[2],
        out_share,
        dln[2],
        dln[3],
        up_share,
        down_share,
    )


def solution(mesh):
    row, act, vec = P(BOTH, None), P("dp", "seq", None), P(BOTH)
    in_specs = (act, P("dp", None), vec, vec, row, row, row, row, vec, vec, row, row, act)
    out_specs = (act, act, vec, vec, row, row, row, row, vec, vec, row, row)
    return jax.shard_map(body, mesh=mesh, in_specs=in_specs, out_specs=out_specs, check_vma=False)
```

```python
import math
from functools import partial

import jax
import jax.numpy as jnp
from jax import lax
from jax.experimental import pallas as pl
from jax.experimental.pallas import tpu as pltpu
from jax.sharding import PartitionSpec as P

BF16 = jnp.bfloat16
F32 = jnp.float32
HEAD_DIM = 64
GROUP = 4
GROUP_WIDTH = GROUP * HEAD_DIM
NEG = -1000000000.0
BOTH = ("dp", "seq")
ATT_Q = 256
ATT_K = 512
BACK_K = 256
ROW_ALIGN = 16
ROWS = 512
FF_COLS = 512
COST_SCALE = 100000
STEP_BITS = 1


def dot_nn(left, right):
    return lax.dot_general(left, right, (((1,), (0,)), ((), ())), preferred_element_type=F32)


def dot_nt(left, right):
    return lax.dot_general(left, right, (((1,), (1,)), ((), ())), preferred_element_type=F32)


def dot_tn(left, right):
    return lax.dot_general(left, right, (((0,), (0,)), ((), ())), preferred_element_type=F32)


def params(mib):
    return pltpu.CompilerParams(vmem_limit_bytes=mib << 20)


def cost(flops, nbytes, scale=None):
    if scale:
        return pl.CostEstimate(flops=scale * flops, bytes_accessed=scale * nbytes, transcendentals=0)
    return pl.CostEstimate(flops=flops // COST_SCALE, bytes_accessed=nbytes // COST_SCALE, transcendentals=0)


def normed(values):
    centre = values - jnp.mean(values, axis=-1, keepdims=True)
    scale = lax.rsqrt(jnp.mean(centre * centre, axis=-1, keepdims=True) + 1e-05)
    return centre * scale, scale


def norm_back(grad, gain_vec, hat, scale):
    inner = grad * gain_vec
    return scale * (
        inner
        - jnp.mean(inner, axis=-1, keepdims=True)
        - hat * jnp.mean(inner * hat, axis=-1, keepdims=True)
    )


def flat(ref):
    value = ref[...]
    return value.reshape(-1, value.shape[-1])


def resident(shape):
    zeros = (0,) * len(shape)
    return pl.BlockSpec(shape, lambda *_: zeros, pipeline_mode=pl.Buffered(1))


class Spread:
    def __init__(self, block, pieces):
        self.block, self.pieces = block, pieces
        self.args = [b for rounds, *_ in pieces for b in rounds.buffers]

    def start(self, refs, place, target, sem, columns=None):
        for i, (rounds, first, count, at) in enumerate(self.pieces):
            for ref, (flips, core) in zip(refs[4 * i : 4 * i + 4], rounds.parts, strict=True):
                for e, flip in enumerate(flips):
                    device = (place[0] ^ flip) * 2 + (place[1] ^ core)
                    row = pl.multiple_of(device * self.block + at, count)
                    source = ref.at[e, pl.ds(first, count)]
                    if columns is not None:
                        source = ref.at[e, pl.ds(first, count), columns]
                    pltpu.make_async_copy(source, target.at[pl.ds(row, count), :], sem).start()

    def start_rows(self, refs, place, target, sem, first, group):
        ((rounds, begin, count, _),) = self.pieces
        for k in range(group):
            device = first + k
            flip = (device // 2) ^ place[0]
            at, last = rounds.index(flip)
            core = (device % 2) ^ place[1]
            for i, ref in enumerate(refs):

                @pl.when((last == i % 2) & (core == i // 2))
                def _(ref=ref, at=at, k=k):
                    pltpu.make_async_copy(
                        ref.at[at, pl.ds(begin, count)], target.at[pl.ds(k * count, count), :], sem
                    ).start()


class Plain:
    def __init__(self, array, block):
        self.args, self.block = [array], block

    def start(self, refs, place, target, sem, columns=None):
        source = refs[0] if columns is None else refs[0].at[:, columns]
        pltpu.make_async_copy(source, target, sem).start()

    def start_rows(self, refs, place, target, sem, first, group):
        pltpu.make_async_copy(refs[0].at[pl.ds(first * self.block, group * self.block), :], target, sem).start()


def arrived(target, sem):
    pltpu.make_async_copy(target, target, sem).wait()


def cut(refs, weights):
    parts = []
    for weight in weights:
        parts.append(refs[: len(weight.args)])
        refs = refs[len(weight.args) :]
    return parts, refs


def load_all(weights, parts, place, targets, sem, wait=True):
    @pl.when(pl.program_id(0) == 0)
    def _():
        for i, weight in enumerate(weights):
            weight.start(parts[i], place, targets[i], sem.at[i])
        if wait:
            for i in range(len(weights)):
                arrived(targets[i], sem.at[i])


def loaded(targets, sem, i):
    @pl.when(pl.program_id(0) == 0)
    def _():
        arrived(targets[i], sem.at[i])

    return targets[i][...]


HBM = pl.BlockSpec(memory_space=pltpu.HBM)


def weight_args(weights):
    args = [a for w in weights for a in w.args]
    return [HBM] * len(args), args


def kv_kernel(weights, place, x_ref, gain_ref, bias_ref, *refs):
    parts, refs = cut(refs, weights)
    h_ref, kv_ref, wk, wv, sem = refs
    load_all(weights, parts, place, (wk, wv), sem)
    hat, _ = normed(x_ref[...].astype(F32))
    low = (hat * gain_ref[...] + bias_ref[...]).astype(BF16)
    h_ref[...] = low
    kv_ref[0] = dot_nn(low, wk[...]).astype(BF16)
    kv_ref[1] = dot_nn(low, wv[...]).astype(BF16)


def kv_call(place, x, gain, bias, weights):
    n, d = x.shape
    row = pl.BlockSpec((ROWS, d), lambda i, *_: (i, 0))
    specs, args = weight_args(weights)
    spec = pltpu.PrefetchScalarGridSpec(
        num_scalar_prefetch=1,
        grid=(n // ROWS,),
        in_specs=[row, resident((1, d)), resident((1, d))] + specs,
        out_specs=[row, pl.BlockSpec((2, ROWS, d), lambda i, *_: (0, i, 0))],
        scratch_shapes=[pltpu.VMEM((d, d), BF16)] * 2 + [pltpu.SemaphoreType.DMA((2,))],
    )
    return pl.pallas_call(
        partial(kv_kernel, weights),
        grid_spec=spec,
        out_shape=[jax.ShapeDtypeStruct((n, d), BF16), jax.ShapeDtypeStruct((2, n, d), BF16)],
        compiler_params=params(40),
        cost_estimate=cost(4 * n * d * d, 4 * d * d + 8 * n * d),
        name="kv_proj",
    )(place, x, gain, bias, *args)


def q_kernel(weights, place, h_ref, *refs):
    parts, refs = cut(refs, weights)
    q_ref, wq, sem = refs
    load_all(weights, parts, place, (wq,), sem)
    q_ref[...] = (dot_nn(h_ref[...], wq[...]).astype(BF16).astype(F32) * 0.125).astype(BF16)


def q_call(place, h, weights):
    n, d = h.shape
    row = pl.BlockSpec((ROWS, d), lambda i, *_: (i, 0))
    specs, args = weight_args(weights)
    spec = pltpu.PrefetchScalarGridSpec(
        num_scalar_prefetch=1,
        grid=(n // ROWS,),
        in_specs=[row] + specs,
        out_specs=row,
        scratch_shapes=[pltpu.VMEM((d, d), BF16), pltpu.SemaphoreType.DMA((1,))],
    )
    return pl.pallas_call(
        partial(q_kernel, weights),
        grid_spec=spec,
        out_shape=jax.ShapeDtypeStruct((n, d), BF16),
        compiler_params=params(32),
        cost_estimate=cost(2 * n * d * d, 2 * d * d + 4 * n * d),
        name="q_proj",
    )(place, h, *args)


def stack_heads(block):
    lane = lax.broadcasted_iota(jnp.int32, block.shape, 1) // HEAD_DIM
    zero = jnp.zeros_like(block)
    return jnp.concatenate([jnp.where(lane == h, block, zero) for h in range(GROUP)], axis=0)


def head_cols(value, h, width):
    return value[:, h * width : (h + 1) * width]


def head_rows(value, h):
    return value[h * HEAD_DIM : (h + 1) * HEAD_DIM, :]


def line_up(target, own_ref, other_ref, which, mine):
    n = own_ref.shape[1]
    target[pl.ds(pl.multiple_of(mine * n, n), n), :] = own_ref[which]
    target[pl.ds(pl.multiple_of((1 - mine) * n, n), n), :] = other_ref[which]
    target[2 * n :, :] = jnp.zeros((target.shape[0] - 2 * n, target.shape[1]), target.dtype)


def attend_kernel(bq, bk, tab, q_ref, own_ref, other_ref, sq_ref, s_ref, o_ref, lse_ref, k_s, v_s):
    i = pl.program_id(1)

    @pl.when(i == 0)
    def _():
        mine = tab[2 * pl.num_programs(1)]
        line_up(k_s, own_ref, other_ref, 0, mine)
        line_up(v_s, own_ref, other_ref, 1, mine)

    stacked = stack_heads(q_ref[...])
    seg_q = jnp.concatenate([sq_ref[0]] * GROUP, axis=1)
    first = tab[2 * i]

    def step(j, carry):
        top, total, acc = carry
        at = pl.multiple_of(first + j * bk, ROW_ALIGN)
        scores = dot_nt(k_s[pl.ds(at, bk), :], stacked)
        scores = jnp.where(s_ref[pl.ds(at, bk), :] == seg_q, scores, NEG)
        new_top = jnp.maximum(top, jnp.max(scores, axis=0, keepdims=True))
        decay = jnp.exp(top - new_top)
        probs = jnp.exp(scores - new_top)
        total = total * decay + jnp.sum(probs, axis=0, keepdims=True)
        low = probs.astype(BF16)
        values = v_s[pl.ds(at, bk), :].T
        acc = tuple(
            acc[h] * head_cols(decay, h, bq) + dot_nn(head_rows(values, h), head_cols(low, h, bq))
            for h in range(GROUP)
        )
        return new_top, total, acc

    state = (
        jnp.full((1, GROUP * bq), -jnp.inf, F32),
        jnp.zeros((1, GROUP * bq), F32),
        tuple(jnp.zeros((HEAD_DIM, bq), F32) for _ in range(GROUP)),
    )
    top, total, acc = lax.fori_loop(0, tab[2 * i + 1], step, state)
    out = jnp.concatenate([acc[h] / head_cols(total, h, bq) for h in range(GROUP)], axis=0)
    o_ref[...] = out.T.astype(BF16)
    lse_ref[0, 0] = top + jnp.log(total)


def attend_specs(n, bq, padded, first):
    def half(_):
        return pl.BlockSpec((2, n, GROUP_WIDTH), lambda g, i, *_: (0, 0, g + first))

    return [
        half(0),
        half(1),
        pl.BlockSpec((1, 1, bq), lambda g, i, *_: (i, 0, 0)),
        pl.BlockSpec((padded, 1), lambda *_: (0, 0)),
    ]


def attend_call(tab, q, own, other, seg_q, seg_col, bq, bk, first, groups):
    n, d = q.shape
    blocks = n // bq
    padded = seg_col.shape[0]
    spec = pltpu.PrefetchScalarGridSpec(
        num_scalar_prefetch=1,
        grid=(groups, blocks),
        in_specs=[pl.BlockSpec((bq, GROUP_WIDTH), lambda g, i, *_: (i, g + first))]
        + attend_specs(n, bq, padded, first),
        out_specs=[
            pl.BlockSpec((bq, GROUP_WIDTH), lambda g, i, *_: (i, g)),
            pl.BlockSpec((1, 1, 1, GROUP * bq), lambda g, i, *_: (g, i, 0, 0)),
        ],
        scratch_shapes=[pltpu.VMEM((padded, GROUP_WIDTH), BF16)] * 2,
    )
    return pl.pallas_call(
        partial(attend_kernel, bq, bk),
        grid_spec=spec,
        out_shape=[
            jax.ShapeDtypeStruct((n, groups * GROUP_WIDTH), BF16),
            jax.ShapeDtypeStruct((groups, blocks, 1, GROUP * bq), F32),
        ],
        compiler_params=params(56),
        cost_estimate=cost(8_000_000_000 * groups, 3 * groups * n * d),
        name="attend",
    )(tab, q, own, other, seg_q, seg_col)


def attend_back_kernel(
    bq, bk, tab, q_ref, go_ref, o_ref, lse_ref, own_ref, other_ref, sq_ref, s_ref,
    dq_ref, down_ref, dpart_ref, k_s, v_s, dk_s, dv_s,
):
    i = pl.program_id(1)
    mine = tab[2 * pl.num_programs(1)]

    @pl.when(i == 0)
    def _():
        line_up(k_s, own_ref, other_ref, 0, mine)
        line_up(v_s, own_ref, other_ref, 1, mine)
        dk_s[...] = jnp.zeros_like(dk_s)
        dv_s[...] = jnp.zeros_like(dv_s)

    stacked = stack_heads(q_ref[...])
    grad = go_ref[...]
    stacked_grad = stack_heads(grad)
    product = (grad.astype(F32) * o_ref[...].astype(F32)).T
    inner = jnp.concatenate(
        [jnp.sum(head_rows(product, h), axis=0, keepdims=True) for h in range(GROUP)], axis=1
    )
    seg_q = jnp.concatenate([sq_ref[0]] * GROUP, axis=1)
    lse = lse_ref[0, 0]
    first = tab[2 * i]

    def step(j, acc):
        at = pl.multiple_of(first + j * bk, ROW_ALIGN)
        keys = k_s[pl.ds(at, bk), :]
        scores = dot_nt(keys, stacked)
        scores = jnp.where(s_ref[pl.ds(at, bk), :] == seg_q, scores, NEG)
        probs = jnp.exp(scores - lse)
        grad_probs = dot_nt(v_s[pl.ds(at, bk), :], stacked_grad)
        grad_scores = (probs * (grad_probs - inner)).astype(BF16)
        dv_s[pl.ds(at, bk), :] += dot_nn(probs.astype(BF16), stacked_grad)
        dk_s[pl.ds(at, bk), :] += dot_nn(grad_scores, stacked)
        keys_t = keys.T
        return tuple(
            acc[h] + dot_nn(head_rows(keys_t, h), head_cols(grad_scores, h, bq)) for h in range(GROUP)
        )

    state = tuple(jnp.zeros((HEAD_DIM, bq), F32) for _ in range(GROUP))
    state = lax.fori_loop(0, tab[2 * i + 1], step, state)
    dq_ref[...] = (jnp.concatenate(state, axis=0).T * 0.125).astype(BF16)

    @pl.when(i == pl.num_programs(1) - 1)
    def _():
        n = down_ref.shape[1]
        for ref, half in ((down_ref, mine), (dpart_ref, 1 - mine)):
            rows = pl.ds(pl.multiple_of(half * n, n), n)
            ref[0] = dk_s[rows, :].astype(BF16)
            ref[1] = dv_s[rows, :].astype(BF16)


def attend_back_call(tab, q, grad, out, own, other, seg_q, seg_col, lse, bq, bk, first, groups, out_first):
    n, d = q.shape
    blocks = n // bq
    padded = seg_col.shape[0]
    query = pl.BlockSpec((bq, GROUP_WIDTH), lambda g, i, *_: (i, g + first))
    pair = pl.BlockSpec((2, n, GROUP_WIDTH), lambda g, i, *_: (0, 0, g))
    spec = pltpu.PrefetchScalarGridSpec(
        num_scalar_prefetch=1,
        grid=(groups, blocks),
        in_specs=[
            query,
            query,
            pl.BlockSpec((bq, GROUP_WIDTH), lambda g, i, *_: (i, g + out_first)),
            pl.BlockSpec((1, 1, 1, GROUP * bq), lambda g, i, *_: (g + out_first, i, 0, 0)),
        ]
        + attend_specs(n, bq, padded, first),
        out_specs=[pl.BlockSpec((bq, GROUP_WIDTH), lambda g, i, *_: (i, g)), pair, pair],
        scratch_shapes=[pltpu.VMEM((padded, GROUP_WIDTH), BF16)] * 2
        + [pltpu.VMEM((padded, GROUP_WIDTH), F32)] * 2,
    )
    width = groups * GROUP_WIDTH
    return pl.pallas_call(
        partial(attend_back_kernel, bq, bk),
        grid_spec=spec,
        out_shape=[
            jax.ShapeDtypeStruct((n, width), BF16),
            jax.ShapeDtypeStruct((2, n, width), BF16),
            jax.ShapeDtypeStruct((2, n, width), BF16),
        ],
        compiler_params=params(56),
        cost_estimate=cost(12_000_000_000 * groups, 6 * groups * n * d),
        name="attend_back",
    )(tab, q, grad, out, lse, own, other, seg_q, seg_col)


def mid_kernel(weights, count, place, x_ref, gain_ref, bias_ref, *refs):
    outs, refs = refs[:count], refs[count:]
    parts, refs = cut(refs, weights)
    r_ref, h_ref, wo, sem = refs
    load_all(weights, parts, place, (wo,), sem)
    mid = x_ref[...].astype(F32) + dot_nn(jnp.concatenate([o[...] for o in outs], axis=1), wo[...])
    r_ref[...] = mid
    hat, _ = normed(mid)
    h_ref[...] = (hat * gain_ref[...] + bias_ref[...]).astype(BF16)


def mid_call(place, x, outs, weights, gain, bias):
    n, d = x.shape
    row = pl.BlockSpec((ROWS, d), lambda i, *_: (i, 0))
    specs, args = weight_args(weights)
    spec = pltpu.PrefetchScalarGridSpec(
        num_scalar_prefetch=1,
        grid=(n // ROWS,),
        in_specs=[row, resident((1, d)), resident((1, d))]
        + [pl.BlockSpec((ROWS, o.shape[1]), lambda i, *_: (i, 0)) for o in outs]
        + specs,
        out_specs=[row, row],
        scratch_shapes=[pltpu.VMEM((d, d), BF16), pltpu.SemaphoreType.DMA((1,))],
    )
    return pl.pallas_call(
        partial(mid_kernel, weights, len(outs)),
        grid_spec=spec,
        out_shape=[jax.ShapeDtypeStruct((n, d), F32), jax.ShapeDtypeStruct((n, d), BF16)],
        compiler_params=params(32),
        cost_estimate=cost(2 * n * d * d, 2 * d * d + 10 * n * d),
        name="out_proj",
    )(place, x, gain, bias, *outs, *args)


def mid_back_kernel(weights, count, place, gh_ref, r_ref, g_ref, gain_ref, *refs):
    outs, refs = refs[:count], refs[count:]
    parts, refs = cut(refs, weights)
    gr_ref, go_ref, keep_ref, send_ref, dln_ref, acc, wo, sem = refs
    load_all(weights, parts, place, (wo,), sem, wait=False)
    i = pl.program_id(0)
    hat, scale = normed(r_ref[...])
    grad = gh_ref[...]
    total = g_ref[...].astype(F32) + norm_back(grad, gain_ref[...], hat, scale)
    gr_ref[...] = total
    low = total.astype(BF16)
    part = dot_tn(jnp.concatenate([o[...] for o in outs], axis=1), low)
    go_ref[...] = dot_nt(low, loaded((wo,), sem, 0)).astype(BF16)
    dgain = jnp.sum(grad * hat, axis=0, keepdims=True)
    dbias = jnp.sum(grad, axis=0, keepdims=True)

    @pl.when(i == 0)
    def _():
        acc[...] = part
        dln_ref[0:1, :] = dgain
        dln_ref[1:2, :] = dbias

    @pl.when(i > 0)
    def _():
        acc[...] += part
        dln_ref[0:1, :] += dgain
        dln_ref[1:2, :] += dbias

    @pl.when(i == pl.num_programs(0) - 1)
    def _():
        lanes = keep_ref.shape[3]
        for ref, value in zip(
            (keep_ref, send_ref), split_pairs(acc[...].astype(BF16), keep_ref.shape[1], place[1]), strict=True
        ):
            for t in range(ref.shape[0]):
                ref[t] = value[:, :, t * lanes : (t + 1) * lanes]


def mid_back_call(place, grad, mid, cot, outs, weights, gain, groups):
    n, d = mid.shape
    row = pl.BlockSpec((ROWS, d), lambda i, *_: (i, 0))
    share = (d // GROUP_WIDTH, groups, d // (2 * groups), GROUP_WIDTH)
    specs, args = weight_args(weights)
    spec = pltpu.PrefetchScalarGridSpec(
        num_scalar_prefetch=1,
        grid=(n // ROWS,),
        in_specs=[row, row, row, resident((1, d))]
        + [pl.BlockSpec((ROWS, o.shape[1]), lambda i, *_: (i, 0)) for o in outs]
        + specs,
        out_specs=[
            row,
            row,
            pl.BlockSpec(share, lambda *_: (0, 0, 0, 0)),
            pl.BlockSpec(share, lambda *_: (0, 0, 0, 0)),
            pl.BlockSpec((2, d), lambda *_: (0, 0)),
        ],
        scratch_shapes=[
            pltpu.VMEM((d, d), F32),
            pltpu.VMEM((d, d), BF16),
            pltpu.SemaphoreType.DMA((1,)),
        ],
    )
    return pl.pallas_call(
        partial(mid_back_kernel, weights, len(outs)),
        grid_spec=spec,
        out_shape=[
            jax.ShapeDtypeStruct((n, d), F32),
            jax.ShapeDtypeStruct((n, d), BF16),
            jax.ShapeDtypeStruct(share, BF16),
            jax.ShapeDtypeStruct(share, BF16),
            jax.ShapeDtypeStruct((2, d), F32),
        ],
        compiler_params=params(48),
        cost_estimate=cost(4 * n * d * d, 4 * d * d + 18 * n * d),
        name="out_proj_back",
    )(place, grad, mid, cot, gain, *outs, *args)


def split_pairs(value, groups, my_index):
    rows = value.shape[0] // (2 * groups)
    pairs = value.reshape(groups, 2, rows, value.shape[1])
    even, odd = pairs[:, 0], pairs[:, 1]
    first = my_index == 0
    return jnp.where(first, even, odd), jnp.where(first, odd, even)


def ffn_grads(h, grad, wu, wd):
    up = dot_nn(h, wu)
    cdf = 0.5 * (1.0 + lax.erf(up * 0.7071067811865476))
    act = (up * cdf).astype(BF16)
    slope = cdf + up * (jnp.exp(-0.5 * up * up) * 0.3989422804014327)
    gu = (dot_nt(grad, wd) * slope).astype(BF16)
    return act, gu, dot_tn(h, gu).astype(BF16), dot_tn(act, grad).astype(BF16)


def ffn_sums(j, act, gu, wu, wd, mid_ref, mixed_ref, gh_ref, acc):
    @pl.when(j == 0)
    def _():
        acc[...] = mid_ref[...] + dot_nn(act, wd)
        gh_ref[...] = dot_nt(gu, wu)

    @pl.when(j > 0)
    def _():
        acc[...] += dot_nn(act, wd)
        gh_ref[...] += dot_nt(gu, wu)

    @pl.when(j == pl.num_programs(0) - 1)
    def _():
        mixed_ref[...] = acc[...].astype(BF16)


def ffn_kernel(ups, downs, aligned, place, h_ref, g_ref, mid_ref, *refs):
    parts, refs = cut(refs, ups + downs)
    mixed_ref, gh_ref = refs[:2]
    grads = refs[2:6] if aligned else refs[2:4]
    wu_s, wd_s, acc, sem = refs[-4:]
    j, steps = pl.program_id(0), pl.num_programs(0)
    per_tile = h_ref.shape[1] // FF_COLS
    group = FF_COLS // sum(w.block for w in downs)

    def fetch(step, slot):
        column = pl.ds(pl.multiple_of((step % per_tile) * FF_COLS, FF_COLS), FF_COLS)
        for t, up in enumerate(ups):

            @pl.when(step // per_tile == t)
            def _(t=t, up=up):
                up.start(parts[t], place, wu_s.at[slot], sem.at[slot, 0], column)

        at = 0
        for i, down in enumerate(downs):
            count = group * down.block
            down.start_rows(
                parts[len(ups) + i], place, wd_s.at[slot, pl.ds(at, count), :], sem.at[slot, 1], step * group, group
            )
            at += count

    @pl.when(j == 0)
    def _():
        fetch(j, 0)

    @pl.when(j + 1 < steps)
    def _():
        fetch(j + 1, (j + 1) % 2)

    slot = j % 2
    arrived(wu_s.at[slot], sem.at[slot, 0])
    arrived(wd_s.at[slot], sem.at[slot, 1])
    wu, wd = wu_s[slot], wd_s[slot]
    if len(downs) > 1:
        width = wd.shape[1]
        stack, at = [], 0
        for down in downs:
            count = group * down.block
            stack.append(wd[at : at + count].reshape(group, down.block, width))
            at += count
        wd = jnp.concatenate(stack, axis=1).reshape(FF_COLS, width)
    act, gu, dwu, dwd = ffn_grads(h_ref[...], g_ref[...], wu, wd)
    if aligned:
        grads[0][...], grads[1][...] = split_pairs(dwu, grads[0].shape[0], place[1])
        for ref, value in zip(grads[2:], split_pairs(dwd, grads[2].shape[1], place[1]), strict=True):
            for t in range(ref.shape[0]):
                ref[t] = value[:, t * ref.shape[2] : (t + 1) * ref.shape[2]]
    else:
        grads[0][...] = dwu
        grads[1][...] = dwd
    ffn_sums(j, act, gu, wu, wd, mid_ref, mixed_ref, gh_ref, acc)


def ffn_call(place, h, cot, ups, downs, mid, grad_specs, hidden, aligned):
    n, d = h.shape
    full = resident((n, d))
    const = pl.BlockSpec((n, d), lambda j, *_: (0, 0))
    specs, args = weight_args(ups + downs)
    spec = pltpu.PrefetchScalarGridSpec(
        num_scalar_prefetch=1,
        grid=(hidden // FF_COLS,),
        in_specs=[full, full, full] + specs,
        out_specs=[const, const] + [g[0] for g in grad_specs],
        scratch_shapes=[
            pltpu.VMEM((2, d, FF_COLS), BF16),
            pltpu.VMEM((2, FF_COLS, d), BF16),
            pltpu.VMEM((n, d), F32),
            pltpu.SemaphoreType.DMA((2, 2)),
        ],
    )
    return pl.pallas_call(
        partial(ffn_kernel, ups, downs, aligned),
        grid_spec=spec,
        out_shape=[jax.ShapeDtypeStruct((n, d), BF16), jax.ShapeDtypeStruct((n, d), F32)]
        + [g[1] for g in grad_specs],
        compiler_params=params(60),
        cost_estimate=cost(12 * n * d * hidden, 8 * d * hidden + 14 * n * d),
        name="ffn",
    )(place, h, cot, mid, *args)


def qkv_grad_kernel(groups, place, h_ref, dq_ref, dkv_ref, rkv_ref, keep_ref, send_ref, sum_ref):
    h = h_ref[...]
    my_index = place[1]
    keep_ref[0], send_ref[0] = split_pairs(dot_tn(h, dq_ref[...]).astype(BF16), groups, my_index)
    for t in range(2):
        grad = (dkv_ref[t].astype(F32) + rkv_ref[t].astype(F32)).astype(BF16)
        sum_ref[t] = grad
        keep_ref[t + 1], send_ref[t + 1] = split_pairs(dot_tn(h, grad).astype(BF16), groups, my_index)


def qkv_grad_call(place, h, dq, dkv, rkv, groups):
    n, d = h.shape
    width = dq.shape[1]
    rows = d // (2 * groups)
    heads = width // GROUP_WIDTH
    pair = pl.BlockSpec((2, n, GROUP_WIDTH), lambda g, *_: (0, 0, g))
    share = pl.BlockSpec((3, groups, rows, GROUP_WIDTH), lambda g, *_: (g, 0, 0, 0))
    out = jax.ShapeDtypeStruct((3 * heads, groups, rows, GROUP_WIDTH), BF16)
    spec = pltpu.PrefetchScalarGridSpec(
        num_scalar_prefetch=1,
        grid=(heads,),
        in_specs=[resident((n, d)), pl.BlockSpec((n, GROUP_WIDTH), lambda g, *_: (0, g)), pair, pair],
        out_specs=[share, share, pair],
    )
    return pl.pallas_call(
        partial(qkv_grad_kernel, groups),
        grid_spec=spec,
        out_shape=[out, out, jax.ShapeDtypeStruct((2, n, width), BF16)],
        compiler_params=params(40),
        cost_estimate=cost(6 * n * d * width, 6 * d * width + 2 * n * d + 8 * n * width),
        name="qkv_grad",
    )(place, h, dq, dkv, rkv)


def head_back_kernel(weights, count, place, *refs):
    dqs, dkvs = refs[:count], refs[count : 2 * count]
    x_ref, gr_ref, gain_ref = refs[2 * count : 2 * count + 3]
    parts, refs = cut(refs[2 * count + 3 :], weights)
    tg_ref, dln_ref, wq, wk, wv, sem = refs
    load_all(weights, parts, place, (wq, wk, wv), sem)
    i = pl.program_id(0)
    dq = jnp.concatenate([r[...] for r in dqs], axis=1)
    dk = jnp.concatenate([r[0] for r in dkvs], axis=1)
    dv = jnp.concatenate([r[1] for r in dkvs], axis=1)
    grad = dot_nt(dq, wq[...]) + dot_nt(dk, wk[...]) + dot_nt(dv, wv[...])
    hat, scale = normed(x_ref[...].astype(F32))
    tg_ref[...] = (gr_ref[...] + norm_back(grad, gain_ref[...], hat, scale)).astype(BF16)
    dgain = jnp.sum(grad * hat, axis=0, keepdims=True)
    dbias = jnp.sum(grad, axis=0, keepdims=True)

    @pl.when(i == 0)
    def _():
        dln_ref[0:1, :] = dgain
        dln_ref[1:2, :] = dbias

    @pl.when(i > 0)
    def _():
        dln_ref[0:1, :] += dgain
        dln_ref[1:2, :] += dbias


def head_back_call(place, dqs, dkvs, x, gr, weights, gain):
    n, d = x.shape
    row = pl.BlockSpec((ROWS, d), lambda i, *_: (i, 0))
    specs, args = weight_args(weights)
    spec = pltpu.PrefetchScalarGridSpec(
        num_scalar_prefetch=1,
        grid=(n // ROWS,),
        in_specs=[pl.BlockSpec((ROWS, a.shape[1]), lambda i, *_: (i, 0)) for a in dqs]
        + [pl.BlockSpec((2, ROWS, a.shape[2]), lambda i, *_: (0, i, 0)) for a in dkvs]
        + [row, row, resident((1, d))]
        + specs,
        out_specs=[row, pl.BlockSpec((2, d), lambda *_: (0, 0))],
        scratch_shapes=[pltpu.VMEM((d, d), BF16)] * 3 + [pltpu.SemaphoreType.DMA((3,))],
    )
    return pl.pallas_call(
        partial(head_back_kernel, weights, len(dqs)),
        grid_spec=spec,
        out_shape=[jax.ShapeDtypeStruct((n, d), BF16), jax.ShapeDtypeStruct((2, d), F32)],
        compiler_params=params(48),
        cost_estimate=cost(6 * n * d * d, 6 * d * d + 14 * n * d),
        name="qkv_back",
    )(place, *dqs, *dkvs, x, gr, gain, *args)


class Term:
    def __init__(self, array, axes, first=0, count=None):
        self.array, self.axes, self.first = array, axes, first
        self.count = array.shape[0] if count is None else count
        self.whole = first % self.count != 0

    def spec(self, settled, flipped, open_bits, steps_bits):
        def index_map(step, mine):
            at = [0 if self.whole else self.first // self.count]
            for b in self.axes:
                if (flipped >> b) & 1:
                    at.append(1 - mine[b])
                elif b in settled:
                    at.append(mine[b])
                elif b in steps_bits:
                    at.append((step >> (len(steps_bits) - 1 - steps_bits.index(b))) & 1)
                else:
                    at.append(0)
            return (*at, 0, 0)

        lead = self.array.shape[0] if self.whole else self.count
        inner = tuple(2 if b in open_bits and b not in steps_bits else None for b in self.axes)
        return pl.BlockSpec((lead,) + inner + self.array.shape[-2:], index_map)

    def read(self, ref):
        start = self.first if self.whole else 0
        return ref[start : start + self.count].astype(F32)


class Cube:
    def __init__(self, dp, index, order):
        self.bits = dp.bit_length() - 1
        self.dp, self.order, self.mib = dp, order, 40
        self.mine = ((index >> jnp.arange(self.bits, dtype=jnp.int32)) & 1).astype(jnp.int32)

    def send(self, array, flip):
        return lax.ppermute(array, "dp", [(i, i ^ flip) for i in range(self.dp)])

    def far(self, low=2):
        return [f << low for f in range(1, 1 << (self.bits - low))]

    def terms(self, arrays, first=0, count=None):
        made = []
        for array in arrays:
            lead, _, rows, width = array.shape
            shape = (lead,) + (2,) * self.bits + (rows, width)
            made.append(Term(array.reshape(shape), list(range(self.bits))[::-1], first, count))
        return made

    def add(self, outputs, dtype):
        in_specs, args, plan, out_specs, out_shape = [], [], [], [], []
        for output in outputs:
            lead = 0
            for stream, settled, flipped in output:
                open_bits = [b for b in range(self.bits)[::-1] if b not in settled and not (flipped >> b) & 1]
                steps_bits = open_bits[:STEP_BITS]
                for term in stream:
                    in_specs.append(term.spec(settled, flipped, open_bits, steps_bits))
                    args.append(term.array)
                plan.append((len(out_specs), lead, list(stream)))
                lead += stream[0].count
            outer, inner = len(steps_bits), len(open_bits) - len(steps_bits)

            def out_map(step, mine, outer=outer, inner=inner):
                return (0, *[(step >> (outer - 1 - k)) & 1 for k in range(outer)], *[0] * inner, 0, 0)

            shape = output[0][0][0].array.shape[-2:]
            out_specs.append(pl.BlockSpec((lead,) + (None,) * outer + (2,) * inner + shape, out_map))
            out_shape.append(jax.ShapeDtypeStruct((lead,) + (2,) * (outer + inner) + shape, dtype))

        def kernel(mine, *refs):
            ins, outs = refs[: len(args)], refs[len(args) :]
            at = 0
            for out, first, stream in plan:
                total = stream[0].read(ins[at])
                for k in range(1, len(stream)):
                    total = total + stream[k].read(ins[at + k])
                outs[out][first : first + stream[0].count] = total.astype(dtype)
                at += len(stream)

        spec = pltpu.PrefetchScalarGridSpec(
            num_scalar_prefetch=1, grid=(2**outer,), in_specs=in_specs, out_specs=out_specs
        )
        size = sum(math.prod(o.shape) for o in out_shape)
        call = pl.pallas_call(
            kernel,
            grid_spec=spec,
            out_shape=out_shape,
            compiler_params=params(self.mib),
            cost_estimate=cost(4 * size, 8 * size),
            name="add_terms",
        )
        return self.order.run(call, self.mine, *args)


def join(cube, parts, streams):
    done = list(range(cube.bits))
    count, rows, width = parts[0].shape
    terms = [term for stream in streams for term in stream]

    def kernel(mine, *refs):
        outs = refs[len(parts) + len(terms) :]
        for k in range(len(parts)):
            for t, out in enumerate(outs):
                out[:, k * width : (k + 1) * width] = refs[k][t]
        at = len(parts)
        for k, stream in enumerate(streams):
            total = stream[0].read(refs[at])
            for m in range(1, len(stream)):
                total = total + stream[m].read(refs[at + m])
            at += len(stream)
            column = (len(parts) + k) * width
            for t, out in enumerate(outs):
                out[:, column : column + width] = total[t]

    whole = (rows, (len(parts) + len(streams)) * width)
    spec = pltpu.PrefetchScalarGridSpec(
        num_scalar_prefetch=1,
        grid=(1,),
        in_specs=[pl.BlockSpec(p.shape, lambda *_: (0, 0, 0)) for p in parts]
        + [term.spec(done, 0, [], []) for term in terms],
        out_specs=[pl.BlockSpec(whole, lambda *_: (0, 0))] * count,
    )
    call = pl.pallas_call(
        kernel,
        grid_spec=spec,
        out_shape=[jax.ShapeDtypeStruct(whole, F32)] * count,
        compiler_params=params(62),
        cost_estimate=cost(4 * count * rows, 8 * count * rows),
        name="join_terms",
    )
    return cube.order.run(call, cube.mine, *parts, *[term.array for term in terms])


def merge(arrays, outputs, *awaited):
    d = arrays[0].shape[-1]
    shapes = []
    for output in outputs:
        blocks = sum(arrays[i].shape[0] for i, _, _ in output)
        shapes.append(jax.ShapeDtypeStruct((blocks, output[0][2], d), BF16))

    def kernel(*refs):
        ins, outs = refs[: len(arrays)], refs[len(arrays) + len(awaited) :]
        for out, output in zip(outs, outputs, strict=True):
            at = 0
            for i, first, count in output:
                blocks = ins[i].shape[0]
                out[at : at + blocks] = ins[i][:, first : first + count]
                at += blocks

    whole = pl.BlockSpec(memory_space=pltpu.VMEM)
    size = sum(math.prod(shape.shape) for shape in shapes)
    return pl.pallas_call(
        kernel,
        in_specs=[whole] * len(arrays) + [HBM] * len(awaited),
        out_specs=[whole] * len(outputs),
        out_shape=shapes,
        compiler_params=params(40),
        cost_estimate=cost(size, 4 * size),
        name="merge",
    )(*arrays, *awaited)


class Side:
    def __init__(self, cube, order):
        self.cube, self.order = cube, order

    def hold(self, held, bit):
        self.held = held
        self.got = self.cube.send(held, 1 << bit)

    def parts_of(self):
        last = 1 << self.order[1]
        flips = [0] + self.cube.far()
        flips = flips + [f ^ (1 << self.order[0]) for f in flips]
        moved = [f ^ last for f in flips]
        return [(flips, 0), (moved, 0), (flips, 1), (moved, 1)]

    def index(self, flip):
        first, last = self.order
        return (flip >> 2) + (((flip >> first) & 1) << (self.cube.bits - 2)), (flip >> last) & 1


class Gather:
    def __init__(self, cube, order, exchange, one, two):
        self.cube, self.order, self.exchange = cube, order, exchange
        self.rows = one.shape[0]
        self.local = jnp.concatenate([one, two], axis=0)[None]
        self.sides = (Side(cube, (1, 0)), Side(cube, (0, 1)))

    def far(self):
        local = self.order.after(self.local)
        self.pieces = [local] + [self.cube.send(local, f) for f in self.cube.far()]
        self.order.note(local)

    def near(self, *awaited):
        total = self.local.shape[1]
        outputs = [
            [(i, first, count) for i in range(len(self.pieces))]
            for first, count in ((0, self.rows), (self.rows, total - self.rows))
        ]
        held = self.order.run(lambda first, *rest: merge((first, *rest), outputs, *awaited), *self.pieces)
        for s, array in zip(self.sides, held, strict=True):
            s.hold(array, s.order[0])

    def last(self, *awaited):
        arrays = [a for s in self.sides for a in (s.held, s.got)]
        outputs = [[(i, 0, arrays[i].shape[1]), (i + 1, 0, arrays[i].shape[1])] for i in (0, 2)]
        held = self.order.run(lambda first, *rest: merge((first, *rest), outputs, *awaited), *arrays)
        for s, array in zip(self.sides, held, strict=True):
            s.hold(array, s.order[1])

    def cross(self):
        for s in self.sides:
            s.other = self.exchange(self.order.after(s.held))

    def finish(self):
        for s in self.sides:
            s.rest = self.exchange(self.order.after(s.got))

    def ready(self):
        for s in self.sides:
            s.buffers = [s.held, s.got, s.other, s.rest]
            s.parts = s.parts_of()


class Order:
    def __init__(self):
        self.token = ()

    def after(self, *values):
        if self.token:
            values = lax.optimization_barrier((values, self.token))[0]
        return values if len(values) > 1 else values[0]

    def note(self, *token):
        self.token = token

    def run(self, call, first, *rest):
        out = call(self.after(first), *rest)
        self.note(jax.tree.leaves(out)[0])
        return out


class Scatter:
    def __init__(self, cube, one, two, direct):
        self.cube, self.sides, self.step, self.direct = cube, (one, two), 0, direct
        self.sent, self.last = [], []

    def advance(self):
        step, cube = self.step, self.cube
        if step < 2:
            flips = (1 << step, 1 << (1 - step))
            done = ([], []) if step == 0 else ([0], [1])
            self.sent = cube.add(
                [[(stream, done[s], flips[s]) for stream in self.sides[s]] for s in range(2)], BF16
            )
            self.last = []
            for s in range(2):
                got = cube.send(self.sent[s], flips[s])
                self.last.append(got)
                axes = [b for b in range(cube.bits)[::-1] if b not in done[s] and not (flips[s] >> b) & 1]
                at = 0
                for stream in self.sides[s]:
                    stream.append(Term(got, axes, at, stream[0].count))
                    at += stream[0].count
        else:
            streams = [stream for side in self.sides for stream in side]
            if self.direct:
                done, flips = list(range(cube.bits)), cube.far()
            else:
                done, flips = list(range(step)), [1 << step]
            self.sent = cube.add([[(stream, done, f) for stream in streams] for f in flips], BF16)
            self.last = [cube.send(sent, f) for sent, f in zip(self.sent, flips, strict=True)]
            axes = [] if self.direct else list(range(step + 1, cube.bits))[::-1]
            for got in self.last:
                at = 0
                for stream in streams:
                    stream.append(Term(got, axes, at, stream[0].count))
                    at += stream[0].count
        self.step += 1
        return self

    def finish(self):
        while self.step < (3 if self.direct else self.cube.bits):
            self.advance()
        done = list(range(self.cube.bits))
        return self.cube.add([[(stream, done, 0)] for side in self.sides for stream in side], F32)


def gate(value, *others):
    return lax.optimization_barrier((value, others))[0]


def block_table(seg_full, seg_local, my_index, bq, bk):
    first, last = seg_local[::bq], seg_local[bq - 1 :: bq]
    low = jnp.sum((seg_full[None, :] < first[:, None]).astype(jnp.int32), axis=1)
    high = jnp.sum((seg_full[None, :] <= last[:, None]).astype(jnp.int32), axis=1)
    start = low // ROW_ALIGN * ROW_ALIGN
    table = jnp.stack([start, (high - start + bk - 1) // bk], axis=1).reshape(-1)
    return jnp.concatenate([table, my_index[None]]).astype(jnp.int32)


def body(
    tokens,
    segments,
    ln1_gain,
    ln1_bias,
    w_query,
    w_key,
    w_value,
    w_out,
    ln2_gain,
    ln2_bias,
    w_up,
    w_down,
    cotangent,
):
    x = tokens[0]
    n, d = x.shape
    cot = cotangent[0]
    rows = w_query.shape[0]
    devices = d // rows
    hidden = w_up.shape[1]
    per_device = hidden // devices
    my_index = lax.axis_index("seq")
    seg_full = segments[0]
    seg_local = lax.dynamic_slice_in_dim(seg_full, my_index * n, n)
    tab = block_table(seg_full, seg_local, my_index, ATT_Q, ATT_K)
    tab_back = block_table(seg_full, seg_local, my_index, ATT_Q, BACK_K)
    seg_q = seg_local.reshape(n // ATT_Q, 1, ATT_Q)
    seg_col = jnp.pad(seg_full, (0, max(ATT_K, BACK_K)), constant_values=-1)[:, None]

    dp = devices // 2
    dp_index = lax.axis_index("dp")
    order = Order()
    cube = Cube(dp, dp_index, order)
    place = jnp.stack([dp_index, my_index]).astype(jnp.int32)
    swap = [(0, 1), (1, 0)]
    tiles = hidden // d

    def exchange(value):
        return lax.ppermute(value, "seq", swap)

    def halves(value, axis):
        keep = lax.dynamic_index_in_dim(value, my_index, axis, keepdims=False)
        send = lax.dynamic_index_in_dim(value, 1 - my_index, axis, keepdims=False)
        return keep, send

    vectors = jnp.concatenate([ln1_gain, ln1_bias, ln2_gain, ln2_bias]).astype(F32)
    vectors = jnp.broadcast_to(vectors[None], (devices, 4 * rows))
    vectors = lax.all_to_all(vectors, BOTH, 0, 0, tiled=True)
    ln = vectors.reshape(devices, 4, rows).transpose(1, 0, 2).reshape(4, 1, d)

    aligned = rows % 32 == 0
    groups = d // GROUP_WIDTH
    if aligned:
        cut_row, half_down = rows // 2, per_device // 2
        up_tiles = w_up.reshape(rows, tiles, d).transpose(1, 0, 2)
        half_up = tiles // 2 * rows
        low_up, high_up = (u.reshape(half_up, d) for u in (up_tiles[: tiles // 2], up_tiles[tiles // 2 :]))
        head = Gather(
            cube, order, exchange,
            jnp.concatenate([w_key, w_query[:cut_row]]), jnp.concatenate([w_value, w_query[cut_row:]]),
        )
        low = Gather(
            cube, order, exchange,
            jnp.concatenate([low_up, w_out[:cut_row]]), jnp.concatenate([w_down[:half_down], w_out[cut_row:]]),
        )
        high = Gather(cube, order, exchange, high_up, w_down[half_down:])
        head.far()
        head.near(vectors, seg_col, seg_q, tab, tab_back)
        low.far()
        head.last()
        head.cross()
        order.note(*[side.got for side in head.sides])
        head.finish()
        head.ready()
        low.near()
        key_w = Spread(rows, [(head.sides[0], 0, rows, 0)])
        value_w = Spread(rows, [(head.sides[1], 0, rows, 0)])
        query_w = Spread(rows, [(head.sides[0], rows, cut_row, 0), (head.sides[1], rows, cut_row, cut_row)])
    else:
        every = jnp.concatenate([w_query, w_key, w_value, w_out], axis=0).reshape(4, rows, d)
        every = lax.all_gather(every, BOTH, axis=1, tiled=True)
        query_w, key_w, value_w, out_w = (Plain(every[t], rows) for t in range(4))
        up_all = lax.all_gather(w_up, BOTH, axis=0, tiled=True)
        ups = [Plain(up_all[:, t * d : (t + 1) * d], rows) for t in range(tiles)]
        downs = [Plain(lax.all_gather(w_down, BOTH, axis=0, tiled=True), per_device)]

    h1, own = order.run(kv_call, place, x, ln[0], ln[1], [key_w, value_w])
    if aligned:
        low.last()
    other = exchange(order.after(own))
    q = order.run(q_call, place, h1, [query_w])
    if aligned:
        high.far()
    outs, lses = [], []
    plan = [(0, 2), (2, 1), (3, 1)] if groups == 4 else [(g, 1) for g in range(groups)]
    for i, (start, count) in enumerate(plan):
        if aligned and i == 1:
            high.near()
            low.finish()
        if aligned and i == 2:
            high.last(*[side.rest for side in low.sides])
            low.cross()
        out, lse = order.run(
            attend_call, tab, q, own, other, seg_q, seg_col, ATT_Q, ATT_K, start, count
        )
        outs.append(out)
        lses.append(lse)
    if aligned:
        low.ready()
        high.cross()
        out_w = Spread(
            rows, [(low.sides[0], half_up, cut_row, 0), (low.sides[1], half_down, cut_row, cut_row)]
        )
    mid, h2 = order.run(mid_call, place, x, outs, [out_w], ln[2], ln[3])
    if aligned:
        high.finish()
        high.ready()

    up_rows = tiles * rows
    if aligned:
        ups = [
            Spread(rows, [((low, high)[t // (tiles // 2)].sides[0], t % (tiles // 2) * rows, rows, 0)])
            for t in range(tiles)
        ]
        downs = [Spread(half_down, [(r.sides[1], 0, half_down, 0)]) for r in (low, high)]
        per_tile = d // FF_COLS
        group = FF_COLS // per_device
        up_out = (
            pl.BlockSpec((None, dp, rows, FF_COLS), lambda j, *_: (j // per_tile, 0, 0, j % per_tile)),
            jax.ShapeDtypeStruct((tiles, dp, rows, d), BF16),
        )
        down_out = (
            pl.BlockSpec((tiles, group // 2, rows, d), lambda j, *_: (0, j, 0, 0)),
            jax.ShapeDtypeStruct((tiles, dp, rows, d), BF16),
        )
        grad_specs = [up_out, up_out, down_out, down_out]
    else:
        grad_specs = [
            (pl.BlockSpec((d, FF_COLS), lambda j, *_: (0, j)), jax.ShapeDtypeStruct((d, hidden), BF16)),
            (pl.BlockSpec((FF_COLS, d), lambda j, *_: (j, 0)), jax.ShapeDtypeStruct((hidden, d), BF16)),
        ]
    mixed, gmid, *grads = order.run(ffn_call, place, h2, cot, ups, downs, mid, grad_specs, hidden, aligned)
    if not aligned:
        dwu = grads[0].reshape(dp, 2, rows, tiles, d).transpose(3, 0, 1, 2, 4)
        dwd = grads[1].reshape(dp, 2, tiles, rows, d).transpose(2, 0, 1, 3, 4)
        grads = [*halves(dwu, 2), *halves(dwd, 2)]
    keep_up, send_up, keep_down, send_down = grads
    got_up, got_down = exchange(send_up), exchange(send_down)
    big = Scatter(cube, [cube.terms([keep_up, got_up])], [cube.terms([keep_down, got_down])], False)

    grad_mid, grad_att, keep_out, send_out, dln2 = order.run(
        mid_back_call, place, gmid, mid, cot, outs, [out_w], ln[2], dp
    )
    big.advance()
    got_out = exchange(order.after(send_out))
    dqs, dkvs = [], []

    def attend_back(g):
        which = [i for i, (start, _) in enumerate(plan) if start <= g][-1]
        return order.run(
            attend_back_call, tab_back, q, grad_att, outs[which], own, other, seg_q, seg_col,
            lses[which], ATT_Q, BACK_K, g, 1, g - plan[which][0],
        )

    def finish_group(dq, dkv, got):
        keep, send, dkv = order.run(qkv_grad_call, place, h1, dq, dkv, got, dp)
        dqs.append(dq)
        dkvs.append(dkv)
        return keep, send

    dq_0, dkv_0, sent_0 = attend_back(0)
    got_0 = exchange(sent_0)
    dq_1, dkv_1, sent_1 = attend_back(1)
    keep_0, send_0 = finish_group(dq_0, dkv_0, got_0)
    big.advance()
    got_1 = exchange(order.after(sent_1))
    keep_1, send_1 = finish_group(dq_1, dkv_1, got_1)
    terms_0, terms_1 = [keep_0, exchange(order.after(send_0))], [keep_1, exchange(order.after(send_1))]
    dq_2, dkv_2, sent_2 = attend_back(2)
    big.advance()
    tail_one = Scatter(
        cube,
        [cube.terms(terms_0), cube.terms([keep_out, got_out], 0, 2)],
        [cube.terms(terms_1), cube.terms([keep_out, got_out], 2, 2)],
        False,
    )
    tail_one.advance()
    got_2 = exchange(order.after(sent_2))
    dq_3, dkv_3, sent_3 = attend_back(3)
    big.advance()
    tail_one.advance()
    got_3 = exchange(order.after(sent_3))
    keep_2, send_2 = finish_group(dq_2, dkv_2, got_2)
    keep_3, send_3 = finish_group(dq_3, dkv_3, got_3)
    tail_one.advance()
    terms_2, terms_3 = [keep_2, exchange(order.after(send_2))], [keep_3, exchange(order.after(send_3))]
    tail_two = Scatter(cube, [cube.terms(terms_2)], [cube.terms(terms_3)], True)
    tail_two.advance()
    token_grad, dln1 = order.run(
        head_back_call, place, dqs, dkvs, x, grad_mid, [query_w, key_w, value_w], ln[0]
    )
    cube.mib = 62
    tail_two.advance()
    tail_one.advance()
    tail_two.advance()
    up_share, down_share = big.finish()
    one_a, out_a, one_b, out_b = tail_one.finish()
    dln = jnp.concatenate([dln1, gate(dln2, *tail_two.last)], axis=0).reshape(4, devices, rows).transpose(1, 0, 2)
    dln = lax.all_to_all(dln.reshape(devices, 4 * rows), BOTH, 0, 0, tiled=True)
    dln = jnp.sum(dln.reshape(devices, 4, rows), axis=0)
    qkv_share = join(cube, [one_a, one_b], [stream for side in tail_two.sides for stream in side])

    up_share = up_share.transpose(1, 0, 2).reshape(rows, hidden)
    down_share = down_share.reshape(per_device, d)
    out_share = jnp.concatenate([out_a, out_b], axis=0).transpose(1, 0, 2).reshape(rows, d)
    return (
        mixed[None],
        token_grad[None],
        dln[0],
        dln[1],
        qkv_share[0],
        qkv_share[1],
        qkv_share[2],
        out_share,
        dln[2],
        dln[3],
        up_share,
        down_share,
    )


def solution(mesh):
    row, act, vec = P(BOTH, None), P("dp", "seq", None), P(BOTH)
    in_specs = (act, P("dp", None), vec, vec, row, row, row, row, vec, vec, row, row, act)
    out_specs = (act, act, vec, vec, row, row, row, row, vec, vec, row, row)
    return jax.shard_map(body, mesh=mesh, in_specs=in_specs, out_specs=out_specs, check_vma=False)
```
